128 devices in a mesh: head: 4 (over z_lo, core), tok: 32 (over x, z_hi, y).
Axes of the slice: x: 4, y: 4, z: 4 (z_hi: 2, z_lo: 2; z = z_hi * 2 + z_lo), core: 2. Of those that a mesh axis runs over, the one named last changes fastest.
Arguments:
- hidden_in: bfloat16 [8192, 2048], P('tok'), may hold values from -6 to 6
- queries: bfloat16 [8192, 2048], P('tok', 'head'), may hold values from -4.5 to 4.5
- keys: bfloat16 [8192, 2048], P('tok', 'head'), may hold values from -4.5 to 4.5
- values: bfloat16 [8192, 2048], P('tok', 'head'), may hold values from -6 to 6
- request_ids: int32 [8192], replicated, may hold values from 0 to 63, never falling along the last dimension, each value on 1 to 1024 neighbouring positions
- out_proj: bfloat16 [2048, 2048], P('head'), may hold values from -0.125 to 0.125
- norm_gain: float32 [2048], replicated, may hold values from 0.1 to 1.9
- expert_gate_up: bfloat16 [32, 2048, 2, 1408], P('tok', None, None, 'head'), may hold values from -0.125 to 0.125
- expert_down: bfloat16 [32, 1408, 2048], P('tok', 'head'), may hold values from -0.15625 to 0.15625
- shared_gate_up: bfloat16 [2048, 2, 2816], P(None, None, 'head'), may hold values from -0.125 to 0.125
- shared_down: bfloat16 [2816, 2048], P('head'), may hold values from -0.109375 to 0.109375
- shared_gate: bfloat16 [2048], replicated, may hold values from -0.125 to 0.125
- routes: int32 [8192, 4], P('tok'), may hold values from 0 to 31, all different within a row; in each aligned block of 256 rows (0 to 255, 256 to 511, ...) at most 48 rows name the same one
- route_weights: float32 [8192, 4], P('tok'), may hold values from 0.05 to 0.5
- page_slots: int32 [1024], replicated, may hold values from 0 to 1023, as said below
Outputs:
- layer_out: bfloat16 [8192, 2048], P('tok', 'head')
- decode_cache: bfloat16 [1024, 8, 4096], P('tok', 'head')
The draws below stay inside these ranges and needn't reach their ends.
Inputs may be any that keep to these rules, and one draw needn't show every extreme that they name: `request_ids`: ids never fall along the tokens; each request holds 1 to 1024 consecutive tokens, and one holds exactly 1024. `routes`: each row names 4 different experts; among the rows of one device no expert is named more than 48 times, a bound that some block reaches. `page_slots`: a permutation; for any two aligned blocks, one of 32 pages and one of 32 cache rows, the number of pages of the first that go to rows of the second is exactly 1.
All inputs are finite; a program needn't handle non-finite values.
Results may differ from the reference program's by a relative error of at most 0.0065.
Values may be sent and summed in bfloat16 or wider, within the bound.
No kernel may reach another device: no remote copies, remote signals or barrier semaphores. Data moves between devices by JAX's collectives and lax.ppermute only.
A program may use at most 128 MiB of HBM per device.

```python
import math
import jax
import jax.numpy as jnp
import numpy as np
from jax import lax

D = 2048
H = 16
HD = 128
F_EXP = 1408
TOP = 4
EXPERTS = 32
F_SHARED = 2816
PAGE = 8
REACH = 4
TOK_DEV = 256
TOKENS = 8192
CAP = 48
MAXLEN = 1024
REQUESTS = 64
PAGES_DEV = 32
PAGES = 1024
N_TOK = 32


def attention_pair(key):
    base = jax.random.fold_in(key, 7)
    first, second = jax.random.split(base, 2)
    shape = (TOKENS, H * HD)
    query_part = jnp.clip(jax.random.normal(first, shape, jnp.float32), -4.5, 4.5)
    key_part = jnp.clip(jax.random.normal(second, shape, jnp.float32), -4.5, 4.5)
    return (query_part, key_part)


def draw_queries(key, part):
    return attention_pair(key)[0].astype(jnp.bfloat16)


def draw_keys(key, part):
    return attention_pair(key)[1].astype(jnp.bfloat16)


def draw_page_slots(key, part):
    first, second = jax.random.split(jax.random.fold_in(key, 11))
    pair = PAGES_DEV // N_TOK
    source_perm = jax.vmap(lambda k: jax.random.permutation(k, PAGES_DEV))(jax.random.split(first, N_TOK)).astype(jnp.int32)
    target_perm = jax.vmap(lambda k: jax.random.permutation(k, PAGES_DEV))(jax.random.split(second, N_TOK)).astype(jnp.int32)
    inverse = jnp.argsort(target_perm, axis=1).astype(jnp.int32)
    position = jnp.arange(PAGES_DEV, dtype=jnp.int32)
    sources = jnp.arange(N_TOK, dtype=jnp.int32)[:, None]
    owner = jnp.broadcast_to((position // pair)[None, :], (N_TOK, PAGES_DEV))
    arrival = sources * pair + (position % pair)[None, :]
    place = inverse[owner, arrival]
    row = owner * PAGES_DEV + place
    page = sources * PAGES_DEV + source_perm
    return jnp.zeros((PAGES,), jnp.int32).at[page.reshape(-1)].set(row.reshape(-1))


def shard_levels(own_key, shape, shards, least, largest):
    def one(dim, blocks):
        steps = jax.random.uniform(jax.random.fold_in(jax.random.fold_in(own_key, 6), dim), (blocks,), jnp.float32, least / len(shards), largest / len(shards))
        return jnp.repeat(jnp.exp(steps), shape[dim] // blocks).reshape((-1,) + (1,) * (len(shape) - dim - 1))

    level = one(*shards[0])
    for cut in shards[1:]:
        level = level * one(*cut)
    return level


def profile(count, total, bound, lean):
    weights = [(1 << 20) // math.isqrt(grade ** lean) + 1 for grade in range(2, count + 1)]
    surplus, holding = total - bound - (count - 1), [1] * (count - 1)
    while surplus > 0:
        movable = [i for i in range(count - 1) if holding[i] < bound]
        mass, remaining = sum([weights[i] for i in movable]), surplus
        for i in movable:
            extra = min(bound - holding[i], max(1, remaining * weights[i] // mass), surplus)
            holding[i] = holding[i] + extra
            surplus = surplus - extra
    return np.array([bound] + holding)


def ragged_sizes(own_key, number_of, total, limit, lean):
    if number_of == 2:
        one = jax.random.randint(own_key, (), max(1, total - limit), min(limit, total - 1) + 1)
        return jnp.stack([one, total - one])
    lengths = jnp.asarray(profile(number_of, total, limit, lean), jnp.int32)
    pairs = (number_of - 1) // 2
    giver, taker = lengths[1:1 + 2 * pairs:2], lengths[2:2 + 2 * pairs:2]
    room = jnp.minimum(giver - 1, limit - taker)
    passed = jax.random.randint(jax.random.fold_in(own_key, 1), (pairs,), 0, 1 << 20) % (room + 1)
    lengths = lengths.at[1:1 + 2 * pairs:2].set(giver - passed).at[2:2 + 2 * pairs:2].set(taker + passed)
    return lengths[jax.random.permutation(jax.random.fold_in(own_key, 2), number_of)]


def deal_out(stream_key, own, number, rows, number_of, top, limit, slope):
    sequence = jax.random.permutation(stream_key, number_of)
    heavy_load, usual = load_shares(number_of, rows * top, limit, slope, True), load_shares(number_of, rows * top, limit, slope, False)
    places = jnp.arange(number_of)

    def named(lengths, rotation):
        used = int((lengths > 0).sum())
        fixed = max(1, used // 4)
        shifted = fixed + (places - fixed + rotation * (used - fixed)) % max(1, number_of - fixed)
        return jnp.zeros((number_of,), jnp.int32).at[sequence[jnp.where(places < fixed, places, shifted)]].set(jnp.asarray(lengths, jnp.int32))

    lengths = jnp.where(number % 4 == 0, named(heavy_load, number // 4), named(usual, number - number // 4 - 1))
    mixed = jax.random.permutation(jax.random.fold_in(own, 3), number_of)
    donor, receiver = mixed[0:number_of // 2 * 2:2], mixed[1:number_of // 2 * 2:2]
    room = jnp.minimum(lengths[donor] - 1, limit - lengths[receiver]) // 2
    room = jnp.where((donor == sequence[0]) | (receiver == sequence[0]) | (lengths[receiver] == 0), 0, jnp.maximum(room, 0))
    shifted = jax.random.randint(jax.random.fold_in(own, 4), (number_of // 2,), 0, 1 << 20) % (room + 1)
    lengths = lengths.at[donor].add(-shifted).at[receiver].add(shifted)
    members = jnp.searchsorted(jnp.cumsum(lengths), jnp.arange(rows * top), side="right").astype(jnp.int32)
    grid = members.reshape(top, rows).T
    grid = grid[jax.random.permutation(jax.random.fold_in(own, 1), rows)]
    rotation = jax.random.randint(jax.random.fold_in(own, 2), (rows, 1), 0, top)
    return jnp.take_along_axis(grid, (jnp.arange(top)[None, :] + rotation) % top, axis=1)


def load_shares(number_of, total, most, skew, full):
    loads = [(1 << 20) // math.isqrt(grade ** skew) + 1 for grade in range(1, number_of + 1)]
    largest = most if full else min(most, max(-(-total // number_of), total * loads[0] // sum(loads)))
    least = 1 if total - largest >= number_of - 1 else 0
    holding, spare = [largest] + [least] * (number_of - 1), total - largest - least * (number_of - 1)
    while spare > 0:
        movable = [i for i in range(1, number_of) if holding[i] < largest] or [i for i in range(1, number_of) if holding[i] < most]
        whole, remaining = sum([loads[i] for i in movable]), spare
        for i in movable:
            addition = min(most - holding[i], max(1, remaining * loads[i] // whole), spare)
            holding[i] = holding[i] + addition
            spare = spare - addition
    return np.array(holding)


def scatter_about(key, dims, spread, most, shards=(), kind=jnp.bfloat16):
    level = shard_levels(key, dims, shards, -0.22, 0.18) if shards else 1.0
    entries = jax.random.normal(key, dims, jnp.float32) * spread * level
    return jnp.minimum(jnp.maximum(entries, -most), most).astype(kind)


def setup_inputs(seed: int = 0) -> dict:
    streams_of = jax.random.split(jax.random.key(seed), 16)
    hidden_in = scatter_about(streams_of[0], (TOKENS, D), 1.0, 6.0, ((0, 32),))
    queries = draw_queries(jax.random.fold_in(streams_of[15], 71), 0)
    keys = draw_keys(jax.random.fold_in(streams_of[15], 71), 0)
    values = scatter_about(streams_of[3], (TOKENS, H * HD), 1.0, 6.0, ((0, 32), (1, 4)))
    request_ids = jnp.searchsorted(jnp.cumsum(ragged_sizes(streams_of[4], REQUESTS, TOKENS, MAXLEN, 2)), jnp.arange(TOKENS), side="right").astype(jnp.int32)
    out_proj = scatter_about(streams_of[5], (H * HD, D), (H * HD) ** -0.5, 0.125, ((0, 4),))
    norm_gain = jnp.clip(1.0 + 0.18 * jax.random.normal(streams_of[6], (D,), jnp.float32), 0.1, 1.9)
    expert_gate_up = scatter_about(streams_of[7], (EXPERTS, D, 2, F_EXP), D ** -0.5, 0.125, ((0, 32), (3, 4)))
    expert_down = scatter_about(streams_of[8], (EXPERTS, F_EXP, D), F_EXP ** -0.5, 0.15625, ((0, 32), (1, 4)))
    shared_gate_up = scatter_about(streams_of[9], (D, 2, F_SHARED), D ** -0.5, 0.125, ((2, 4),))
    shared_down = scatter_about(streams_of[10], (F_SHARED, D), F_SHARED ** -0.5, 0.109375, ((0, 4),))
    shared_gate = scatter_about(streams_of[11], (D,), D ** -0.5, 0.125)
    routes_keys = jax.random.split(jax.random.fold_in(streams_of[12], 1), TOKENS // TOK_DEV)
    routes_turns = jax.random.permutation(jax.random.fold_in(streams_of[12], 3), TOKENS // TOK_DEV)
    routes = jax.vmap(lambda own, number: deal_out(jax.random.fold_in(streams_of[12], 2), own, number, TOK_DEV, EXPERTS, TOP, CAP, 1))(routes_keys, routes_turns).reshape((TOKENS, TOP))
    route_weights = jnp.clip(0.05 + 0.45 * jax.random.uniform(streams_of[13], (TOKENS, TOP), jnp.float32) ** shard_levels(streams_of[13], (TOKENS, TOP), ((0, 32),), -0.2, 0.2), 0.05, 0.5)
    page_slots = draw_page_slots(jax.random.fold_in(streams_of[15], 71), 0)
    return {"hidden_in": hidden_in, "queries": queries, "keys": keys, "values": values, "request_ids": request_ids, "out_proj": out_proj, "norm_gain": norm_gain, "expert_gate_up": expert_gate_up, "expert_down": expert_down, "shared_gate_up": shared_gate_up, "shared_down": shared_down, "shared_gate": shared_gate, "routes": routes, "route_weights": route_weights, "page_slots": page_slots}


def reference(hidden_in, queries, keys, values, request_ids, out_proj, norm_gain, expert_gate_up, expert_down, shared_gate_up, shared_down, shared_gate, routes, route_weights, page_slots):
    width = H * HD
    span = REACH * TOK_DEV
    scale = 1.0 / math.sqrt(HD)
    padded_keys = jnp.concatenate([jnp.zeros((span, width), keys.dtype), keys], 0)
    padded_values = jnp.concatenate([jnp.zeros((span, width), values.dtype), values], 0)
    padded_ids = jnp.concatenate([jnp.full((span,), -1, jnp.int32), request_ids.astype(jnp.int32)], 0)
    query_pos = jnp.arange(TOK_DEV, dtype=jnp.int32) + span
    key_pos = jnp.arange(span + TOK_DEV, dtype=jnp.int32)

    def attend(block):
        start = (block * TOK_DEV).astype(jnp.int32)
        query_rows = lax.dynamic_slice_in_dim(queries, start, TOK_DEV, 0).reshape(TOK_DEV, H, HD).astype(jnp.float32)
        key_rows = lax.dynamic_slice_in_dim(padded_keys, start, span + TOK_DEV, 0).reshape(-1, H, HD).astype(jnp.float32)
        value_rows = lax.dynamic_slice_in_dim(padded_values, start, span + TOK_DEV, 0).reshape(-1, H, HD).astype(jnp.float32)
        query_ids = lax.dynamic_slice_in_dim(request_ids.astype(jnp.int32), start, TOK_DEV, 0)
        key_ids = lax.dynamic_slice_in_dim(padded_ids, start, span + TOK_DEV, 0)
        allowed = (query_ids[:, None] == key_ids[None, :]) & (key_pos[None, :] <= query_pos[:, None])
        scores = jnp.einsum('qhd,khd->hqk', query_rows, key_rows) * scale
        scores = jnp.where(allowed[None], scores, -1e+30)
        top = lax.optimization_barrier(jnp.max(scores, axis=-1, keepdims=True))
        weights = jnp.exp(scores - top)
        probs = (weights / lax.optimization_barrier(jnp.sum(weights, axis=-1, keepdims=True))).astype(jnp.bfloat16)
        mixed = jnp.einsum('hqk,khd->qhd', probs.astype(jnp.float32), value_rows)
        return mixed.astype(jnp.bfloat16).reshape(TOK_DEV, width)
    attended = lax.map(attend, jnp.arange(TOKENS // TOK_DEV, dtype=jnp.int32)).reshape(TOKENS, width)
    resid = hidden_in.astype(jnp.float32) + jnp.dot(attended, out_proj, preferred_element_type=jnp.float32)
    mean_square = lax.optimization_barrier(jnp.mean(resid * resid, axis=-1, keepdims=True))
    normed = (resid * lax.rsqrt(mean_square + 1e-06) * norm_gain).astype(jnp.bfloat16)
    shared_both = jnp.einsum('td,dgf->tgf', normed.astype(jnp.float32), shared_gate_up.astype(jnp.float32))
    shared_act = (jax.nn.silu(shared_both[:, 0, :]) * shared_both[:, 1, :]).astype(jnp.bfloat16)
    shared_scale = jax.nn.sigmoid(jnp.dot(normed, shared_gate, preferred_element_type=jnp.float32))
    shared_term = shared_scale[:, None] * jnp.dot(shared_act, shared_down, preferred_element_type=jnp.float32)
    flat = routes.reshape(-1).astype(jnp.int32)
    assign = TOKENS * TOP
    order = jnp.argsort(flat, stable=True).astype(jnp.int32)
    expert_ids = jnp.arange(EXPERTS, dtype=jnp.int32)
    counts = lax.optimization_barrier(jnp.sum((flat[:, None] == expert_ids[None, :]).astype(jnp.int32), 0))
    starts = (jnp.cumsum(counts) - counts).astype(jnp.int32)
    most = N_TOK * CAP
    flat_weights = route_weights.reshape(-1)

    def one_expert(total, expert):
        index = starts[expert] + jnp.arange(most, dtype=jnp.int32)
        live = jnp.arange(most, dtype=jnp.int32) < counts[expert]
        pick = order[jnp.minimum(index, assign - 1)]
        rows = normed[pick // TOP].astype(jnp.float32)
        both = jnp.einsum('td,dgf->tgf', rows, expert_gate_up[expert].astype(jnp.float32))
        expert_act = (jax.nn.silu(both[:, 0, :]) * both[:, 1, :]).astype(jnp.bfloat16)
        expert_out = jnp.dot(expert_act, expert_down[expert], preferred_element_type=jnp.float32)
        factor = jnp.where(live, flat_weights[pick], jnp.zeros((), flat_weights.dtype))
        return (total.at[pick // TOP].add(expert_out * factor[:, None]), None)
    moe, unused = lax.scan(one_expert, jnp.zeros((TOKENS, D), jnp.float32), expert_ids)
    layer_out = (resid + shared_term + moe).astype(jnp.bfloat16)
    pages = jnp.stack([keys, values], 1).reshape(PAGES, PAGE, 2 * width)
    decode_cache = jnp.zeros((PAGES, PAGE, 2 * width), jnp.bfloat16).at[page_slots.astype(jnp.int32)].set(pages)
    return (layer_out, decode_cache)
```

```python
import math

import jax
import jax.numpy as jnp
from jax import lax
from jax.experimental import pallas as pl
from jax.experimental.pallas import tpu as pltpu
from jax.sharding import PartitionSpec as P

HD = 128
TOP = 4
EXPERTS = 32
PAGE = 8
CAP = 48
ROW = 4
CORES = 2
CHIPS = 2
BF = jnp.bfloat16
F32 = jnp.float32
BOTH = ("head", "tok")
INTRA = [(0, 1), (1, 0), (2, 3), (3, 2)]
CROSS = [(0, 2), (2, 0), (1, 3), (3, 1)]


def attention_kernel(ids_col, ids_row, own, past, out):
    block = out.shape[2] * 2
    scale = 1.0 / math.sqrt(HD)
    span = ROW * block
    row_pos = lax.broadcasted_iota(jnp.int32, (block, block), 0)
    col_pos = lax.broadcasted_iota(jnp.int32, (block, block), 1)
    causal = col_pos <= row_pos
    for y in range(ROW):
        query = own[y, :, 0:HD]
        query_ids = ids_col[pl.ds(y * block, block), 0:1]
        pieces = []
        for b in range(y, ROW):
            key = past[b, :, 0:HD]
            key_ids = ids_row[0:1, pl.ds(b * block, block)]
            score = lax.dot_general(
                query, key, (((1,), (1,)), ((), ())), preferred_element_type=F32
            )
            pieces.append(jnp.where(query_ids == key_ids, score * scale, -1e30))
        for b in range(y + 1):
            key = own[b, :, HD : 2 * HD]
            key_ids = ids_row[0:1, pl.ds(span + b * block, block)]
            score = lax.dot_general(
                query, key, (((1,), (1,)), ((), ())), preferred_element_type=F32
            )
            allowed = query_ids == key_ids
            if b == y:
                allowed = allowed & causal
            pieces.append(jnp.where(allowed, score * scale, -1e30))
        top = pieces[0].max(-1, keepdims=True)
        for piece in pieces[1:]:
            top = jnp.maximum(top, piece.max(-1, keepdims=True))
        weights = [jnp.exp(piece - top) for piece in pieces]
        total = weights[0].sum(-1, keepdims=True)
        for weight in weights[1:]:
            total = total + weight.sum(-1, keepdims=True)
        inverse = 1.0 / total
        mixed = jnp.zeros((block, HD), F32)
        index = 0
        for b in range(y, ROW):
            prob = (weights[index] * inverse).astype(BF)
            mixed += jnp.dot(prob, past[b, :, HD : 2 * HD], preferred_element_type=F32)
            index += 1
        for b in range(y + 1):
            prob = (weights[index] * inverse).astype(BF)
            mixed += jnp.dot(prob, own[b, :, 2 * HD : 3 * HD], preferred_element_type=F32)
            index += 1
        half = block // 2
        out[0, y] = mixed[:half].astype(BF)
        out[1, y] = mixed[half:].astype(BF)


def attention(ids_col, ids_row, own, past):
    block = own.shape[1]
    return pl.pallas_call(
        attention_kernel,
        out_shape=jax.ShapeDtypeStruct((2, ROW, block // 2, HD), BF),
        in_specs=[pl.BlockSpec(memory_space=pltpu.VMEM)] * 4,
        out_specs=pl.BlockSpec(memory_space=pltpu.VMEM),
        compiler_params=pltpu.CompilerParams(vmem_limit_bytes=48 << 20),
        cost_estimate=pl.CostEstimate(
            flops=4 * 5 * ROW * block * block * HD,
            bytes_accessed=6 << 20,
            transcendentals=5 * ROW * block * block,
        ),
        name="row_attention",
    )(ids_col, ids_row, own, past)


def page_copy(keys, values, page_slots, tok_rows, tok_count, head_count, tok_index, heads_here):
    pages_here = tok_rows // PAGE
    quarter_page = PAGE // head_count
    width = heads_here * HD
    slots_all = page_slots.reshape(tok_count, pages_here)
    owner_all = slots_all // pages_here
    mine = lax.dynamic_index_in_dim(owner_all, tok_index, 0, keepdims=False)
    pick = (jnp.arange(tok_count, dtype=jnp.int32)[:, None] == mine[None, :]).astype(BF)
    kv = jnp.stack(
        [
            keys.reshape(pages_here, head_count, quarter_page, width),
            values.reshape(pages_here, head_count, quarter_page, width),
        ],
        3,
    )
    spread = jnp.einsum("op,phqsw->hoqsw", pick, kv, preferred_element_type=F32).astype(BF)
    spread = spread.reshape(head_count * tok_count, quarter_page * 2, width)
    landed = lax.all_to_all(spread, BOTH, split_axis=0, concat_axis=0, tiled=True)
    arrival = jnp.sum(jnp.where(owner_all == tok_index, slots_all % pages_here, 0), 1)
    place = (jnp.arange(pages_here, dtype=jnp.int32)[:, None] == arrival[None, :]).astype(BF)
    landed = landed.reshape(head_count, tok_count, quarter_page, 2, width)
    cache = jnp.einsum("ro,hoqsw->rqshw", place, landed, preferred_element_type=F32).astype(BF)
    return cache.reshape(pages_here, quarter_page, 2 * head_count * width)


def per_device(
    hidden_in,
    queries,
    keys,
    values,
    request_ids,
    out_proj,
    norm_gain,
    expert_gate_up,
    expert_down,
    shared_gate_up,
    shared_down,
    shared_gate,
    routes,
    route_weights,
    page_slots,
):
    tok_rows, model_width = hidden_in.shape
    head_width = queries.shape[1]
    heads_here = head_width // HD
    tok_count = lax.axis_size("tok")
    head_count = lax.axis_size("head")
    tok_index = lax.axis_index("tok")
    head_index = lax.axis_index("head")
    core = head_index % CORES
    column_width = model_width // head_count
    rows_of_blocks = tok_count // ROW
    half = tok_rows // 2
    slots_core = CAP // CORES

    gate_up_own = jnp.transpose(expert_gate_up[0], (1, 2, 0))
    down_own = expert_down[0]
    out_peer = lax.ppermute(out_proj, "head", INTRA)
    gate_up_peer = lax.ppermute(gate_up_own, "head", INTRA)
    down_peer = lax.ppermute(down_own, "head", INTRA)

    packed = jnp.stack(
        [
            jnp.concatenate(
                [part[:, i * HD : (i + 1) * HD] for part in (queries, keys, values)], 1
            )
            for i in range(heads_here)
        ],
        0,
    )
    row_groups = [[r * ROW + y for y in range(ROW)] for r in range(rows_of_blocks)]
    own = lax.all_to_all(
        packed, "tok", split_axis=0, concat_axis=0, tiled=True, axis_index_groups=row_groups
    )
    past = lax.ppermute(
        own[:, :, HD:], "tok", [(s, s + ROW) for s in range(tok_count - ROW)]
    )
    span = ROW * tok_rows
    base = (tok_index // ROW) * span
    padded_ids = jnp.concatenate([jnp.full((span,), -1, jnp.int32), request_ids], 0)
    window_ids = lax.dynamic_slice_in_dim(padded_ids, base, 2 * span, 0)
    ids_row = window_ids[None, :]
    ids_col = jnp.broadcast_to(window_ids[span:, None], (span, HD))
    attended = attention(ids_col, ids_row, own, past)

    core_groups = [
        [
            (chip * CORES + c) * tok_count + r * ROW + y
            for c in range(CORES)
            for y in range(ROW)
        ]
        for chip in range(CHIPS)
        for r in range(rows_of_blocks)
    ]
    gathered = lax.all_to_all(
        attended.reshape(CORES * ROW, half, HD),
        BOTH,
        split_axis=0,
        concat_axis=0,
        tiled=True,
        axis_index_groups=core_groups,
    ).reshape(CORES, ROW, half, HD)
    att_own = lax.dynamic_index_in_dim(gathered, core, 0, keepdims=False)
    att_peer = lax.dynamic_index_in_dim(gathered, 1 - core, 0, keepdims=False)
    att = jnp.concatenate([att_own[y] for y in range(ROW)] + [att_peer[y] for y in range(ROW)], 1)
    projected = jnp.dot(att[:, :head_width], out_proj, preferred_element_type=F32) + jnp.dot(
        att[:, head_width:], out_peer, preferred_element_type=F32
    )
    projected_far = lax.ppermute(projected.astype(BF), "head", CROSS)
    hidden_half = lax.dynamic_slice_in_dim(hidden_in, core * half, half, 0)
    resid = hidden_half.astype(F32) + (projected + projected_far.astype(F32))
    mean_square = jnp.mean(resid * resid, axis=-1, keepdims=True)
    normed_own = (resid * lax.rsqrt(mean_square + 1e-06) * norm_gain).astype(BF)
    normed_peer = lax.ppermute(normed_own, "head", INTRA)

    expert_ids = jnp.arange(EXPERTS, dtype=jnp.int32)
    named = routes[:, :, None] == expert_ids[None, None, :]
    onehot = jnp.sum(named.astype(F32), 1)
    weight_of = jnp.sum(jnp.where(named, route_weights[:, :, None], 0.0), 1)
    earlier = (
        jnp.arange(tok_rows, dtype=jnp.int32)[None, :] < jnp.arange(tok_rows, dtype=jnp.int32)[:, None]
    ).astype(BF)
    rank = jnp.dot(earlier, onehot.astype(BF), preferred_element_type=F32).astype(jnp.int32)
    rank_t = jnp.where(onehot > 0, rank, -1).T
    weight_t = weight_of.T
    rank_rel = jnp.where(core == 0, rank_t, jnp.roll(rank_t, half, 1))
    place = jnp.arange(slots_core, dtype=jnp.int32) * CORES
    select = (rank_rel[:, None, :] == (place + core)[None, :, None]).astype(BF)
    select = select.reshape(EXPERTS * slots_core, tok_rows)
    normed_rel = jnp.concatenate([normed_own, normed_peer], 0)
    outgoing = jnp.dot(select, normed_rel, preferred_element_type=F32).astype(BF)
    arrived = lax.all_to_all(
        outgoing.reshape(tok_count, slots_core, model_width),
        "tok",
        split_axis=0,
        concat_axis=0,
        tiled=True,
    ).reshape(tok_count * slots_core, model_width)

    normed_abs = jnp.where(
        core == 0, normed_rel, jnp.concatenate([normed_peer, normed_own], 0)
    )
    shared_both = jnp.einsum("td,dgf->tgf", normed_abs, shared_gate_up, preferred_element_type=F32)
    shared_act = (jax.nn.silu(shared_both[:, 0, :]) * shared_both[:, 1, :]).astype(BF)
    shared_scale = jax.nn.sigmoid(jnp.dot(normed_abs, shared_gate, preferred_element_type=F32))
    shared_term = shared_scale[:, None] * jnp.dot(
        shared_act, shared_down, preferred_element_type=F32
    )
    shared_cols = lax.psum_scatter(
        shared_term.astype(BF), "head", scatter_dimension=1, tiled=True
    ).astype(F32)

    def expert(gate_up, down):
        gate = lax.dot_general(
            arrived, gate_up[0], (((1,), (1,)), ((), ())), preferred_element_type=F32
        )
        up = lax.dot_general(
            arrived, gate_up[1], (((1,), (1,)), ((), ())), preferred_element_type=F32
        )
        active = (jax.nn.silu(gate) * up).astype(BF)
        return jnp.dot(active, down, preferred_element_type=F32)

    partial = (expert(gate_up_own, down_own) + expert(gate_up_peer, down_peer)).astype(BF)
    partial = partial.reshape(tok_count, slots_core, head_count, column_width)
    partial = jnp.transpose(partial, (2, 0, 1, 3)).reshape(
        head_count * tok_count, slots_core, column_width
    )
    returned = lax.all_to_all(partial, BOTH, split_axis=0, concat_axis=0, tiled=True)
    returned = returned.reshape(CHIPS, CORES * EXPERTS * slots_core, column_width)

    wanted = place[None, :] + jnp.arange(CORES, dtype=jnp.int32)[:, None]
    spread = jnp.where(
        rank_t[None, :, None, :] == wanted[:, None, :, None], weight_t[None, :, None, :], 0.0
    ).reshape(CORES * EXPERTS * slots_core, tok_rows)
    high = spread.astype(BF)
    low = (spread - high.astype(F32)).astype(BF)
    contract = (((0,), (0,)), ((), ()))
    moe_cols = sum(
        lax.dot_general(side, returned[chip], contract, preferred_element_type=F32)
        for chip in range(CHIPS)
        for side in (high, low)
    )

    own_cols = lax.dynamic_slice_in_dim(resid, head_index * column_width, column_width, 1)
    peer_cols = lax.dynamic_slice_in_dim(
        resid, (head_index + 1 - 2 * core) * column_width, column_width, 1
    )
    from_peer = lax.ppermute(peer_cols, "head", INTRA)
    resid_cols = jnp.where(
        core == 0,
        jnp.concatenate([own_cols, from_peer], 0),
        jnp.concatenate([from_peer, own_cols], 0),
    )
    layer_out = (resid_cols + shared_cols + moe_cols).astype(BF)
    decode_cache = page_copy(
        keys, values, page_slots, tok_rows, tok_count, head_count, tok_index, heads_here
    )
    return (layer_out, decode_cache)


def solution(mesh):
    in_specs = (
        P("tok", None),
        P("tok", "head"),
        P("tok", "head"),
        P("tok", "head"),
        P(),
        P("head", None),
        P(),
        P("tok", None, None, "head"),
        P("tok", "head", None),
        P(None, None, "head"),
        P("head", None),
        P(),
        P("tok", None),
        P("tok", None),
        P(),
    )
    out_specs = (P("tok", "head"), P("tok", "head", None))
    return jax.shard_map(
        per_device, mesh=mesh, in_specs=in_specs, out_specs=out_specs, check_vma=False
    )
```

```python
import math

import jax
import jax.numpy as jnp
from jax import lax
from jax.experimental import pallas as pl
from jax.experimental.pallas import tpu as pltpu
from jax.sharding import PartitionSpec as P

HD = 128
TOP = 4
EXPERTS = 32
PAGE = 8
CAP = 48
ROW = 4
CORES = 2
CHIPS = 2
BF = jnp.bfloat16
F32 = jnp.float32
BOTH = ("head", "tok")
INTRA = [(0, 1), (1, 0), (2, 3), (3, 2)]
CROSS = [(0, 2), (2, 0), (1, 3), (3, 1)]


def attention_kernel(ids_col, ids_row, own, past, out):
    block = out.shape[2] * 2
    scale = 1.0 / math.sqrt(HD)
    span = ROW * block
    row_pos = lax.broadcasted_iota(jnp.int32, (block, block), 0)
    col_pos = lax.broadcasted_iota(jnp.int32, (block, block), 1)
    causal = col_pos <= row_pos
    for y in range(ROW):
        query = own[y, :, 0:HD]
        query_ids = ids_col[pl.ds(y * block, block), 0:1]
        pieces = []
        for b in range(y, ROW):
            key = past[b, :, 0:HD]
            key_ids = ids_row[0:1, pl.ds(b * block, block)]
            score = lax.dot_general(
                query, key, (((1,), (1,)), ((), ())), preferred_element_type=F32
            )
            pieces.append(jnp.where(query_ids == key_ids, score * scale, -1e30))
        for b in range(y + 1):
            key = own[b, :, HD : 2 * HD]
            key_ids = ids_row[0:1, pl.ds(span + b * block, block)]
            score = lax.dot_general(
                query, key, (((1,), (1,)), ((), ())), preferred_element_type=F32
            )
            allowed = query_ids == key_ids
            if b == y:
                allowed = allowed & causal
            pieces.append(jnp.where(allowed, score * scale, -1e30))
        top = pieces[0].max(-1, keepdims=True)
        for piece in pieces[1:]:
            top = jnp.maximum(top, piece.max(-1, keepdims=True))
        weights = [jnp.exp(piece - top) for piece in pieces]
        total = weights[0].sum(-1, keepdims=True)
        for weight in weights[1:]:
            total = total + weight.sum(-1, keepdims=True)
        inverse = 1.0 / total
        mixed = jnp.zeros((block, HD), F32)
        index = 0
        for b in range(y, ROW):
            prob = (weights[index] * inverse).astype(BF)
            mixed += jnp.dot(prob, past[b, :, HD : 2 * HD], preferred_element_type=F32)
            index += 1
        for b in range(y + 1):
            prob = (weights[index] * inverse).astype(BF)
            mixed += jnp.dot(prob, own[b, :, 2 * HD : 3 * HD], preferred_element_type=F32)
            index += 1
        half = block // 2
        out[0, y] = mixed[:half].astype(BF)
        out[1, y] = mixed[half:].astype(BF)


def attention(ids_col, ids_row, own, past):
    block = own.shape[1]
    return pl.pallas_call(
        attention_kernel,
        out_shape=jax.ShapeDtypeStruct((2, ROW, block // 2, HD), BF),
        in_specs=[pl.BlockSpec(memory_space=pltpu.VMEM)] * 4,
        out_specs=pl.BlockSpec(memory_space=pltpu.VMEM),
        compiler_params=pltpu.CompilerParams(vmem_limit_bytes=24 << 20),
        cost_estimate=pl.CostEstimate(
            flops=4 * 5 * ROW * block * block * HD,
            bytes_accessed=6 << 20,
            transcendentals=5 * ROW * block * block,
        ),
        name="row_attention",
    )(ids_col, ids_row, own, past)


def project_kernel(core, att, out_own, out_peer, total, total_low):
    c = core[0]
    left = jnp.concatenate([att[c, y] for y in range(ROW)], 1)
    right = jnp.concatenate([att[1 - c, y] for y in range(ROW)], 1)
    width = total.shape[1]
    step = width // 4
    for i in range(4):
        cols = pl.ds(i * step, step)
        part = jnp.dot(left, out_own[:, cols], preferred_element_type=F32) + jnp.dot(
            right, out_peer[:, cols], preferred_element_type=F32
        )
        total[:, cols] = part
        total_low[:, cols] = part.astype(BF)


def project(core, att, out_own, out_peer):
    rows = att.shape[2]
    depth, width = out_own.shape
    vmem = pl.BlockSpec(memory_space=pltpu.VMEM)
    return pl.pallas_call(
        project_kernel,
        out_shape=(
            jax.ShapeDtypeStruct((rows, width), F32),
            jax.ShapeDtypeStruct((rows, width), BF),
        ),
        in_specs=[pl.BlockSpec(memory_space=pltpu.SMEM), vmem, vmem, vmem],
        out_specs=(vmem, vmem),
        compiler_params=pltpu.CompilerParams(vmem_limit_bytes=24 << 20),
        cost_estimate=pl.CostEstimate(
            flops=4 * rows * depth * width, bytes_accessed=6 << 20, transcendentals=0
        ),
        name="project",
    )(core, att, out_own, out_peer)


def norm_kernel(core, hidden, near, far, gain, resid, normed):
    rows = near.shape[0]
    start = pl.multiple_of(core[0] * rows, rows)
    block = rows // 4
    for i in range(4):
        here = pl.ds(i * block, block)
        value = hidden[pl.ds(start + i * block, block), :].astype(F32) + (
            near[here, :] + far[here, :].astype(F32)
        )
        resid[here, :] = value
        mean_square = jnp.mean(value * value, axis=-1, keepdims=True)
        normed[here, :] = (value * lax.rsqrt(mean_square + 1e-06) * gain[...]).astype(BF)


def add_and_norm(core, hidden, near, far, gain):
    rows, width = near.shape
    vmem = pl.BlockSpec(memory_space=pltpu.VMEM)
    return pl.pallas_call(
        norm_kernel,
        out_shape=(
            jax.ShapeDtypeStruct((rows, width), F32),
            jax.ShapeDtypeStruct((rows, width), BF),
        ),
        in_specs=[pl.BlockSpec(memory_space=pltpu.SMEM), vmem, vmem, vmem, vmem],
        out_specs=(vmem, vmem),
        compiler_params=pltpu.CompilerParams(vmem_limit_bytes=16 << 20),
        cost_estimate=pl.CostEstimate(
            flops=8 * rows * width, bytes_accessed=4 << 20, transcendentals=rows
        ),
        name="add_and_norm",
    )(core, hidden, near, far, gain)


def expert_kernel(
    x_hbm, both_own, both_peer, down_own, down_peer, out_hbm, x, gate, up, down, act, out, sems, out_sems
):
    hidden = both_own.shape[1]
    rows = x.shape[0]
    groups, _, width = out.shape
    block = rows // 2
    first = pl.ds(0, hidden)
    second = pl.ds(hidden, hidden)
    copies = [
        pltpu.make_async_copy(x_hbm, x, sems.at[0]),
        pltpu.make_async_copy(both_own.at[0], gate.at[first], sems.at[1]),
        pltpu.make_async_copy(both_peer.at[0], gate.at[second], sems.at[2]),
        pltpu.make_async_copy(both_own.at[1], up.at[first], sems.at[3]),
        pltpu.make_async_copy(both_peer.at[1], up.at[second], sems.at[4]),
        pltpu.make_async_copy(down_own, down.at[first], sems.at[5]),
        pltpu.make_async_copy(down_peer, down.at[second], sems.at[6]),
    ]
    for copy in copies:
        copy.start()
    for copy in copies[:5]:
        copy.wait()

    @pl.loop(0, 2)
    def _(m):
        here = pl.ds(pl.multiple_of(m * block, block), block)
        left = x[here, :]
        contract = (((1,), (1,)), ((), ()))
        g = lax.dot_general(left, gate[...], contract, preferred_element_type=F32)
        u = lax.dot_general(left, up[...], contract, preferred_element_type=F32)
        act[here, :] = (g / (1.0 + jnp.exp(-g)) * u).astype(BF)

    for copy in copies[5:]:
        copy.wait()

    @pl.loop(0, 2)
    def _(m):
        here = pl.ds(pl.multiple_of(m * block, block), block)
        left = act[here, :]
        for i in range(groups):
            result = jnp.dot(
                left, down[:, i * width : (i + 1) * width], preferred_element_type=F32
            )
            out[i, here, :] = result.astype(BF)
            pltpu.make_async_copy(
                out.at[i, here], out_hbm.at[i, here], out_sems.at[m, i]
            ).start()

    for m in range(2):
        here = pl.ds(m * block, block)
        for i in range(groups):
            pltpu.make_async_copy(
                out.at[i, here], out_hbm.at[i, here], out_sems.at[m, i]
            ).wait()


def experts(x, both_own, both_peer, down_own, down_peer, groups):
    rows, depth = x.shape
    hidden, width = down_own.shape
    column_width = width // groups
    anywhere = pl.BlockSpec(memory_space=pltpu.HBM)
    return pl.pallas_call(
        expert_kernel,
        out_shape=jax.ShapeDtypeStruct((groups, rows, column_width), BF),
        in_specs=[anywhere] * 5,
        out_specs=anywhere,
        scratch_shapes=[
            pltpu.VMEM((rows, depth), BF),
            pltpu.VMEM((2 * hidden, depth), BF),
            pltpu.VMEM((2 * hidden, depth), BF),
            pltpu.VMEM((2 * hidden, width), BF),
            pltpu.VMEM((rows, 2 * hidden), BF),
            pltpu.VMEM((groups, rows, column_width), BF),
            pltpu.SemaphoreType.DMA((7,)),
            pltpu.SemaphoreType.DMA((2, groups)),
        ],
        compiler_params=pltpu.CompilerParams(vmem_limit_bytes=28 << 20),
        cost_estimate=pl.CostEstimate(
            flops=12 * rows * depth * hidden,
            bytes_accessed=15 << 20,
            transcendentals=2 * rows * hidden,
        ),
        name="experts",
    )(x, both_own, both_peer, down_own, down_peer)


def combine_kernel(core, high, low, returned, mine, peers, shared, out):
    rows = mine.shape[0]
    sides = (high, low)
    total = shared[...]
    for chip in range(returned.shape[0]):
        for side in sides:
            total += jnp.dot(side[...], returned[chip], preferred_element_type=F32)
    first = core[0] == 0
    low_half = jnp.where(first, mine[...], peers[...])
    high_half = jnp.where(first, peers[...], mine[...])
    out[0:rows, :] = (total[0:rows] + low_half).astype(BF)
    out[rows : 2 * rows, :] = (total[rows:] + high_half).astype(BF)


def combine(core, high, low, returned, mine, peers, shared):
    vmem = pl.BlockSpec(memory_space=pltpu.VMEM)
    rows, width = shared.shape
    return pl.pallas_call(
        combine_kernel,
        out_shape=jax.ShapeDtypeStruct((rows, width), BF),
        in_specs=[pl.BlockSpec(memory_space=pltpu.SMEM)] + [vmem] * 6,
        out_specs=vmem,
        compiler_params=pltpu.CompilerParams(vmem_limit_bytes=24 << 20),
        cost_estimate=pl.CostEstimate(
            flops=8 * rows * width * high.shape[1], bytes_accessed=7 << 20, transcendentals=0
        ),
        name="combine",
    )(core, high, low, returned, mine, peers, shared)


def page_pieces(keys, values, owner_all, tok_count, head_count, tok_index):
    pages_here = owner_all.shape[1]
    tok_rows = keys.shape[0]
    quarter_page = PAGE // head_count
    mine = lax.dynamic_index_in_dim(owner_all, tok_index, 0, keepdims=False)
    row = jnp.arange(tok_rows, dtype=jnp.int32)
    quarter = row // (tok_count * quarter_page)
    owner = row // quarter_page % tok_count
    line = quarter * quarter_page + row % quarter_page
    token_owner = jnp.repeat(mine, PAGE)
    token_line = jnp.arange(tok_rows, dtype=jnp.int32) % PAGE
    pick = (
        (owner[:, None] == token_owner[None, :]) & (line[:, None] == token_line[None, :])
    ).astype(BF)
    parts = [
        jnp.dot(pick, part, preferred_element_type=F32).astype(BF) for part in (keys, values)
    ]
    return jnp.concatenate(parts, 1).reshape(head_count * tok_count, quarter_page, -1)


def place_pages(landed, slots_all, owner_all, tok_count, head_count, tok_index):
    pages_here = owner_all.shape[1]
    quarter_page = PAGE // head_count
    rows = pages_here * quarter_page
    arrival = jnp.sum(jnp.where(owner_all == tok_index, slots_all % pages_here, 0), 1)
    row = jnp.arange(rows, dtype=jnp.int32)
    target = jnp.repeat(arrival, quarter_page) * quarter_page + row % quarter_page
    place = (row[:, None] == target[None, :]).astype(BF)
    landed = landed.reshape(head_count, rows, -1)
    width = landed.shape[2] // 2
    placed = [
        jnp.dot(place, landed[h], preferred_element_type=F32).astype(BF)
        for h in range(head_count)
    ]
    cache = jnp.concatenate(
        [p[:, :width] for p in placed] + [p[:, width:] for p in placed], 1
    )
    return cache.reshape(pages_here, quarter_page, 2 * head_count * width)


def per_device(
    hidden_in,
    queries,
    keys,
    values,
    request_ids,
    out_proj,
    norm_gain,
    expert_gate_up,
    expert_down,
    shared_gate_up,
    shared_down,
    shared_gate,
    routes,
    route_weights,
    page_slots,
):
    tok_rows, model_width = hidden_in.shape
    head_width = queries.shape[1]
    heads_here = head_width // HD
    tok_count = lax.axis_size("tok")
    head_count = lax.axis_size("head")
    tok_index = lax.axis_index("tok")
    head_index = lax.axis_index("head")
    core = head_index % CORES
    column_width = model_width // head_count
    rows_of_blocks = tok_count // ROW
    half = tok_rows // 2
    slots_core = CAP // CORES

    gate_up_own = jnp.transpose(expert_gate_up[0], (1, 2, 0))
    down_own = expert_down[0]
    out_peer = lax.ppermute(out_proj, "head", INTRA)
    gate_up_peer = lax.ppermute(gate_up_own, "head", INTRA)
    down_peer = lax.ppermute(down_own, "head", INTRA)

    packed = jnp.stack(
        [
            jnp.concatenate(
                [part[:, i * HD : (i + 1) * HD] for part in (queries, keys, values)], 1
            )
            for i in range(heads_here)
        ],
        0,
    )
    row_groups = [[r * ROW + y for y in range(ROW)] for r in range(rows_of_blocks)]
    own = lax.all_to_all(
        packed, "tok", split_axis=0, concat_axis=0, tiled=True, axis_index_groups=row_groups
    )
    slots_all = page_slots.reshape(tok_count, tok_rows // PAGE)
    owner_all = slots_all // (tok_rows // PAGE)
    pieces = page_pieces(keys, values, owner_all, tok_count, head_count, tok_index)
    pieces, own = lax.optimization_barrier((pieces, own))
    landed = lax.all_to_all(pieces, BOTH, split_axis=0, concat_axis=0, tiled=True)
    past = lax.ppermute(
        own[:, :, HD:], "tok", [(s, s + ROW) for s in range(tok_count - ROW)]
    )
    span = ROW * tok_rows
    base = (tok_index // ROW) * span
    padded_ids = jnp.concatenate([jnp.full((span,), -1, jnp.int32), request_ids], 0)
    window_ids = lax.dynamic_slice_in_dim(padded_ids, base, 2 * span, 0)
    ids_row = window_ids[None, :]
    ids_col = jnp.broadcast_to(window_ids[span:, None], (span, HD))
    past, landed = lax.optimization_barrier((past, landed))
    attended = attention(ids_col, ids_row, own, past)

    core_groups = [
        [
            (chip * CORES + c) * tok_count + r * ROW + y
            for c in range(CORES)
            for y in range(ROW)
        ]
        for chip in range(CHIPS)
        for r in range(rows_of_blocks)
    ]
    gathered = lax.all_to_all(
        attended.reshape(CORES * ROW, half, HD),
        BOTH,
        split_axis=0,
        concat_axis=0,
        tiled=True,
        axis_index_groups=core_groups,
    ).reshape(CORES, ROW, half, HD)
    core_ref = core.reshape(1)
    projected, projected_low = project(core_ref, gathered, out_proj, out_peer)
    projected_far = lax.ppermute(projected_low, "head", CROSS)
    resid, normed_own = add_and_norm(
        core_ref, hidden_in, projected, projected_far, norm_gain[None, :]
    )
    normed_peer = lax.ppermute(normed_own, "head", INTRA)

    expert_ids = jnp.arange(EXPERTS, dtype=jnp.int32)
    named = routes[:, :, None] == expert_ids[None, None, :]
    onehot = jnp.sum(named.astype(F32), 1)
    weight_of = jnp.sum(jnp.where(named, route_weights[:, :, None], 0.0), 1)
    earlier = (
        jnp.arange(tok_rows, dtype=jnp.int32)[None, :] < jnp.arange(tok_rows, dtype=jnp.int32)[:, None]
    ).astype(BF)
    rank = jnp.dot(earlier, onehot.astype(BF), preferred_element_type=F32).astype(jnp.int32)
    rank_t = jnp.where(onehot > 0, rank, -1).T
    weight_t = weight_of.T
    rank_rel = jnp.where(core == 0, rank_t, jnp.roll(rank_t, half, 1))
    place = jnp.arange(slots_core, dtype=jnp.int32) * CORES
    select = (rank_rel[:, None, :] == (place + core)[None, :, None]).astype(BF)
    select = select.reshape(EXPERTS * slots_core, tok_rows)
    normed_rel = jnp.concatenate([normed_own, normed_peer], 0)
    outgoing = jnp.dot(select, normed_rel, preferred_element_type=F32).astype(BF)
    arrived = lax.all_to_all(
        outgoing.reshape(tok_count, slots_core, model_width),
        "tok",
        split_axis=0,
        concat_axis=0,
        tiled=True,
    ).reshape(tok_count * slots_core, model_width)

    normed_abs = jnp.where(
        core == 0, normed_rel, jnp.concatenate([normed_peer, normed_own], 0)
    )
    shared_both = jnp.einsum("td,dgf->tgf", normed_abs, shared_gate_up, preferred_element_type=F32)
    shared_act = (jax.nn.silu(shared_both[:, 0, :]) * shared_both[:, 1, :]).astype(BF)
    shared_scale = jax.nn.sigmoid(jnp.dot(normed_abs, shared_gate, preferred_element_type=F32))
    shared_term = shared_scale[:, None] * jnp.dot(
        shared_act, shared_down, preferred_element_type=F32
    )
    chip = head_index // CORES
    chip_width = CORES * column_width
    shared_near = lax.dynamic_slice_in_dim(shared_term, chip * chip_width, chip_width, 1)
    shared_send = lax.dynamic_slice_in_dim(
        shared_term, (1 - chip) * chip_width, chip_width, 1
    ).astype(BF)
    shared_near, shared_send, arrived = lax.optimization_barrier(
        (shared_near, shared_send, arrived)
    )
    shared_far = lax.ppermute(shared_send, "head", CROSS)

    partial = experts(arrived, gate_up_own, gate_up_peer, down_own, down_peer, head_count)
    partial = partial.reshape(head_count * tok_count, slots_core, column_width)
    returned = lax.all_to_all(partial, BOTH, split_axis=0, concat_axis=0, tiled=True)
    returned = returned.reshape(CHIPS, CORES * EXPERTS * slots_core, column_width)

    wanted = place[None, :] + jnp.arange(CORES, dtype=jnp.int32)[:, None]
    spread = jnp.where(
        rank_t[None, :, None, :] == wanted[:, None, :, None], weight_t[None, :, None, :], 0.0
    ).reshape(CORES * EXPERTS * slots_core, tok_rows)
    high = spread.astype(BF)
    low = (spread - high.astype(F32)).astype(BF).T
    high = high.T
    shared_chip = shared_near + shared_far.astype(F32)
    shared_own = lax.dynamic_slice_in_dim(shared_chip, core * column_width, column_width, 1)
    shared_peer = lax.dynamic_slice_in_dim(
        shared_chip, (1 - core) * column_width, column_width, 1
    ).astype(BF)
    shared_cols = shared_own + lax.ppermute(shared_peer, "head", INTRA).astype(F32)
    own_cols = lax.dynamic_slice_in_dim(resid, head_index * column_width, column_width, 1)
    peer_cols = lax.dynamic_slice_in_dim(
        resid, (head_index + 1 - 2 * core) * column_width, column_width, 1
    )
    from_peer = lax.ppermute(peer_cols, "head", INTRA)
    layer_out = combine(core_ref, high, low, returned, own_cols, from_peer, shared_cols)
    decode_cache = place_pages(landed, slots_all, owner_all, tok_count, head_count, tok_index)
    return (layer_out, decode_cache)


def solution(mesh):
    in_specs = (
        P("tok", None),
        P("tok", "head"),
        P("tok", "head"),
        P("tok", "head"),
        P(),
        P("head", None),
        P(),
        P("tok", None, None, "head"),
        P("tok", "head", None),
        P(None, None, "head"),
        P("head", None),
        P(),
        P("tok", None),
        P("tok", None),
        P(),
    )
    out_specs = (P("tok", "head"), P("tok", "head", None))
    return jax.shard_map(
        per_device, mesh=mesh, in_specs=in_specs, out_specs=out_specs, check_vma=False
    )
```

```python
import math

import jax
import jax.numpy as jnp
from jax import lax
from jax.experimental import pallas as pl
from jax.experimental.pallas import tpu as pltpu
from jax.sharding import PartitionSpec as P

HD = 128
TOP = 4
EXPERTS = 32
PAGE = 8
CAP = 48
ROW = 4
CORES = 2
CHIPS = 2
BF = jnp.bfloat16
F32 = jnp.float32
BOTH = ("head", "tok")
INTRA = [(0, 1), (1, 0), (2, 3), (3, 2)]
CROSS = [(0, 2), (2, 0), (1, 3), (3, 1)]


def attention_kernel(
    place, ids_col_hbm, ids_row_hbm, query_hbm, own_hbm, past_hbm, out_hbm,
    ids_col, ids_row, query_parts, own, past, out, sems, out_sems,
):
    block = out.shape[2] * 2
    pairs = (
        (query_hbm, query_parts),
        (own_hbm, own),
        (past_hbm, past),
        (ids_col_hbm, ids_col),
        (ids_row_hbm, ids_row),
    )
    copies = [
        pltpu.make_async_copy(source, target, sems.at[i])
        for i, (source, target) in enumerate(pairs)
    ]
    for copy in copies:
        copy.start()
    for copy in copies:
        copy.wait()
    stores = []
    scale = 1.0 / math.sqrt(HD)
    span = ROW * block
    row_pos = lax.broadcasted_iota(jnp.int32, (block, block), 0)
    col_pos = lax.broadcasted_iota(jnp.int32, (block, block), 1)
    causal = col_pos <= row_pos
    for y in range(ROW):
        query = query_parts[lax.rem(place[0] + (ROW - y), ROW)]
        query_ids = ids_col[pl.ds(y * block, block), 0:1]
        pieces = []
        for b in range(y, ROW):
            key = past[b, :, 0:HD]
            key_ids = ids_row[0:1, pl.ds(b * block, block)]
            score = lax.dot_general(
                query, key, (((1,), (1,)), ((), ())), preferred_element_type=F32
            )
            pieces.append(jnp.where(query_ids == key_ids, score * scale, -1e30))
        for b in range(y + 1):
            key = own[b, :, 0:HD]
            key_ids = ids_row[0:1, pl.ds(span + b * block, block)]
            score = lax.dot_general(
                query, key, (((1,), (1,)), ((), ())), preferred_element_type=F32
            )
            allowed = query_ids == key_ids
            if b == y:
                allowed = allowed & causal
            pieces.append(jnp.where(allowed, score * scale, -1e30))
        top = pieces[0].max(-1, keepdims=True)
        for piece in pieces[1:]:
            top = jnp.maximum(top, piece.max(-1, keepdims=True))
        weights = [jnp.exp(piece - top) for piece in pieces]
        total = weights[0].sum(-1, keepdims=True)
        for weight in weights[1:]:
            total = total + weight.sum(-1, keepdims=True)
        inverse = 1.0 / total
        mixed = jnp.zeros((block, HD), F32)
        index = 0
        for b in range(y, ROW):
            prob = (weights[index] * inverse).astype(BF)
            mixed += jnp.dot(prob, past[b, :, HD : 2 * HD], preferred_element_type=F32)
            index += 1
        for b in range(y + 1):
            prob = (weights[index] * inverse).astype(BF)
            mixed += jnp.dot(prob, own[b, :, HD : 2 * HD], preferred_element_type=F32)
            index += 1
        half = block // 2
        out[0, y] = mixed[:half].astype(BF)
        out[1, y] = mixed[half:].astype(BF)
        for c in range(2):
            store = pltpu.make_async_copy(out.at[c, y], out_hbm.at[c, y], out_sems.at[c, y])
            store.start()
            stores.append(store)
    for store in stores:
        store.wait()


def attention(place, ids_col, ids_row, query_parts, own, past):
    block = own.shape[1]
    hbm = pl.BlockSpec(memory_space=pltpu.HBM)
    operands = (ids_col, ids_row, query_parts, own, past)
    result = jax.ShapeDtypeStruct((2, ROW, block // 2, HD), BF)
    return pl.pallas_call(
        attention_kernel,
        out_shape=result,
        in_specs=[pl.BlockSpec(memory_space=pltpu.SMEM)] + [hbm] * 5,
        out_specs=hbm,
        scratch_shapes=[pltpu.VMEM(o.shape, o.dtype) for o in operands]
        + [
            pltpu.VMEM(result.shape, BF),
            pltpu.SemaphoreType.DMA((5,)),
            pltpu.SemaphoreType.DMA((2, ROW)),
        ],
        compiler_params=pltpu.CompilerParams(vmem_limit_bytes=58 << 20),
        cost_estimate=pl.CostEstimate(
            flops=4 * 5 * ROW * block * block * HD,
            bytes_accessed=3 << 20,
            transcendentals=5 * ROW * block * block,
        ),
        name="row_attention",
    )(place, *operands)


def project_kernel(
    core, att_hbm, own_hbm, peer_hbm, total_hbm, low_hbm,
    att, own, peer, total, total_low, att_sem, sems, out_sems,
):
    width = total.shape[1]
    step = width // 4
    att_copy = pltpu.make_async_copy(att_hbm, att, att_sem)
    att_copy.start()
    copies = []
    for i in range(4):
        cols = pl.ds(i * step, step)
        copies.append(
            (
                pltpu.make_async_copy(own_hbm.at[:, cols], own.at[:, cols], sems.at[0, i]),
                pltpu.make_async_copy(peer_hbm.at[:, cols], peer.at[:, cols], sems.at[1, i]),
            )
        )
    for pair in copies:
        for copy in pair:
            copy.start()
    att_copy.wait()
    c = core[0]
    stores = []
    left = jnp.concatenate([att[c, y] for y in range(ROW)], 1)
    right = jnp.concatenate([att[1 - c, y] for y in range(ROW)], 1)
    for i in range(4):
        cols = pl.ds(i * step, step)
        for copy in copies[i]:
            copy.wait()
        part = jnp.dot(left, own[:, cols], preferred_element_type=F32) + jnp.dot(
            right, peer[:, cols], preferred_element_type=F32
        )
        total_low[:, cols] = part.astype(BF)
        total[:, cols] = part
        for j, (source, target) in enumerate(((total_low, low_hbm), (total, total_hbm))):
            store = pltpu.make_async_copy(
                source.at[:, cols], target.at[:, cols], out_sems.at[j, i]
            )
            store.start()
            stores.append(store)
    for store in stores:
        store.wait()


def project(core, att, out_own, out_peer):
    rows = att.shape[2]
    depth, width = out_own.shape
    hbm = pl.BlockSpec(memory_space=pltpu.HBM)
    return pl.pallas_call(
        project_kernel,
        out_shape=(
            jax.ShapeDtypeStruct((rows, width), F32),
            jax.ShapeDtypeStruct((rows, width), BF),
        ),
        in_specs=[pl.BlockSpec(memory_space=pltpu.SMEM), hbm, hbm, hbm],
        out_specs=(hbm, hbm),
        scratch_shapes=[
            pltpu.VMEM(att.shape, BF),
            pltpu.VMEM((depth, width), BF),
            pltpu.VMEM((depth, width), BF),
            pltpu.VMEM((rows, width), F32),
            pltpu.VMEM((rows, width), BF),
            pltpu.SemaphoreType.DMA,
            pltpu.SemaphoreType.DMA((2, 4)),
            pltpu.SemaphoreType.DMA((2, 4)),
        ],
        compiler_params=pltpu.CompilerParams(vmem_limit_bytes=58 << 20),
        cost_estimate=pl.CostEstimate(
            flops=4 * rows * depth * width, bytes_accessed=6 << 20, transcendentals=0
        ),
        name="project",
    )(core, att, out_own, out_peer)


def norm_kernel(
    core, hidden_hbm, near_hbm, far_hbm, gain_hbm, resid_hbm, normed_hbm,
    hidden, near, far, gain, normed, sems, out_sems,
):
    rows = near.shape[0]
    parts = 2
    block = rows // parts
    start = pl.multiple_of(core[0] * rows, rows)
    gain_copy = pltpu.make_async_copy(gain_hbm, gain, sems.at[3, 0])
    gain_copy.start()
    copies = []
    for i in range(parts):
        here = pl.ds(i * block, block)
        copies.append(
            [
                pltpu.make_async_copy(near_hbm.at[here], near.at[here], sems.at[0, i]),
                pltpu.make_async_copy(far_hbm.at[here], far.at[here], sems.at[1, i]),
                pltpu.make_async_copy(
                    hidden_hbm.at[pl.ds(start + i * block, block)], hidden.at[here], sems.at[2, i]
                ),
            ]
        )
        for copy in copies[i]:
            copy.start()
    gain_copy.wait()
    stores = []
    for i in range(parts):
        here = pl.ds(i * block, block)
        for copy in copies[i]:
            copy.wait()
        value = hidden[here, :].astype(F32) + (near[here, :] + far[here, :].astype(F32))
        mean_square = jnp.mean(value * value, axis=-1, keepdims=True)
        normed[here, :] = (value * lax.rsqrt(mean_square + 1e-06) * gain[...]).astype(BF)
        near[here, :] = value
        for j, (source, target) in enumerate(((normed, normed_hbm), (near, resid_hbm))):
            store = pltpu.make_async_copy(source.at[here], target.at[here], out_sems.at[j, i])
            store.start()
            stores.append(store)
    for store in stores:
        store.wait()


def add_and_norm(core, hidden, near, far, gain):
    rows, width = near.shape
    hbm = pl.BlockSpec(memory_space=pltpu.HBM)
    return pl.pallas_call(
        norm_kernel,
        out_shape=(
            jax.ShapeDtypeStruct((rows, width), F32),
            jax.ShapeDtypeStruct((rows, width), BF),
        ),
        in_specs=[pl.BlockSpec(memory_space=pltpu.SMEM), hbm, hbm, hbm, hbm],
        out_specs=(hbm, hbm),
        scratch_shapes=[
            pltpu.VMEM((rows, width), BF),
            pltpu.VMEM((rows, width), F32),
            pltpu.VMEM((rows, width), BF),
            pltpu.VMEM((1, width), F32),
            pltpu.VMEM((rows, width), BF),
            pltpu.SemaphoreType.DMA((4, 2)),
            pltpu.SemaphoreType.DMA((2, 2)),
        ],
        compiler_params=pltpu.CompilerParams(vmem_limit_bytes=58 << 20),
        cost_estimate=pl.CostEstimate(
            flops=8 * rows * width, bytes_accessed=4 << 20, transcendentals=rows
        ),
        name="add_and_norm",
    )(core, hidden, near, far, gain)


def gather_kernel(
    select_hbm, own_hbm, peer_hbm, out_hbm, select, rows, out, sems, out_sems
):
    half = rows.shape[0] // 2
    total, block = out.shape[0], out.shape[0] // 3
    copies = [
        pltpu.make_async_copy(own_hbm, rows.at[pl.ds(0, half)], sems.at[0]),
        pltpu.make_async_copy(peer_hbm, rows.at[pl.ds(half, half)], sems.at[1]),
        pltpu.make_async_copy(select_hbm, select, sems.at[2]),
    ]
    for copy in copies:
        copy.start()
    for copy in copies:
        copy.wait()
    stores = []
    for i in range(total // block):
        here = pl.ds(i * block, block)
        out[here, :] = jnp.dot(
            select[here, :], rows[...], preferred_element_type=F32
        ).astype(BF)
        store = pltpu.make_async_copy(out.at[here], out_hbm.at[here], out_sems.at[i])
        store.start()
        stores.append(store)
    for store in stores:
        store.wait()


def gather_rows(select, own, peer):
    slots, rows = select.shape
    width = own.shape[1]
    hbm = pl.BlockSpec(memory_space=pltpu.HBM)
    return pl.pallas_call(
        gather_kernel,
        out_shape=jax.ShapeDtypeStruct((slots, width), BF),
        in_specs=[hbm, hbm, hbm],
        out_specs=hbm,
        scratch_shapes=[
            pltpu.VMEM((slots, rows), BF),
            pltpu.VMEM((rows, width), BF),
            pltpu.VMEM((slots, width), BF),
            pltpu.SemaphoreType.DMA((3,)),
            pltpu.SemaphoreType.DMA((3,)),
        ],
        compiler_params=pltpu.CompilerParams(vmem_limit_bytes=58 << 20),
        cost_estimate=pl.CostEstimate(
            flops=2 * slots * rows * width, bytes_accessed=5 << 20, transcendentals=0
        ),
        name="gather_rows",
    )(select, own, peer)


def slot_weight_kernel(rank, weight, high, low):
    slots = high.shape[1]
    per_core = CAP // CORES
    experts_here = rank.shape[1]
    lane = lax.broadcasted_iota(jnp.int32, (1, slots), 1)
    expert_of = lax.rem(lax.div(lane, per_core), experts_here)
    wanted = lax.rem(lane, per_core) * CORES + lax.div(lane, per_core * experts_here)
    expand = (
        lax.broadcasted_iota(jnp.int32, (experts_here, slots), 0) == expert_of
    ).astype(BF)
    ranks = jnp.dot(rank[...].astype(BF), expand, preferred_element_type=F32)
    hit = ranks.astype(jnp.int32) == wanted
    top = weight[...].astype(BF)
    rest = (weight[...] - top.astype(F32)).astype(BF)
    for side, out in ((top, high), (rest, low)):
        spread = jnp.dot(side, expand, preferred_element_type=F32)
        out[...] = jnp.where(hit, spread, 0.0).astype(BF)


def slot_weights(rank, weight, slots):
    rows = rank.shape[0]
    vmem = pl.BlockSpec(memory_space=pltpu.VMEM)
    shape = jax.ShapeDtypeStruct((rows, slots), BF)
    return pl.pallas_call(
        slot_weight_kernel,
        out_shape=(shape, shape),
        in_specs=[vmem, vmem],
        out_specs=(vmem, vmem),
        compiler_params=pltpu.CompilerParams(vmem_limit_bytes=16 << 20),
        cost_estimate=pl.CostEstimate(
            flops=6 * rows * slots * 32, bytes_accessed=2 << 20, transcendentals=0
        ),
        name="slot_weights",
    )(rank, weight)


def expert_kernel(
    x_hbm, both_own, both_peer, down_own, down_peer, out_hbm, x, gate, up, down, act, out, sems, out_sems
):
    hidden = both_own.shape[1]
    rows = x.shape[0]
    groups, _, width = out.shape
    block = rows // 2
    first = pl.ds(0, hidden)
    second = pl.ds(hidden, hidden)
    top_rows, low_rows = pl.ds(0, block), pl.ds(block, block)
    copies = [
        pltpu.make_async_copy(x_hbm.at[top_rows], x.at[top_rows], sems.at[0]),
        pltpu.make_async_copy(both_own.at[0], gate.at[first], sems.at[1]),
        pltpu.make_async_copy(both_peer.at[0], gate.at[second], sems.at[2]),
        pltpu.make_async_copy(both_own.at[1], up.at[first], sems.at[3]),
        pltpu.make_async_copy(both_peer.at[1], up.at[second], sems.at[4]),
        pltpu.make_async_copy(x_hbm.at[low_rows], x.at[low_rows], sems.at[5]),
        pltpu.make_async_copy(down_own, down.at[first], sems.at[6]),
        pltpu.make_async_copy(down_peer, down.at[second], sems.at[7]),
    ]
    for copy in copies:
        copy.start()
    contract = (((1,), (1,)), ((), ()))
    for copy in copies[:3]:
        copy.wait()
    for m in range(2):
        here = pl.ds(m * block, block)
        if m == 1:
            copies[5].wait()
        left = x[here, :]
        g = lax.dot_general(left, gate[...], contract, preferred_element_type=F32)
        if m == 0:
            copies[3].wait()
            copies[4].wait()
        u = lax.dot_general(left, up[...], contract, preferred_element_type=F32)
        act[here, :] = (g / (1.0 + jnp.exp(-g)) * u).astype(BF)

    for copy in copies[6:]:
        copy.wait()

    @pl.loop(0, 2)
    def _(m):
        here = pl.ds(pl.multiple_of(m * block, block), block)
        left = act[here, :]
        for i in range(groups):
            result = jnp.dot(
                left, down[:, i * width : (i + 1) * width], preferred_element_type=F32
            )
            out[i, here, :] = result.astype(BF)
            pltpu.make_async_copy(
                out.at[i, here], out_hbm.at[i, here], out_sems.at[m, i]
            ).start()

    for m in range(2):
        here = pl.ds(m * block, block)
        for i in range(groups):
            pltpu.make_async_copy(
                out.at[i, here], out_hbm.at[i, here], out_sems.at[m, i]
            ).wait()


def experts(x, both_own, both_peer, down_own, down_peer, groups):
    rows, depth = x.shape
    hidden, width = down_own.shape
    column_width = width // groups
    anywhere = pl.BlockSpec(memory_space=pltpu.HBM)
    return pl.pallas_call(
        expert_kernel,
        out_shape=jax.ShapeDtypeStruct((groups, rows, column_width), BF),
        in_specs=[anywhere] * 5,
        out_specs=anywhere,
        scratch_shapes=[
            pltpu.VMEM((rows, depth), BF),
            pltpu.VMEM((2 * hidden, depth), BF),
            pltpu.VMEM((2 * hidden, depth), BF),
            pltpu.VMEM((2 * hidden, width), BF),
            pltpu.VMEM((rows, 2 * hidden), BF),
            pltpu.VMEM((groups, rows, column_width), BF),
            pltpu.SemaphoreType.DMA((8,)),
            pltpu.SemaphoreType.DMA((2, groups)),
        ],
        compiler_params=pltpu.CompilerParams(vmem_limit_bytes=60 << 20),
        cost_estimate=pl.CostEstimate(
            flops=12 * rows * depth * hidden,
            bytes_accessed=15 << 20,
            transcendentals=2 * rows * hidden,
        ),
        name="experts",
    )(x, both_own, both_peer, down_own, down_peer)


def combine_kernel(
    core, high_hbm, low_hbm, back_hbm, mine_hbm, peers_hbm, shared_hbm, out,
    high, low, back, mine, peers, shared, sems,
):
    rows = mine.shape[0]
    pairs = (
        (high_hbm, high),
        (back_hbm.at[0], back.at[0]),
        (low_hbm, low),
        (back_hbm.at[1], back.at[1]),
        (shared_hbm, shared),
        (mine_hbm, mine),
        (peers_hbm, peers),
    )
    copies = [
        pltpu.make_async_copy(source, target, sems.at[i])
        for i, (source, target) in enumerate(pairs)
    ]
    for copy in copies:
        copy.start()
    copies[0].wait()
    copies[1].wait()
    total = jnp.dot(high[...], back[0], preferred_element_type=F32)
    copies[2].wait()
    total += jnp.dot(low[...], back[0], preferred_element_type=F32)
    copies[3].wait()
    total += jnp.dot(high[...], back[1], preferred_element_type=F32)
    total += jnp.dot(low[...], back[1], preferred_element_type=F32)
    for copy in copies[4:]:
        copy.wait()
    total += shared[...]
    first = core[0] == 0
    low_half = jnp.where(first, mine[...], peers[...])
    high_half = jnp.where(first, peers[...], mine[...])
    out[0:rows, :] = (total[0:rows] + low_half).astype(BF)
    out[rows : 2 * rows, :] = (total[rows:] + high_half).astype(BF)


def combine(core, high, low, returned, mine, peers, shared):
    hbm = pl.BlockSpec(memory_space=pltpu.HBM)
    rows, width = shared.shape
    operands = (high, low, returned, mine, peers, shared)
    return pl.pallas_call(
        combine_kernel,
        out_shape=jax.ShapeDtypeStruct((rows, width), BF),
        in_specs=[pl.BlockSpec(memory_space=pltpu.SMEM)] + [hbm] * 6,
        out_specs=pl.BlockSpec(memory_space=pltpu.VMEM),
        scratch_shapes=[pltpu.VMEM(o.shape, o.dtype) for o in operands]
        + [pltpu.SemaphoreType.DMA((7,))],
        compiler_params=pltpu.CompilerParams(vmem_limit_bytes=60 << 20),
        cost_estimate=pl.CostEstimate(
            flops=8 * rows * width * high.shape[1], bytes_accessed=7 << 20, transcendentals=0
        ),
        name="combine",
    )(core, *operands)


def page_pieces(keys, values, owner_all, tok_count, head_count, tok_index):
    pages_here = owner_all.shape[1]
    tok_rows = keys.shape[0]
    quarter_page = PAGE // head_count
    mine = lax.dynamic_index_in_dim(owner_all, tok_index, 0, keepdims=False)
    row = jnp.arange(tok_rows, dtype=jnp.int32)
    quarter = row // (tok_count * quarter_page)
    owner = row // quarter_page % tok_count
    line = quarter * quarter_page + row % quarter_page
    token_owner = jnp.repeat(mine, PAGE)
    token_line = jnp.arange(tok_rows, dtype=jnp.int32) % PAGE
    pick = (
        (owner[:, None] == token_owner[None, :]) & (line[:, None] == token_line[None, :])
    ).astype(BF)
    parts = [
        jnp.dot(pick, part, preferred_element_type=F32).astype(BF) for part in (keys, values)
    ]
    return jnp.concatenate(parts, 1).reshape(head_count * tok_count, quarter_page, -1)


def place_pages(landed, slots_all, owner_all, tok_count, head_count, tok_index):
    pages_here = owner_all.shape[1]
    quarter_page = PAGE // head_count
    rows = pages_here * quarter_page
    arrival = jnp.sum(jnp.where(owner_all == tok_index, slots_all % pages_here, 0), 1)
    row = jnp.arange(rows, dtype=jnp.int32)
    target = jnp.repeat(arrival, quarter_page) * quarter_page + row % quarter_page
    place = (row[:, None] == target[None, :]).astype(BF)
    landed = landed.reshape(head_count, rows, -1)
    width = landed.shape[2] // 2
    placed = [
        jnp.dot(place, landed[h], preferred_element_type=F32).astype(BF)
        for h in range(head_count)
    ]
    cache = jnp.concatenate(
        [p[:, :width] for p in placed] + [p[:, width:] for p in placed], 1
    )
    return cache.reshape(pages_here, quarter_page, 2 * head_count * width)


def per_device(
    hidden_in,
    queries,
    keys,
    values,
    request_ids,
    out_proj,
    norm_gain,
    expert_gate_up,
    expert_down,
    shared_gate_up,
    shared_down,
    shared_gate,
    routes,
    route_weights,
    page_slots,
):
    tok_rows, model_width = hidden_in.shape
    head_width = queries.shape[1]
    heads_here = head_width // HD
    tok_count = lax.axis_size("tok")
    head_count = lax.axis_size("head")
    tok_index = lax.axis_index("tok")
    head_index = lax.axis_index("head")
    core = head_index % CORES
    column_width = model_width // head_count
    rows_of_blocks = tok_count // ROW
    half = tok_rows // 2
    slots_core = CAP // CORES

    gate_up_own = jnp.transpose(expert_gate_up[0], (1, 2, 0))
    down_own = expert_down[0]
    out_peer = lax.ppermute(out_proj, "head", INTRA)
    gate_up_peer = lax.ppermute(gate_up_own, "head", INTRA)
    down_peer = lax.ppermute(down_own, "head", INTRA)

    packed = jnp.stack(
        [
            jnp.concatenate([part[:, i * HD : (i + 1) * HD] for part in (keys, values)], 1)
            for i in range(heads_here)
        ],
        0,
    )
    row_groups = [[r * ROW + y for y in range(ROW)] for r in range(rows_of_blocks)]
    own = lax.all_to_all(
        packed, "tok", split_axis=0, concat_axis=0, tiled=True, axis_index_groups=row_groups
    )
    queries, own = lax.optimization_barrier((queries, own))
    place_in_row = tok_index % ROW
    query_parts = []
    for step in range(ROW):
        target = (place_in_row + step) % ROW
        part = lax.dynamic_slice_in_dim(queries, target * HD, HD, 1)
        if step:
            part = lax.ppermute(
                part,
                "tok",
                [
                    (r * ROW + y, r * ROW + (y + step) % ROW)
                    for r in range(rows_of_blocks)
                    for y in range(ROW)
                ],
            )
        query_parts.append(part)
    slots_all = page_slots.reshape(tok_count, tok_rows // PAGE)
    owner_all = slots_all // (tok_rows // PAGE)
    pieces = page_pieces(keys, values, owner_all, tok_count, head_count, tok_index)
    pieces, own = lax.optimization_barrier((pieces, own))
    landed = lax.all_to_all(pieces, BOTH, split_axis=0, concat_axis=0, tiled=True)
    past = lax.ppermute(
        own, "tok", [(s, s + ROW) for s in range(tok_count - ROW)]
    )
    span = ROW * tok_rows
    base = (tok_index // ROW) * span
    padded_ids = jnp.concatenate([jnp.full((span,), -1, jnp.int32), request_ids], 0)
    window_ids = lax.dynamic_slice_in_dim(padded_ids, base, 2 * span, 0)
    ids_row = window_ids[None, :]
    ids_col = jnp.broadcast_to(window_ids[span:, None], (span, HD))
    past, landed = lax.optimization_barrier((past, landed))
    attended = attention(
        place_in_row.reshape(1), ids_col, ids_row, jnp.stack(query_parts, 0), own, past
    )

    core_groups = [
        [
            (chip * CORES + c) * tok_count + r * ROW + y
            for c in range(CORES)
            for y in range(ROW)
        ]
        for chip in range(CHIPS)
        for r in range(rows_of_blocks)
    ]
    gathered = lax.all_to_all(
        attended.reshape(CORES * ROW, half, HD),
        BOTH,
        split_axis=0,
        concat_axis=0,
        tiled=True,
        axis_index_groups=core_groups,
    ).reshape(CORES, ROW, half, HD)
    core_ref = core.reshape(1)
    projected, projected_low = project(core_ref, gathered, out_proj, out_peer)
    projected_far = lax.ppermute(projected_low, "head", CROSS)
    resid, normed_own = add_and_norm(
        core_ref, hidden_in, projected, projected_far, norm_gain[None, :]
    )
    normed_peer = lax.ppermute(normed_own, "head", INTRA)

    expert_ids = jnp.arange(EXPERTS, dtype=jnp.int32)
    named = routes[:, :, None] == expert_ids[None, None, :]
    onehot = jnp.sum(named.astype(F32), 1)
    weight_of = jnp.sum(jnp.where(named, route_weights[:, :, None], 0.0), 1)
    earlier = (
        jnp.arange(tok_rows, dtype=jnp.int32)[None, :] < jnp.arange(tok_rows, dtype=jnp.int32)[:, None]
    ).astype(BF)
    rank = jnp.dot(earlier, onehot.astype(BF), preferred_element_type=F32).astype(jnp.int32)
    rank = jnp.where(onehot > 0, rank, -1)
    rank_t = rank.T
    rank_rel = jnp.where(core == 0, rank_t, jnp.roll(rank_t, half, 1))
    place = jnp.arange(slots_core, dtype=jnp.int32) * CORES
    select = (rank_rel[:, None, :] == (place + core)[None, :, None]).astype(BF)
    select = select.reshape(EXPERTS * slots_core, tok_rows)
    outgoing = gather_rows(select, normed_own, normed_peer)
    rank, weight_of, outgoing = lax.optimization_barrier((rank, weight_of, outgoing))
    high, low = slot_weights(rank, weight_of, CORES * EXPERTS * slots_core)
    normed_abs = jnp.where(
        core == 0,
        jnp.concatenate([normed_own, normed_peer], 0),
        jnp.concatenate([normed_peer, normed_own], 0),
    )
    normed_abs, outgoing = lax.optimization_barrier((normed_abs, outgoing))
    arrived = lax.all_to_all(
        outgoing.reshape(tok_count, slots_core, model_width),
        "tok",
        split_axis=0,
        concat_axis=0,
        tiled=True,
    ).reshape(tok_count * slots_core, model_width)
    shared_both = jnp.einsum("td,dgf->tgf", normed_abs, shared_gate_up, preferred_element_type=F32)
    shared_act = (jax.nn.silu(shared_both[:, 0, :]) * shared_both[:, 1, :]).astype(BF)
    shared_scale = jax.nn.sigmoid(jnp.dot(normed_abs, shared_gate, preferred_element_type=F32))
    shared_term = shared_scale[:, None] * jnp.dot(
        shared_act, shared_down, preferred_element_type=F32
    )
    chip = head_index // CORES
    chip_width = CORES * column_width
    shared_near = lax.dynamic_slice_in_dim(shared_term, chip * chip_width, chip_width, 1)
    shared_send = lax.dynamic_slice_in_dim(
        shared_term, (1 - chip) * chip_width, chip_width, 1
    ).astype(BF)
    shared_near, shared_send, arrived = lax.optimization_barrier(
        (shared_near, shared_send, arrived)
    )
    shared_far = lax.ppermute(shared_send, "head", CROSS)

    partial = experts(arrived, gate_up_own, gate_up_peer, down_own, down_peer, head_count)
    partial = partial.reshape(head_count * tok_count, slots_core, column_width)
    partial, shared_far = lax.optimization_barrier((partial, shared_far))
    returned = lax.all_to_all(partial, BOTH, split_axis=0, concat_axis=0, tiled=True)
    returned = returned.reshape(CHIPS, CORES * EXPERTS * slots_core, column_width)

    shared_chip = shared_near + shared_far.astype(F32)
    shared_own = lax.dynamic_slice_in_dim(shared_chip, core * column_width, column_width, 1)
    shared_peer = lax.dynamic_slice_in_dim(
        shared_chip, (1 - core) * column_width, column_width, 1
    ).astype(BF)
    shared_cols = shared_own + lax.ppermute(shared_peer, "head", INTRA).astype(F32)
    own_cols = lax.dynamic_slice_in_dim(resid, head_index * column_width, column_width, 1)
    peer_cols = lax.dynamic_slice_in_dim(
        resid, (head_index + 1 - 2 * core) * column_width, column_width, 1
    )
    from_peer = lax.ppermute(peer_cols, "head", INTRA)
    layer_out = combine(core_ref, high, low, returned, own_cols, from_peer, shared_cols)
    decode_cache = place_pages(landed, slots_all, owner_all, tok_count, head_count, tok_index)
    return (layer_out, decode_cache)


def solution(mesh):
    in_specs = (
        P("tok", None),
        P("tok", "head"),
        P("tok", "head"),
        P("tok", "head"),
        P(),
        P("head", None),
        P(),
        P("tok", None, None, "head"),
        P("tok", "head", None),
        P(None, None, "head"),
        P("head", None),
        P(),
        P("tok", None),
        P("tok", None),
        P(),
    )
    out_specs = (P("tok", "head"), P("tok", "head", None))
    return jax.shard_map(
        per_device, mesh=mesh, in_specs=in_specs, out_specs=out_specs, check_vma=False
    )
```

```python
import math

import jax
import jax.numpy as jnp
from jax import lax
from jax.experimental import pallas as pl
from jax.experimental.pallas import tpu as pltpu
from jax.sharding import PartitionSpec as P

HD = 128
TOP = 4
EXPERTS = 32
PAGE = 8
CAP = 48
ROW = 4
CORES = 2
CHIPS = 2
BF = jnp.bfloat16
F32 = jnp.float32
BOTH = ("head", "tok")
INTRA = [(0, 1), (1, 0), (2, 3), (3, 2)]
CROSS = [(0, 2), (2, 0), (1, 3), (3, 1)]


def attention_kernel(
    place, ids_col_hbm, ids_row_hbm, query_hbm, own_hbm, past_hbm, out_hbm,
    ids_col, ids_row, query_parts, own, past, out, sems, out_sems,
):
    block = out.shape[2] * 2
    pairs = (
        (query_hbm, query_parts),
        (own_hbm, own),
        (past_hbm, past),
        (ids_col_hbm, ids_col),
        (ids_row_hbm, ids_row),
    )
    copies = [
        pltpu.make_async_copy(source, target, sems.at[i])
        for i, (source, target) in enumerate(pairs)
    ]
    for copy in copies:
        copy.start()
    for copy in copies:
        copy.wait()
    stores = []
    scale = 1.0 / math.sqrt(HD)
    span = ROW * block
    row_pos = lax.broadcasted_iota(jnp.int32, (block, block), 0)
    col_pos = lax.broadcasted_iota(jnp.int32, (block, block), 1)
    causal = col_pos <= row_pos
    for y in range(ROW):
        query = query_parts[lax.rem(place[0] + (ROW - y), ROW)]
        query_ids = ids_col[pl.ds(y * block, block), 0:1]
        pieces = []
        for b in range(y, ROW):
            key = past[b, :, 0:HD]
            key_ids = ids_row[0:1, pl.ds(b * block, block)]
            score = lax.dot_general(
                query, key, (((1,), (1,)), ((), ())), preferred_element_type=F32
            )
            pieces.append(jnp.where(query_ids == key_ids, score * scale, -1e30))
        for b in range(y + 1):
            key = own[b, :, 0:HD]
            key_ids = ids_row[0:1, pl.ds(span + b * block, block)]
            score = lax.dot_general(
                query, key, (((1,), (1,)), ((), ())), preferred_element_type=F32
            )
            allowed = query_ids == key_ids
            if b == y:
                allowed = allowed & causal
            pieces.append(jnp.where(allowed, score * scale, -1e30))
        top = pieces[0].max(-1, keepdims=True)
        for piece in pieces[1:]:
            top = jnp.maximum(top, piece.max(-1, keepdims=True))
        weights = [jnp.exp(piece - top) for piece in pieces]
        total = weights[0].sum(-1, keepdims=True)
        for weight in weights[1:]:
            total = total + weight.sum(-1, keepdims=True)
        inverse = 1.0 / total
        mixed = jnp.zeros((block, HD), F32)
        index = 0
        for b in range(y, ROW):
            prob = (weights[index] * inverse).astype(BF)
            mixed += jnp.dot(prob, past[b, :, HD : 2 * HD], preferred_element_type=F32)
            index += 1
        for b in range(y + 1):
            prob = (weights[index] * inverse).astype(BF)
            mixed += jnp.dot(prob, own[b, :, HD : 2 * HD], preferred_element_type=F32)
            index += 1
        half = block // 2
        out[0, y] = mixed[:half].astype(BF)
        out[1, y] = mixed[half:].astype(BF)
        for c in range(2):
            store = pltpu.make_async_copy(out.at[c, y], out_hbm.at[c, y], out_sems.at[c, y])
            store.start()
            stores.append(store)
    for store in stores:
        store.wait()


def attention(place, ids_col, ids_row, query_parts, own, past):
    block = own.shape[1]
    hbm = pl.BlockSpec(memory_space=pltpu.HBM)
    operands = (ids_col, ids_row, query_parts, own, past)
    result = jax.ShapeDtypeStruct((2, ROW, block // 2, HD), BF)
    return pl.pallas_call(
        attention_kernel,
        out_shape=result,
        in_specs=[pl.BlockSpec(memory_space=pltpu.SMEM)] + [hbm] * 5,
        out_specs=hbm,
        scratch_shapes=[pltpu.VMEM(o.shape, o.dtype) for o in operands]
        + [
            pltpu.VMEM(result.shape, BF),
            pltpu.SemaphoreType.DMA((5,)),
            pltpu.SemaphoreType.DMA((2, ROW)),
        ],
        compiler_params=pltpu.CompilerParams(vmem_limit_bytes=58 << 20),
        cost_estimate=pl.CostEstimate(
            flops=4 * 5 * ROW * block * block * HD,
            bytes_accessed=3 << 20,
            transcendentals=5 * ROW * block * block,
        ),
        name="row_attention",
    )(place, *operands)


def project_kernel(
    core, att_hbm, own_hbm, peer_hbm, total_hbm, low_hbm,
    att, own, peer, total, total_low, att_sem, sems, out_sems,
):
    width = total.shape[1]
    step = width // 4
    att_copy = pltpu.make_async_copy(att_hbm, att, att_sem)
    att_copy.start()
    copies = []
    for i in range(4):
        cols = pl.ds(i * step, step)
        copies.append(
            (
                pltpu.make_async_copy(own_hbm.at[:, cols], own.at[:, cols], sems.at[0, i]),
                pltpu.make_async_copy(peer_hbm.at[:, cols], peer.at[:, cols], sems.at[1, i]),
            )
        )
    for pair in copies:
        for copy in pair:
            copy.start()
    att_copy.wait()
    c = core[0]
    stores = []
    left = jnp.concatenate([att[c, y] for y in range(ROW)], 1)
    right = jnp.concatenate([att[1 - c, y] for y in range(ROW)], 1)
    for i in range(4):
        cols = pl.ds(i * step, step)
        for copy in copies[i]:
            copy.wait()
        part = jnp.dot(left, own[:, cols], preferred_element_type=F32) + jnp.dot(
            right, peer[:, cols], preferred_element_type=F32
        )
        total_low[:, cols] = part.astype(BF)
        total[:, cols] = part
        for j, (source, target) in enumerate(((total_low, low_hbm), (total, total_hbm))):
            store = pltpu.make_async_copy(
                source.at[:, cols], target.at[:, cols], out_sems.at[j, i]
            )
            store.start()
            stores.append(store)
    for store in stores:
        store.wait()


def project(core, att, out_own, out_peer):
    rows = att.shape[2]
    depth, width = out_own.shape
    hbm = pl.BlockSpec(memory_space=pltpu.HBM)
    return pl.pallas_call(
        project_kernel,
        out_shape=(
            jax.ShapeDtypeStruct((rows, width), F32),
            jax.ShapeDtypeStruct((rows, width), BF),
        ),
        in_specs=[pl.BlockSpec(memory_space=pltpu.SMEM), hbm, hbm, hbm],
        out_specs=(hbm, hbm),
        scratch_shapes=[
            pltpu.VMEM(att.shape, BF),
            pltpu.VMEM((depth, width), BF),
            pltpu.VMEM((depth, width), BF),
            pltpu.VMEM((rows, width), F32),
            pltpu.VMEM((rows, width), BF),
            pltpu.SemaphoreType.DMA,
            pltpu.SemaphoreType.DMA((2, 4)),
            pltpu.SemaphoreType.DMA((2, 4)),
        ],
        compiler_params=pltpu.CompilerParams(vmem_limit_bytes=58 << 20),
        cost_estimate=pl.CostEstimate(
            flops=4 * rows * depth * width, bytes_accessed=6 << 20, transcendentals=0
        ),
        name="project",
    )(core, att, out_own, out_peer)


def norm_kernel(
    core, hidden_hbm, near_hbm, far_hbm, gain_hbm, resid_hbm, normed_hbm,
    hidden, near, far, gain, normed, sems, out_sems,
):
    rows = near.shape[0]
    parts = 2
    block = rows // parts
    start = pl.multiple_of(core[0] * rows, rows)
    gain_copy = pltpu.make_async_copy(gain_hbm, gain, sems.at[3, 0])
    gain_copy.start()
    copies = []
    for i in range(parts):
        here = pl.ds(i * block, block)
        copies.append(
            [
                pltpu.make_async_copy(near_hbm.at[here], near.at[here], sems.at[0, i]),
                pltpu.make_async_copy(far_hbm.at[here], far.at[here], sems.at[1, i]),
                pltpu.make_async_copy(
                    hidden_hbm.at[pl.ds(start + i * block, block)], hidden.at[here], sems.at[2, i]
                ),
            ]
        )
        for copy in copies[i]:
            copy.start()
    gain_copy.wait()
    stores = []
    for i in range(parts):
        here = pl.ds(i * block, block)
        for copy in copies[i]:
            copy.wait()
        value = hidden[here, :].astype(F32) + (near[here, :] + far[here, :].astype(F32))
        mean_square = jnp.mean(value * value, axis=-1, keepdims=True)
        normed[here, :] = (value * lax.rsqrt(mean_square + 1e-06) * gain[...]).astype(BF)
        near[here, :] = value
        for j, (source, target) in enumerate(((normed, normed_hbm), (near, resid_hbm))):
            store = pltpu.make_async_copy(source.at[here], target.at[here], out_sems.at[j, i])
            store.start()
            stores.append(store)
    for store in stores:
        store.wait()


def add_and_norm(core, hidden, near, far, gain):
    rows, width = near.shape
    hbm = pl.BlockSpec(memory_space=pltpu.HBM)
    return pl.pallas_call(
        norm_kernel,
        out_shape=(
            jax.ShapeDtypeStruct((rows, width), F32),
            jax.ShapeDtypeStruct((rows, width), BF),
        ),
        in_specs=[pl.BlockSpec(memory_space=pltpu.SMEM), hbm, hbm, hbm, hbm],
        out_specs=(hbm, hbm),
        scratch_shapes=[
            pltpu.VMEM((rows, width), BF),
            pltpu.VMEM((rows, width), F32),
            pltpu.VMEM((rows, width), BF),
            pltpu.VMEM((1, width), F32),
            pltpu.VMEM((rows, width), BF),
            pltpu.SemaphoreType.DMA((4, 2)),
            pltpu.SemaphoreType.DMA((2, 2)),
        ],
        compiler_params=pltpu.CompilerParams(vmem_limit_bytes=58 << 20),
        cost_estimate=pl.CostEstimate(
            flops=8 * rows * width, bytes_accessed=4 << 20, transcendentals=rows
        ),
        name="add_and_norm",
    )(core, hidden, near, far, gain)


def gather_kernel(
    select_hbm, own_hbm, peer_hbm, out_hbm, select, rows, out, sems, out_sems
):
    half = rows.shape[0] // 2
    total, block = out.shape[0], out.shape[0] // 3
    copies = [
        pltpu.make_async_copy(own_hbm, rows.at[pl.ds(0, half)], sems.at[0]),
        pltpu.make_async_copy(peer_hbm, rows.at[pl.ds(half, half)], sems.at[1]),
        pltpu.make_async_copy(select_hbm, select, sems.at[2]),
    ]
    for copy in copies:
        copy.start()
    for copy in copies:
        copy.wait()
    stores = []
    for i in range(total // block):
        here = pl.ds(i * block, block)
        out[here, :] = jnp.dot(
            select[here, :], rows[...], preferred_element_type=F32
        ).astype(BF)
        store = pltpu.make_async_copy(out.at[here], out_hbm.at[here], out_sems.at[i])
        store.start()
        stores.append(store)
    for store in stores:
        store.wait()


def gather_rows(select, own, peer):
    slots, rows = select.shape
    width = own.shape[1]
    hbm = pl.BlockSpec(memory_space=pltpu.HBM)
    return pl.pallas_call(
        gather_kernel,
        out_shape=jax.ShapeDtypeStruct((slots, width), BF),
        in_specs=[hbm, hbm, hbm],
        out_specs=hbm,
        scratch_shapes=[
            pltpu.VMEM((slots, rows), BF),
            pltpu.VMEM((rows, width), BF),
            pltpu.VMEM((slots, width), BF),
            pltpu.SemaphoreType.DMA((3,)),
            pltpu.SemaphoreType.DMA((3,)),
        ],
        compiler_params=pltpu.CompilerParams(vmem_limit_bytes=58 << 20),
        cost_estimate=pl.CostEstimate(
            flops=2 * slots * rows * width, bytes_accessed=5 << 20, transcendentals=0
        ),
        name="gather_rows",
    )(select, own, peer)


def slot_weight_kernel(rank, weight, high, low):
    slots = high.shape[1]
    per_core = CAP // CORES
    experts_here = rank.shape[1]
    lane = lax.broadcasted_iota(jnp.int32, (1, slots), 1)
    expert_of = lax.rem(lax.div(lane, per_core), experts_here)
    wanted = lax.rem(lane, per_core) * CORES + lax.div(lane, per_core * experts_here)
    expand = (
        lax.broadcasted_iota(jnp.int32, (experts_here, slots), 0) == expert_of
    ).astype(BF)
    ranks = jnp.dot(rank[...].astype(BF), expand, preferred_element_type=F32)
    hit = ranks.astype(jnp.int32) == wanted
    top = weight[...].astype(BF)
    rest = (weight[...] - top.astype(F32)).astype(BF)
    for side, out in ((top, high), (rest, low)):
        spread = jnp.dot(side, expand, preferred_element_type=F32)
        out[...] = jnp.where(hit, spread, 0.0).astype(BF)


def slot_weights(rank, weight, slots):
    rows = rank.shape[0]
    vmem = pl.BlockSpec(memory_space=pltpu.VMEM)
    shape = jax.ShapeDtypeStruct((rows, slots), BF)
    return pl.pallas_call(
        slot_weight_kernel,
        out_shape=(shape, shape),
        in_specs=[vmem, vmem],
        out_specs=(vmem, vmem),
        compiler_params=pltpu.CompilerParams(vmem_limit_bytes=16 << 20),
        cost_estimate=pl.CostEstimate(
            flops=6 * rows * slots * 32, bytes_accessed=2 << 20, transcendentals=0
        ),
        name="slot_weights",
    )(rank, weight)


def expert_kernel(
    x_hbm, both_own, both_peer, down_own, down_peer, out_hbm,
    x, gate, up, down, act, out, x_sems, sems, down_sems, out_sems,
):
    hidden = both_own.shape[1]
    rows = x.shape[0]
    groups, _, width = out.shape
    parts = 3
    block = rows // parts
    step = 256
    bounds = [(lo, min(lo + step, 2 * hidden)) for lo in range(0, 2 * hidden, step)]
    x_copies = [
        pltpu.make_async_copy(
            x_hbm.at[pl.ds(m * block, block)], x.at[pl.ds(m * block, block)], x_sems.at[m]
        )
        for m in range(parts)
    ]
    chunks = []
    for n, (lo, hi) in enumerate(bounds):
        copies = []
        for j, (source, start, stop) in enumerate(
            (
                (both_own, lo, min(hi, hidden)),
                (both_peer, max(lo, hidden) - hidden, hi - hidden),
            )
        ):
            if stop <= start:
                continue
            shift = hidden * j
            for k, target in enumerate((gate, up)):
                copies.append(
                    pltpu.make_async_copy(
                        source.at[k, pl.ds(start, stop - start)],
                        target.at[pl.ds(start + shift, stop - start)],
                        sems.at[n, j, k],
                    )
                )
        chunks.append(copies)
    down_copies = [
        pltpu.make_async_copy(source, down.at[pl.ds(j * hidden, hidden)], down_sems.at[j])
        for j, source in enumerate((down_own, down_peer))
    ]
    for copy in [x_copies[0]] + chunks[0] + x_copies[1:]:
        copy.start()
    for copies in chunks[1:]:
        for copy in copies:
            copy.start()
    for copy in down_copies:
        copy.start()
    contract = (((1,), (1,)), ((), ()))
    for n, (lo, hi) in enumerate(bounds):
        for copy in chunks[n]:
            copy.wait()
        for m in range(parts):
            here = pl.ds(m * block, block)
            if n == 0:
                x_copies[m].wait()
            left = x[here, :]
            g = lax.dot_general(left, gate[lo:hi, :], contract, preferred_element_type=F32)
            u = lax.dot_general(left, up[lo:hi, :], contract, preferred_element_type=F32)
            act[here, lo:hi] = (g / (1.0 + jnp.exp(-g)) * u).astype(BF)
    for copy in down_copies:
        copy.wait()
    stores = []
    for i in range(groups):
        for m in range(parts):
            here = pl.ds(m * block, block)
            result = jnp.dot(
                act[here, :], down[:, i * width : (i + 1) * width], preferred_element_type=F32
            )
            out[i, here, :] = result.astype(BF)
            store = pltpu.make_async_copy(
                out.at[i, here], out_hbm.at[i, here], out_sems.at[m, i]
            )
            store.start()
            stores.append(store)
    for store in stores:
        store.wait()


def experts(x, both_own, both_peer, down_own, down_peer, groups):
    rows, depth = x.shape
    hidden, width = down_own.shape
    column_width = width // groups
    hbm = pl.BlockSpec(memory_space=pltpu.HBM)
    return pl.pallas_call(
        expert_kernel,
        out_shape=jax.ShapeDtypeStruct((groups, rows, column_width), BF),
        in_specs=[hbm] * 5,
        out_specs=hbm,
        scratch_shapes=[
            pltpu.VMEM((rows, depth), BF),
            pltpu.VMEM((2 * hidden, depth), BF),
            pltpu.VMEM((2 * hidden, depth), BF),
            pltpu.VMEM((2 * hidden, width), BF),
            pltpu.VMEM((rows, 2 * hidden), BF),
            pltpu.VMEM((groups, rows, column_width), BF),
            pltpu.SemaphoreType.DMA((3,)),
            pltpu.SemaphoreType.DMA((pl.cdiv(2 * hidden, 256), 2, 2)),
            pltpu.SemaphoreType.DMA((2,)),
            pltpu.SemaphoreType.DMA((3, groups)),
        ],
        compiler_params=pltpu.CompilerParams(vmem_limit_bytes=60 << 20),
        cost_estimate=pl.CostEstimate(
            flops=12 * rows * depth * hidden,
            bytes_accessed=15 << 20,
            transcendentals=2 * rows * hidden,
        ),
        name="experts",
    )(x, both_own, both_peer, down_own, down_peer)


def combine_kernel(
    core, high_hbm, low_hbm, back_hbm, mine_hbm, peers_hbm, shared_hbm, out,
    high, low, back, mine, peers, shared, sems,
):
    rows = mine.shape[0]
    chips, depth = back.shape[0], back.shape[1]
    block = depth // CORES
    pieces = [(chip, pl.ds(c * block, block)) for chip in range(chips) for c in range(CORES)]
    copies = [
        pltpu.make_async_copy(back_hbm.at[chip, here], back.at[chip, here], sems.at[i])
        for i, (chip, here) in enumerate(pieces)
    ]
    rest = [
        pltpu.make_async_copy(source, target, sems.at[len(pieces) + i])
        for i, (source, target) in enumerate(
            (
                (high_hbm, high),
                (low_hbm, low),
                (shared_hbm, shared),
                (mine_hbm, mine),
                (peers_hbm, peers),
            )
        )
    ]
    for copy in [rest[0], copies[0], rest[1]] + copies[1:] + rest[2:]:
        copy.start()
    total = None
    for i, (copy, (chip, here)) in enumerate(zip(copies, pieces)):
        if i == 0:
            rest[0].wait()
        copy.wait()
        for side in (high, low):
            if i == 0 and side is low:
                rest[1].wait()
            part = jnp.dot(side[:, here], back[chip, here], preferred_element_type=F32)
            total = part if total is None else total + part
    for copy in rest[2:]:
        copy.wait()
    total += shared[...]
    first = core[0] == 0
    low_half = jnp.where(first, mine[...], peers[...])
    high_half = jnp.where(first, peers[...], mine[...])
    out[0:rows, :] = (total[0:rows] + low_half).astype(BF)
    out[rows : 2 * rows, :] = (total[rows:] + high_half).astype(BF)


def combine(core, high, low, returned, mine, peers, shared):
    hbm = pl.BlockSpec(memory_space=pltpu.HBM)
    vmem = pl.BlockSpec(memory_space=pltpu.VMEM)
    rows, width = shared.shape
    operands = (high, low, returned, mine, peers, shared)
    return pl.pallas_call(
        combine_kernel,
        out_shape=jax.ShapeDtypeStruct((rows, width), BF),
        in_specs=[pl.BlockSpec(memory_space=pltpu.SMEM)] + [hbm] * 6,
        out_specs=vmem,
        scratch_shapes=[pltpu.VMEM(o.shape, o.dtype) for o in operands]
        + [pltpu.SemaphoreType.DMA((9,))],
        compiler_params=pltpu.CompilerParams(vmem_limit_bytes=60 << 20),
        cost_estimate=pl.CostEstimate(
            flops=8 * rows * width * high.shape[1], bytes_accessed=7 << 20, transcendentals=0
        ),
        name="combine",
    )(core, *operands)


def page_pieces(keys, values, owner_all, tok_count, head_count, tok_index):
    pages_here = owner_all.shape[1]
    tok_rows = keys.shape[0]
    quarter_page = PAGE // head_count
    mine = lax.dynamic_index_in_dim(owner_all, tok_index, 0, keepdims=False)
    row = jnp.arange(tok_rows, dtype=jnp.int32)
    quarter = row // (tok_count * quarter_page)
    owner = row // quarter_page % tok_count
    line = quarter * quarter_page + row % quarter_page
    token_owner = jnp.repeat(mine, PAGE)
    token_line = jnp.arange(tok_rows, dtype=jnp.int32) % PAGE
    pick = (
        (owner[:, None] == token_owner[None, :]) & (line[:, None] == token_line[None, :])
    ).astype(BF)
    parts = [
        jnp.dot(pick, part, preferred_element_type=F32).astype(BF) for part in (keys, values)
    ]
    return jnp.concatenate(parts, 1).reshape(head_count * tok_count, quarter_page, -1)


def place_pages(landed, slots_all, owner_all, tok_count, head_count, tok_index):
    pages_here = owner_all.shape[1]
    quarter_page = PAGE // head_count
    rows = pages_here * quarter_page
    arrival = jnp.sum(jnp.where(owner_all == tok_index, slots_all % pages_here, 0), 1)
    row = jnp.arange(rows, dtype=jnp.int32)
    target = jnp.repeat(arrival, quarter_page) * quarter_page + row % quarter_page
    place = (row[:, None] == target[None, :]).astype(BF)
    landed = landed.reshape(head_count, rows, -1)
    width = landed.shape[2] // 2
    placed = [
        jnp.dot(place, landed[h], preferred_element_type=F32).astype(BF)
        for h in range(head_count)
    ]
    cache = jnp.concatenate(
        [p[:, :width] for p in placed] + [p[:, width:] for p in placed], 1
    )
    return cache.reshape(pages_here, quarter_page, 2 * head_count * width)


def per_device(
    hidden_in,
    queries,
    keys,
    values,
    request_ids,
    out_proj,
    norm_gain,
    expert_gate_up,
    expert_down,
    shared_gate_up,
    shared_down,
    shared_gate,
    routes,
    route_weights,
    page_slots,
):
    tok_rows, model_width = hidden_in.shape
    head_width = queries.shape[1]
    heads_here = head_width // HD
    tok_count = lax.axis_size("tok")
    head_count = lax.axis_size("head")
    tok_index = lax.axis_index("tok")
    head_index = lax.axis_index("head")
    core = head_index % CORES
    column_width = model_width // head_count
    rows_of_blocks = tok_count // ROW
    half = tok_rows // 2
    slots_core = CAP // CORES

    gate_up_own = jnp.transpose(expert_gate_up[0], (1, 2, 0))
    down_own = expert_down[0]
    out_peer = lax.ppermute(out_proj, "head", INTRA)
    gate_up_peer = lax.ppermute(gate_up_own, "head", INTRA)
    down_peer = lax.ppermute(down_own, "head", INTRA)

    packed = jnp.stack(
        [
            jnp.concatenate([part[:, i * HD : (i + 1) * HD] for part in (keys, values)], 1)
            for i in range(heads_here)
        ],
        0,
    )
    row_groups = [[r * ROW + y for y in range(ROW)] for r in range(rows_of_blocks)]
    own = lax.all_to_all(
        packed, "tok", split_axis=0, concat_axis=0, tiled=True, axis_index_groups=row_groups
    )
    span = ROW * tok_rows
    base = (tok_index // ROW) * span
    padded_ids = jnp.concatenate([jnp.full((span,), -1, jnp.int32), request_ids], 0)
    window_ids = lax.dynamic_slice_in_dim(padded_ids, base, 2 * span, 0)
    ids_row = window_ids[None, :]
    ids_col = jnp.broadcast_to(window_ids[span:, None], (span, HD))
    queries, own, ids_row, ids_col = lax.optimization_barrier(
        (queries, own, ids_row, ids_col)
    )
    place_in_row = tok_index % ROW
    query_parts = []
    for step in range(ROW):
        target = (place_in_row + step) % ROW
        part = lax.dynamic_slice_in_dim(queries, target * HD, HD, 1)
        if step:
            part = lax.ppermute(
                part,
                "tok",
                [
                    (r * ROW + y, r * ROW + (y + step) % ROW)
                    for r in range(rows_of_blocks)
                    for y in range(ROW)
                ],
            )
        query_parts.append(part)
    slots_all = page_slots.reshape(tok_count, tok_rows // PAGE)
    owner_all = slots_all // (tok_rows // PAGE)
    pieces = page_pieces(keys, values, owner_all, tok_count, head_count, tok_index)
    past = lax.ppermute(
        own, "tok", [(s, s + ROW) for s in range(tok_count - ROW)]
    )
    attended = attention(
        place_in_row.reshape(1), ids_col, ids_row, jnp.stack(query_parts, 0), own, past
    )

    core_groups = [
        [
            (chip * CORES + c) * tok_count + r * ROW + y
            for c in range(CORES)
            for y in range(ROW)
        ]
        for chip in range(CHIPS)
        for r in range(rows_of_blocks)
    ]
    gathered = lax.all_to_all(
        attended.reshape(CORES * ROW, half, HD),
        BOTH,
        split_axis=0,
        concat_axis=0,
        tiled=True,
        axis_index_groups=core_groups,
    ).reshape(CORES, ROW, half, HD)
    expert_ids = jnp.arange(EXPERTS, dtype=jnp.int32)
    named = routes[:, :, None] == expert_ids[None, None, :]
    onehot = jnp.sum(named.astype(F32), 1)
    weight_of = jnp.sum(jnp.where(named, route_weights[:, :, None], 0.0), 1)
    earlier = (
        jnp.arange(tok_rows, dtype=jnp.int32)[None, :] < jnp.arange(tok_rows, dtype=jnp.int32)[:, None]
    ).astype(BF)
    rank = jnp.dot(earlier, onehot.astype(BF), preferred_element_type=F32).astype(jnp.int32)
    rank = jnp.where(onehot > 0, rank, -1)
    rank_t = rank.T
    rank_rel = jnp.where(core == 0, rank_t, jnp.roll(rank_t, half, 1))
    place = jnp.arange(slots_core, dtype=jnp.int32) * CORES
    select = (rank_rel[:, None, :] == (place + core)[None, :, None]).astype(BF)
    select = select.reshape(EXPERTS * slots_core, tok_rows)
    core_ref = core.reshape(1)
    projected, projected_low = project(core_ref, gathered, out_proj, out_peer)
    projected_far = lax.ppermute(projected_low, "head", CROSS)
    pieces, _ = lax.optimization_barrier((pieces, projected_low))
    landed = lax.all_to_all(pieces, BOTH, split_axis=0, concat_axis=0, tiled=True)
    projected_far, select, landed = lax.optimization_barrier((projected_far, select, landed))
    resid, normed_own = add_and_norm(
        core_ref, hidden_in, projected, projected_far, norm_gain[None, :]
    )
    normed_peer = lax.ppermute(normed_own, "head", INTRA)

    outgoing = gather_rows(select, normed_own, normed_peer)
    rank, weight_of, _ = lax.optimization_barrier((rank, weight_of, outgoing))
    high, low = slot_weights(rank, weight_of, CORES * EXPERTS * slots_core)
    late_own, late_peer, _ = lax.optimization_barrier((normed_own, normed_peer, outgoing))
    normed_abs = jnp.where(
        core == 0,
        jnp.concatenate([late_own, late_peer], 0),
        jnp.concatenate([late_peer, late_own], 0),
    )
    arrived = lax.all_to_all(
        outgoing.reshape(tok_count, slots_core, model_width),
        "tok",
        split_axis=0,
        concat_axis=0,
        tiled=True,
    ).reshape(tok_count * slots_core, model_width)
    shared_both = jnp.einsum("td,dgf->tgf", normed_abs, shared_gate_up, preferred_element_type=F32)
    shared_act = (jax.nn.silu(shared_both[:, 0, :]) * shared_both[:, 1, :]).astype(BF)
    shared_scale = jax.nn.sigmoid(jnp.dot(normed_abs, shared_gate, preferred_element_type=F32))
    shared_term = shared_scale[:, None] * jnp.dot(
        shared_act, shared_down, preferred_element_type=F32
    )
    chip = head_index // CORES
    chip_width = CORES * column_width
    shared_near = lax.dynamic_slice_in_dim(shared_term, chip * chip_width, chip_width, 1)
    shared_send = lax.dynamic_slice_in_dim(
        shared_term, (1 - chip) * chip_width, chip_width, 1
    ).astype(BF)
    shared_near, shared_send, arrived = lax.optimization_barrier(
        (shared_near, shared_send, arrived)
    )
    shared_far = lax.ppermute(shared_send, "head", CROSS)

    partial = experts(arrived, gate_up_own, gate_up_peer, down_own, down_peer, head_count)
    partial = partial.reshape(head_count * tok_count, slots_core, column_width)
    partial, shared_far = lax.optimization_barrier((partial, shared_far))
    returned = lax.all_to_all(partial, BOTH, split_axis=0, concat_axis=0, tiled=True)
    returned = returned.reshape(CHIPS, CORES * EXPERTS * slots_core, column_width)

    shared_chip = shared_near + shared_far.astype(F32)
    shared_own = lax.dynamic_slice_in_dim(shared_chip, core * column_width, column_width, 1)
    shared_peer = lax.dynamic_slice_in_dim(
        shared_chip, (1 - core) * column_width, column_width, 1
    ).astype(BF)
    shared_cols = shared_own + lax.ppermute(shared_peer, "head", INTRA).astype(F32)
    own_cols = lax.dynamic_slice_in_dim(resid, head_index * column_width, column_width, 1)
    peer_cols = lax.dynamic_slice_in_dim(
        resid, (head_index + 1 - 2 * core) * column_width, column_width, 1
    )
    from_peer = lax.ppermute(peer_cols, "head", INTRA)
    layer_out = combine(core_ref, high, low, returned, own_cols, from_peer, shared_cols)
    decode_cache = place_pages(landed, slots_all, owner_all, tok_count, head_count, tok_index)
    return (layer_out, decode_cache)


def solution(mesh):
    in_specs = (
        P("tok", None),
        P("tok", "head"),
        P("tok", "head"),
        P("tok", "head"),
        P(),
        P("head", None),
        P(),
        P("tok", None, None, "head"),
        P("tok", "head", None),
        P(None, None, "head"),
        P("head", None),
        P(),
        P("tok", None),
        P("tok", None),
        P(),
    )
    out_specs = (P("tok", "head"), P("tok", "head", None))
    return jax.shard_map(
        per_device, mesh=mesh, in_specs=in_specs, out_specs=out_specs, check_vma=False
    )
```

```python
import math

import jax
import jax.numpy as jnp
from jax import lax
from jax.experimental import pallas as pl
from jax.experimental.pallas import tpu as pltpu
from jax.sharding import PartitionSpec as P

HD = 128
TOP = 4
EXPERTS = 32
PAGE = 8
CAP = 48
ROW = 4
CORES = 2
CHIPS = 2
BF = jnp.bfloat16
F32 = jnp.float32
BOTH = ("head", "tok")
INTRA = [(0, 1), (1, 0), (2, 3), (3, 2)]
CROSS = [(0, 2), (2, 0), (1, 3), (3, 1)]


def pack_kernel(keys, values, out, sems):
    copies = []
    for i in range(out.shape[0]):
        for j, part in enumerate((keys, values)):
            copy = pltpu.make_async_copy(
                part.at[:, pl.ds(i * HD, HD)], out.at[i, :, pl.ds(j * HD, HD)], sems.at[i, j]
            )
            copy.start()
            copies.append(copy)
    for copy in copies:
        copy.wait()


def pack_heads(keys, values):
    rows, width = keys.shape
    hbm = pl.BlockSpec(memory_space=pltpu.HBM)
    heads = width // HD
    return pl.pallas_call(
        pack_kernel,
        out_shape=jax.ShapeDtypeStruct((heads, rows, 2 * HD), BF),
        in_specs=[hbm, hbm],
        out_specs=hbm,
        scratch_shapes=[pltpu.SemaphoreType.DMA((heads, 2))],
        compiler_params=pltpu.CompilerParams(vmem_limit_bytes=60 << 20),
        cost_estimate=pl.CostEstimate(flops=0, bytes_accessed=1 << 20, transcendentals=0),
        name="pack_heads",
    )(keys, values)


def attention_kernel(
    place, ids_row_hbm, query_hbm, own_hbm, past_hbm, out_hbm,
    ids_row, query_parts, own, past, out, sems, out_sems,
):
    block = out.shape[2] * 2
    pairs = (
        (query_hbm, query_parts),
        (own_hbm, own),
        (past_hbm, past),
        (ids_row_hbm, ids_row),
    )
    copies = [
        pltpu.make_async_copy(source, target, sems.at[i])
        for i, (source, target) in enumerate(pairs)
    ]
    for copy in copies:
        copy.start()
    for copy in copies:
        copy.wait()
    stores = []
    scale = 1.0 / math.sqrt(HD)
    span = ROW * block
    row_pos = lax.broadcasted_iota(jnp.int32, (block, block), 0)
    col_pos = lax.broadcasted_iota(jnp.int32, (block, block), 1)
    causal = col_pos <= row_pos
    same = col_pos == row_pos
    for y in range(ROW):
        query = query_parts[lax.rem(place[0] + (ROW - y), ROW)]
        row_ids = ids_row[0:1, pl.ds(span + y * block, block)]
        query_ids = jnp.sum(jnp.where(same, row_ids, 0), axis=1, keepdims=True)
        pieces = []
        for b in range(y, ROW):
            key = past[b, :, 0:HD]
            key_ids = ids_row[0:1, pl.ds(b * block, block)]
            score = lax.dot_general(
                query, key, (((1,), (1,)), ((), ())), preferred_element_type=F32
            )
            pieces.append(jnp.where(query_ids == key_ids, score * scale, -1e30))
        for b in range(y + 1):
            key = own[b, :, 0:HD]
            key_ids = ids_row[0:1, pl.ds(span + b * block, block)]
            score = lax.dot_general(
                query, key, (((1,), (1,)), ((), ())), preferred_element_type=F32
            )
            allowed = query_ids == key_ids
            if b == y:
                allowed = allowed & causal
            pieces.append(jnp.where(allowed, score * scale, -1e30))
        top = pieces[0].max(-1, keepdims=True)
        for piece in pieces[1:]:
            top = jnp.maximum(top, piece.max(-1, keepdims=True))
        weights = [jnp.exp(piece - top) for piece in pieces]
        total = weights[0].sum(-1, keepdims=True)
        for weight in weights[1:]:
            total = total + weight.sum(-1, keepdims=True)
        inverse = 1.0 / total
        mixed = jnp.zeros((block, HD), F32)
        index = 0
        for b in range(y, ROW):
            prob = (weights[index] * inverse).astype(BF)
            mixed += jnp.dot(prob, past[b, :, HD : 2 * HD], preferred_element_type=F32)
            index += 1
        for b in range(y + 1):
            prob = (weights[index] * inverse).astype(BF)
            mixed += jnp.dot(prob, own[b, :, HD : 2 * HD], preferred_element_type=F32)
            index += 1
        half = block // 2
        out[0, y] = mixed[:half].astype(BF)
        out[1, y] = mixed[half:].astype(BF)
        for c in range(2):
            store = pltpu.make_async_copy(out.at[c, y], out_hbm.at[c, y], out_sems.at[c, y])
            store.start()
            stores.append(store)
    for store in stores:
        store.wait()


def attention(place, ids_row, query_parts, own, past):
    block = own.shape[1]
    hbm = pl.BlockSpec(memory_space=pltpu.HBM)
    operands = (ids_row, query_parts, own, past)
    result = jax.ShapeDtypeStruct((2, ROW, block // 2, HD), BF)
    return pl.pallas_call(
        attention_kernel,
        out_shape=result,
        in_specs=[pl.BlockSpec(memory_space=pltpu.SMEM)] + [hbm] * 4,
        out_specs=hbm,
        scratch_shapes=[pltpu.VMEM(o.shape, o.dtype) for o in operands]
        + [
            pltpu.VMEM(result.shape, BF),
            pltpu.SemaphoreType.DMA((4,)),
            pltpu.SemaphoreType.DMA((2, ROW)),
        ],
        compiler_params=pltpu.CompilerParams(vmem_limit_bytes=58 << 20),
        cost_estimate=pl.CostEstimate(
            flops=4 * 5 * ROW * block * block * HD,
            bytes_accessed=3 << 20,
            transcendentals=5 * ROW * block * block,
        ),
        name="row_attention",
    )(place, *operands)


def project_kernel(
    core, att_hbm, own_hbm, peer_hbm, total_hbm, low_hbm,
    att, own, peer, total, total_low, att_sem, sems, out_sems,
):
    width = total.shape[1]
    step = width // 4
    att_copy = pltpu.make_async_copy(att_hbm, att, att_sem)
    att_copy.start()
    copies = []
    for i in range(4):
        cols = pl.ds(i * step, step)
        copies.append(
            (
                pltpu.make_async_copy(own_hbm.at[:, cols], own.at[:, cols], sems.at[0, i]),
                pltpu.make_async_copy(peer_hbm.at[:, cols], peer.at[:, cols], sems.at[1, i]),
            )
        )
    for pair in copies:
        for copy in pair:
            copy.start()
    att_copy.wait()
    c = core[0]
    stores = []
    left = jnp.concatenate([att[c, y] for y in range(ROW)], 1)
    right = jnp.concatenate([att[1 - c, y] for y in range(ROW)], 1)
    for i in range(4):
        cols = pl.ds(i * step, step)
        for copy in copies[i]:
            copy.wait()
        part = jnp.dot(left, own[:, cols], preferred_element_type=F32) + jnp.dot(
            right, peer[:, cols], preferred_element_type=F32
        )
        total_low[:, cols] = part.astype(BF)
        total[:, cols] = part
        for j, (source, target) in enumerate(((total_low, low_hbm), (total, total_hbm))):
            store = pltpu.make_async_copy(
                source.at[:, cols], target.at[:, cols], out_sems.at[j, i]
            )
            store.start()
            stores.append(store)
    for store in stores:
        store.wait()


def project(core, att, out_own, out_peer):
    rows = att.shape[2]
    depth, width = out_own.shape
    hbm = pl.BlockSpec(memory_space=pltpu.HBM)
    return pl.pallas_call(
        project_kernel,
        out_shape=(
            jax.ShapeDtypeStruct((rows, width), F32),
            jax.ShapeDtypeStruct((rows, width), BF),
        ),
        in_specs=[pl.BlockSpec(memory_space=pltpu.SMEM), hbm, hbm, hbm],
        out_specs=(hbm, hbm),
        scratch_shapes=[
            pltpu.VMEM(att.shape, BF),
            pltpu.VMEM((depth, width), BF),
            pltpu.VMEM((depth, width), BF),
            pltpu.VMEM((rows, width), F32),
            pltpu.VMEM((rows, width), BF),
            pltpu.SemaphoreType.DMA,
            pltpu.SemaphoreType.DMA((2, 4)),
            pltpu.SemaphoreType.DMA((2, 4)),
        ],
        compiler_params=pltpu.CompilerParams(vmem_limit_bytes=58 << 20),
        cost_estimate=pl.CostEstimate(
            flops=4 * rows * depth * width, bytes_accessed=6 << 20, transcendentals=0
        ),
        name="project",
    )(core, att, out_own, out_peer)


def norm_kernel(
    core, hidden_hbm, near_hbm, far_hbm, gain_hbm, resid_hbm, normed_hbm,
    hidden, near, far, gain, normed, sems, out_sems,
):
    rows = near.shape[0]
    parts = 2
    block = rows // parts
    start = pl.multiple_of(core[0] * rows, rows)
    gain_copy = pltpu.make_async_copy(gain_hbm, gain, sems.at[3, 0])
    gain_copy.start()
    copies = []
    for i in range(parts):
        here = pl.ds(i * block, block)
        copies.append(
            [
                pltpu.make_async_copy(near_hbm.at[here], near.at[here], sems.at[0, i]),
                pltpu.make_async_copy(far_hbm.at[here], far.at[here], sems.at[1, i]),
                pltpu.make_async_copy(
                    hidden_hbm.at[pl.ds(start + i * block, block)], hidden.at[here], sems.at[2, i]
                ),
            ]
        )
        for copy in copies[i]:
            copy.start()
    gain_copy.wait()
    stores = []
    for i in range(parts):
        here = pl.ds(i * block, block)
        for copy in copies[i]:
            copy.wait()
        value = hidden[here, :].astype(F32) + (near[here, :] + far[here, :].astype(F32))
        mean_square = jnp.mean(value * value, axis=-1, keepdims=True)
        normed[here, :] = (value * lax.rsqrt(mean_square + 1e-06) * gain[...]).astype(BF)
        near[here, :] = value
        for j, (source, target) in enumerate(((normed, normed_hbm), (near, resid_hbm))):
            store = pltpu.make_async_copy(source.at[here], target.at[here], out_sems.at[j, i])
            store.start()
            stores.append(store)
    for store in stores:
        store.wait()


def add_and_norm(core, hidden, near, far, gain):
    rows, width = near.shape
    hbm = pl.BlockSpec(memory_space=pltpu.HBM)
    return pl.pallas_call(
        norm_kernel,
        out_shape=(
            jax.ShapeDtypeStruct((rows, width), F32),
            jax.ShapeDtypeStruct((rows, width), BF),
        ),
        in_specs=[pl.BlockSpec(memory_space=pltpu.SMEM), hbm, hbm, hbm, hbm],
        out_specs=(hbm, hbm),
        scratch_shapes=[
            pltpu.VMEM((rows, width), BF),
            pltpu.VMEM((rows, width), F32),
            pltpu.VMEM((rows, width), BF),
            pltpu.VMEM((1, width), F32),
            pltpu.VMEM((rows, width), BF),
            pltpu.SemaphoreType.DMA((4, 2)),
            pltpu.SemaphoreType.DMA((2, 2)),
        ],
        compiler_params=pltpu.CompilerParams(vmem_limit_bytes=58 << 20),
        cost_estimate=pl.CostEstimate(
            flops=8 * rows * width, bytes_accessed=4 << 20, transcendentals=rows
        ),
        name="add_and_norm",
    )(core, hidden, near, far, gain)


def gather_kernel(
    select_hbm, own_hbm, peer_hbm, out_hbm, select, rows, out, sems, out_sems
):
    half = rows.shape[0] // 2
    total, block = out.shape[0], out.shape[0] // 3
    copies = [
        pltpu.make_async_copy(own_hbm, rows.at[pl.ds(0, half)], sems.at[0]),
        pltpu.make_async_copy(peer_hbm, rows.at[pl.ds(half, half)], sems.at[1]),
        pltpu.make_async_copy(select_hbm, select, sems.at[2]),
    ]
    for copy in copies:
        copy.start()
    for copy in copies:
        copy.wait()
    stores = []
    for i in range(total // block):
        here = pl.ds(i * block, block)
        out[here, :] = jnp.dot(
            select[here, :], rows[...], preferred_element_type=F32
        ).astype(BF)
        store = pltpu.make_async_copy(out.at[here], out_hbm.at[here], out_sems.at[i])
        store.start()
        stores.append(store)
    for store in stores:
        store.wait()


def gather_rows(select, own, peer):
    slots, rows = select.shape
    width = own.shape[1]
    hbm = pl.BlockSpec(memory_space=pltpu.HBM)
    return pl.pallas_call(
        gather_kernel,
        out_shape=jax.ShapeDtypeStruct((slots, width), BF),
        in_specs=[hbm, hbm, hbm],
        out_specs=hbm,
        scratch_shapes=[
            pltpu.VMEM((slots, rows), BF),
            pltpu.VMEM((rows, width), BF),
            pltpu.VMEM((slots, width), BF),
            pltpu.SemaphoreType.DMA((3,)),
            pltpu.SemaphoreType.DMA((3,)),
        ],
        compiler_params=pltpu.CompilerParams(vmem_limit_bytes=58 << 20),
        cost_estimate=pl.CostEstimate(
            flops=2 * slots * rows * width, bytes_accessed=5 << 20, transcendentals=0
        ),
        name="gather_rows",
    )(select, own, peer)


def slot_weight_kernel(rank, weight, high):
    slots = high.shape[1]
    per_core = CAP // CORES
    experts_here = rank.shape[1]
    lane = lax.broadcasted_iota(jnp.int32, (1, slots), 1)
    expert_of = lax.rem(lax.div(lane, per_core), experts_here)
    wanted = lax.rem(lane, per_core) * CORES + lax.div(lane, per_core * experts_here)
    expand = (
        lax.broadcasted_iota(jnp.int32, (experts_here, slots), 0) == expert_of
    ).astype(BF)
    ranks = jnp.dot(rank[...].astype(BF), expand, preferred_element_type=F32)
    hit = ranks.astype(jnp.int32) == wanted
    spread = jnp.dot(weight[...].astype(BF), expand, preferred_element_type=F32)
    high[...] = jnp.where(hit, spread, 0.0).astype(BF)


def slot_weights(rank, weight, slots):
    rows = rank.shape[0]
    vmem = pl.BlockSpec(memory_space=pltpu.VMEM)
    shape = jax.ShapeDtypeStruct((rows, slots), BF)
    return pl.pallas_call(
        slot_weight_kernel,
        out_shape=shape,
        in_specs=[vmem, vmem],
        out_specs=vmem,
        compiler_params=pltpu.CompilerParams(vmem_limit_bytes=16 << 20),
        cost_estimate=pl.CostEstimate(
            flops=6 * rows * slots * 32, bytes_accessed=2 << 20, transcendentals=0
        ),
        name="slot_weights",
    )(rank, weight)


def expert_kernel(
    x_hbm, both_own, both_peer, down_own, down_peer, out_hbm,
    x, gate, up, down, act, out, x_sems, sems, down_sems, out_sems,
):
    hidden = both_own.shape[1]
    rows = x.shape[0]
    groups, _, width = out.shape
    parts = 3
    block = rows // parts
    step = 256
    bounds = [(lo, min(lo + step, 2 * hidden)) for lo in range(0, 2 * hidden, step)]
    x_copies = [
        pltpu.make_async_copy(
            x_hbm.at[pl.ds(m * block, block)], x.at[pl.ds(m * block, block)], x_sems.at[m]
        )
        for m in range(parts)
    ]
    chunks = []
    for n, (lo, hi) in enumerate(bounds):
        copies = []
        for j, (source, start, stop) in enumerate(
            (
                (both_own, lo, min(hi, hidden)),
                (both_peer, max(lo, hidden) - hidden, hi - hidden),
            )
        ):
            if stop <= start:
                continue
            shift = hidden * j
            for k, target in enumerate((gate, up)):
                copies.append(
                    pltpu.make_async_copy(
                        source.at[k, pl.ds(start, stop - start)],
                        target.at[pl.ds(start + shift, stop - start)],
                        sems.at[n, j, k],
                    )
                )
        chunks.append(copies)
    down_copies = [
        pltpu.make_async_copy(source, down.at[pl.ds(j * hidden, hidden)], down_sems.at[j])
        for j, source in enumerate((down_own, down_peer))
    ]
    def begin(copies):
        for copy in copies:
            copy.start()

    def finish(copies):
        for copy in copies:
            copy.wait()

    def halves(n, m):
        lo, hi = bounds[n]
        here = pl.ds(m * block, block)
        left = x[here, :]
        g = lax.dot_general(left, gate[lo:hi, :], contract, preferred_element_type=F32)
        u = lax.dot_general(left, up[lo:hi, :], contract, preferred_element_type=F32)
        act[here, lo:hi] = (g / (1.0 + jnp.exp(-g)) * u).astype(BF)

    contract = (((1,), (1,)), ((), ()))
    begin([x_copies[0]] + chunks[0])
    begin(x_copies[1:])
    finish([x_copies[0]] + chunks[0])
    begin(chunks[1])
    halves(0, 0)
    finish(x_copies[1:])
    begin(chunks[2])
    for m in range(1, parts):
        halves(0, m)
    finish(chunks[1])
    begin(down_copies)
    for m in range(parts):
        halves(1, m)
    finish(chunks[2])
    for m in range(parts):
        halves(2, m)
    finish(down_copies)
    stores = []
    for i in range(groups):
        for m in range(parts):
            here = pl.ds(m * block, block)
            result = jnp.dot(
                act[here, :], down[:, i * width : (i + 1) * width], preferred_element_type=F32
            )
            out[i, here, :] = result.astype(BF)
            store = pltpu.make_async_copy(
                out.at[i, here], out_hbm.at[i, here], out_sems.at[m, i]
            )
            store.start()
            stores.append(store)
    for store in stores:
        store.wait()


def experts(x, both_own, both_peer, down_own, down_peer, groups):
    rows, depth = x.shape
    hidden, width = down_own.shape
    column_width = width // groups
    hbm = pl.BlockSpec(memory_space=pltpu.HBM)
    return pl.pallas_call(
        expert_kernel,
        out_shape=jax.ShapeDtypeStruct((groups, rows, column_width), BF),
        in_specs=[hbm] * 5,
        out_specs=hbm,
        scratch_shapes=[
            pltpu.VMEM((rows, depth), BF),
            pltpu.VMEM((2 * hidden, depth), BF),
            pltpu.VMEM((2 * hidden, depth), BF),
            pltpu.VMEM((2 * hidden, width), BF),
            pltpu.VMEM((rows, 2 * hidden), BF),
            pltpu.VMEM((groups, rows, column_width), BF),
            pltpu.SemaphoreType.DMA((3,)),
            pltpu.SemaphoreType.DMA((pl.cdiv(2 * hidden, 256), 2, 2)),
            pltpu.SemaphoreType.DMA((2,)),
            pltpu.SemaphoreType.DMA((3, groups)),
        ],
        compiler_params=pltpu.CompilerParams(vmem_limit_bytes=60 << 20),
        cost_estimate=pl.CostEstimate(
            flops=12 * rows * depth * hidden,
            bytes_accessed=15 << 20,
            transcendentals=2 * rows * hidden,
        ),
        name="experts",
    )(x, both_own, both_peer, down_own, down_peer)


def combine_kernel(
    core, high_hbm, back_hbm, mine_hbm, peers_hbm, shared_hbm, out,
    high, back, mine, peers, shared, sems,
):
    rows = mine.shape[0]
    chips, depth = back.shape[0], back.shape[1]
    block = depth // CORES
    pieces = [(chip, pl.ds(c * block, block)) for chip in range(chips) for c in range(CORES)]
    copies = [
        pltpu.make_async_copy(back_hbm.at[chip, here], back.at[chip, here], sems.at[i])
        for i, (chip, here) in enumerate(pieces)
    ]
    rest = [
        pltpu.make_async_copy(source, target, sems.at[len(pieces) + i])
        for i, (source, target) in enumerate(
            (
                (high_hbm, high),
                (shared_hbm, shared),
                (mine_hbm, mine),
                (peers_hbm, peers),
            )
        )
    ]
    for copy in [rest[0]] + copies + rest[1:]:
        copy.start()
    total = None
    for i, (copy, (chip, here)) in enumerate(zip(copies, pieces)):
        if i == 0:
            rest[0].wait()
        copy.wait()
        part = jnp.dot(high[:, here], back[chip, here], preferred_element_type=F32)
        total = part if total is None else total + part
    for copy in rest[1:]:
        copy.wait()
    total += shared[...]
    first = core[0] == 0
    low_half = jnp.where(first, mine[...], peers[...])
    high_half = jnp.where(first, peers[...], mine[...])
    out[0:rows, :] = (total[0:rows] + low_half).astype(BF)
    out[rows : 2 * rows, :] = (total[rows:] + high_half).astype(BF)


def combine(core, high, returned, mine, peers, shared):
    hbm = pl.BlockSpec(memory_space=pltpu.HBM)
    vmem = pl.BlockSpec(memory_space=pltpu.VMEM)
    rows, width = shared.shape
    operands = (high, returned, mine, peers, shared)
    return pl.pallas_call(
        combine_kernel,
        out_shape=jax.ShapeDtypeStruct((rows, width), BF),
        in_specs=[pl.BlockSpec(memory_space=pltpu.SMEM)] + [hbm] * 5,
        out_specs=vmem,
        scratch_shapes=[pltpu.VMEM(o.shape, o.dtype) for o in operands]
        + [pltpu.SemaphoreType.DMA((8,))],
        compiler_params=pltpu.CompilerParams(vmem_limit_bytes=60 << 20),
        cost_estimate=pl.CostEstimate(
            flops=8 * rows * width * high.shape[1], bytes_accessed=7 << 20, transcendentals=0
        ),
        name="combine",
    )(core, *operands)


def page_pieces(keys, values, owner_all, tok_count, head_count, tok_index):
    pages_here = owner_all.shape[1]
    tok_rows = keys.shape[0]
    quarter_page = PAGE // head_count
    mine = lax.dynamic_index_in_dim(owner_all, tok_index, 0, keepdims=False)
    row = jnp.arange(tok_rows, dtype=jnp.int32)
    quarter = row // (tok_count * quarter_page)
    owner = row // quarter_page % tok_count
    line = quarter * quarter_page + row % quarter_page
    token_owner = jnp.repeat(mine, PAGE)
    token_line = jnp.arange(tok_rows, dtype=jnp.int32) % PAGE
    pick = (
        (owner[:, None] == token_owner[None, :]) & (line[:, None] == token_line[None, :])
    ).astype(BF)
    parts = [
        jnp.dot(pick, part, preferred_element_type=F32).astype(BF) for part in (keys, values)
    ]
    return jnp.concatenate(parts, 1).reshape(head_count, tok_count * quarter_page, -1)


def place_pages(landed, slots_all, owner_all, head_count, head_index, tok_index):
    pages_here = owner_all.shape[1]
    quarter_page = PAGE // head_count
    rows = pages_here * quarter_page
    arrival = jnp.sum(jnp.where(owner_all == tok_index, slots_all % pages_here, 0), 1)
    row = jnp.arange(rows, dtype=jnp.int32)
    target = jnp.repeat(arrival, quarter_page) * quarter_page + row % quarter_page
    place = (row[:, None] == target[None, :]).astype(BF)
    placed = jnp.dot(
        place, landed.reshape(rows, -1), preferred_element_type=F32
    ).astype(BF)
    chip_width = placed.shape[1] // head_count
    width = chip_width // 2
    ordered = [
        lax.dynamic_slice_in_dim(placed, (g ^ head_index) * chip_width, chip_width, 1)
        for g in range(head_count)
    ]
    cache = jnp.concatenate(
        [p[:, :width] for p in ordered] + [p[:, width:] for p in ordered], 1
    )
    return cache.reshape(pages_here, quarter_page, 2 * head_count * width)


def per_device(
    hidden_in,
    queries,
    keys,
    values,
    request_ids,
    out_proj,
    norm_gain,
    expert_gate_up,
    expert_down,
    shared_gate_up,
    shared_down,
    shared_gate,
    routes,
    route_weights,
    page_slots,
):
    tok_rows, model_width = hidden_in.shape
    head_width = queries.shape[1]
    heads_here = head_width // HD
    tok_count = lax.axis_size("tok")
    head_count = lax.axis_size("head")
    tok_index = lax.axis_index("tok")
    head_index = lax.axis_index("head")
    core = head_index % CORES
    column_width = model_width // head_count
    rows_of_blocks = tok_count // ROW
    half = tok_rows // 2
    slots_core = CAP // CORES

    gate_up_own = jnp.transpose(expert_gate_up[0], (1, 2, 0))
    down_own = expert_down[0]
    out_peer = lax.ppermute(out_proj, "head", INTRA)
    gate_up_peer = lax.ppermute(gate_up_own, "head", INTRA)
    down_peer = lax.ppermute(down_own, "head", INTRA)

    packed = pack_heads(keys, values)
    row_groups = [[r * ROW + y for y in range(ROW)] for r in range(rows_of_blocks)]
    own = lax.all_to_all(
        packed, "tok", split_axis=0, concat_axis=0, tiled=True, axis_index_groups=row_groups
    )
    span = ROW * tok_rows
    base = (tok_index // ROW) * span
    padded_ids = jnp.concatenate([jnp.full((span,), -1, jnp.int32), request_ids], 0)
    window_ids = lax.dynamic_slice_in_dim(padded_ids, base, 2 * span, 0)
    ids_row = window_ids[None, :]
    queries, own = lax.optimization_barrier((queries, own))
    place_in_row = tok_index % ROW
    query_parts = []
    for step in range(ROW):
        target = (place_in_row + step) % ROW
        part = lax.dynamic_slice_in_dim(queries, target * HD, HD, 1)
        if step:
            part = lax.ppermute(
                part,
                "tok",
                [
                    (r * ROW + y, r * ROW + (y + step) % ROW)
                    for r in range(rows_of_blocks)
                    for y in range(ROW)
                ],
            )
        query_parts.append(part)
    slots_all = page_slots.reshape(tok_count, tok_rows // PAGE)
    owner_all = slots_all // (tok_rows // PAGE)
    pieces = page_pieces(keys, values, owner_all, tok_count, head_count, tok_index)
    past = lax.ppermute(
        own, "tok", [(s, s + ROW) for s in range(tok_count - ROW)]
    )
    attended = attention(
        place_in_row.reshape(1), ids_row, jnp.stack(query_parts, 0), own, past
    )

    core_groups = [
        [
            (chip * CORES + c) * tok_count + r * ROW + y
            for c in range(CORES)
            for y in range(ROW)
        ]
        for chip in range(CHIPS)
        for r in range(rows_of_blocks)
    ]
    gathered = lax.all_to_all(
        attended.reshape(CORES * ROW, half, HD),
        BOTH,
        split_axis=0,
        concat_axis=0,
        tiled=True,
        axis_index_groups=core_groups,
    ).reshape(CORES, ROW, half, HD)
    expert_ids = jnp.arange(EXPERTS, dtype=jnp.int32)
    named = routes[:, :, None] == expert_ids[None, None, :]
    onehot = jnp.sum(named.astype(F32), 1)
    weight_of = jnp.sum(jnp.where(named, route_weights[:, :, None], 0.0), 1)
    earlier = (
        jnp.arange(tok_rows, dtype=jnp.int32)[None, :] < jnp.arange(tok_rows, dtype=jnp.int32)[:, None]
    ).astype(BF)
    rank = jnp.dot(earlier, onehot.astype(BF), preferred_element_type=F32).astype(jnp.int32)
    rank = jnp.where(onehot > 0, rank, -1)
    rank_t = rank.T
    rank_rel = jnp.where(core == 0, rank_t, jnp.roll(rank_t, half, 1))
    place = jnp.arange(slots_core, dtype=jnp.int32) * CORES
    select = (rank_rel[:, None, :] == (place + core)[None, :, None]).astype(BF)
    select = select.reshape(EXPERTS * slots_core, tok_rows)
    core_ref = core.reshape(1)
    page_rows = [lax.dynamic_index_in_dim(pieces, head_index, 0, keepdims=False)]
    for flip in range(1, head_count):
        part = lax.dynamic_index_in_dim(pieces, head_index ^ flip, 0, keepdims=False)
        part, _ = lax.optimization_barrier((part, attended))
        page_rows.append(
            lax.ppermute(part, "head", [(h, h ^ flip) for h in range(head_count)])
        )
    page_rows, gathered = lax.optimization_barrier((page_rows, gathered))
    projected, projected_low = project(core_ref, gathered, out_proj, out_peer)
    projected_far = lax.ppermute(projected_low, "head", CROSS)
    page_rows, _ = lax.optimization_barrier((page_rows, projected_low))
    page_rows = jnp.concatenate(page_rows, 1).reshape(tok_count, -1, head_count * 2 * head_width)
    landed = lax.all_to_all(page_rows, "tok", split_axis=0, concat_axis=0, tiled=True)
    projected_far, select, landed = lax.optimization_barrier((projected_far, select, landed))
    resid, normed_own = add_and_norm(
        core_ref, hidden_in, projected, projected_far, norm_gain[None, :]
    )
    normed_peer = lax.ppermute(normed_own, "head", INTRA)

    outgoing = gather_rows(select, normed_own, normed_peer)
    rank, weight_of, _ = lax.optimization_barrier((rank, weight_of, outgoing))
    high = slot_weights(rank, weight_of, CORES * EXPERTS * slots_core)
    late_own, late_peer, _ = lax.optimization_barrier((normed_own, normed_peer, outgoing))
    normed_abs = jnp.where(
        core == 0,
        jnp.concatenate([late_own, late_peer], 0),
        jnp.concatenate([late_peer, late_own], 0),
    )
    arrived = lax.all_to_all(
        outgoing.reshape(tok_count, slots_core, model_width),
        "tok",
        split_axis=0,
        concat_axis=0,
        tiled=True,
    ).reshape(tok_count * slots_core, model_width)
    shared_both = jnp.einsum("td,dgf->tgf", normed_abs, shared_gate_up, preferred_element_type=F32)
    shared_act = (jax.nn.silu(shared_both[:, 0, :]) * shared_both[:, 1, :]).astype(BF)
    shared_scale = jax.nn.sigmoid(jnp.dot(normed_abs, shared_gate, preferred_element_type=F32))
    shared_term = shared_scale[:, None] * jnp.dot(
        shared_act, shared_down, preferred_element_type=F32
    )
    chip = head_index // CORES
    chip_width = CORES * column_width
    shared_near = lax.dynamic_slice_in_dim(shared_term, chip * chip_width, chip_width, 1)
    shared_send = lax.dynamic_slice_in_dim(
        shared_term, (1 - chip) * chip_width, chip_width, 1
    ).astype(BF)
    shared_near, shared_send, arrived = lax.optimization_barrier(
        (shared_near, shared_send, arrived)
    )
    shared_far = lax.ppermute(shared_send, "head", CROSS)

    partial = experts(arrived, gate_up_own, gate_up_peer, down_own, down_peer, head_count)
    partial = partial.reshape(head_count * tok_count, slots_core, column_width)
    partial, shared_far = lax.optimization_barrier((partial, shared_far))
    returned = lax.all_to_all(partial, BOTH, split_axis=0, concat_axis=0, tiled=True)
    returned = returned.reshape(CHIPS, CORES * EXPERTS * slots_core, column_width)

    shared_chip = shared_near + shared_far.astype(F32)
    shared_own = lax.dynamic_slice_in_dim(shared_chip, core * column_width, column_width, 1)
    shared_peer = lax.dynamic_slice_in_dim(
        shared_chip, (1 - core) * column_width, column_width, 1
    ).astype(BF)
    shared_cols = shared_own + lax.ppermute(shared_peer, "head", INTRA).astype(F32)
    own_cols = lax.dynamic_slice_in_dim(resid, head_index * column_width, column_width, 1)
    peer_cols = lax.dynamic_slice_in_dim(
        resid, (head_index + 1 - 2 * core) * column_width, column_width, 1
    )
    from_peer = lax.ppermute(peer_cols, "head", INTRA)
    layer_out = combine(core_ref, high, returned, own_cols, from_peer, shared_cols)
    decode_cache = place_pages(landed, slots_all, owner_all, head_count, head_index, tok_index)
    return (layer_out, decode_cache)


def solution(mesh):
    in_specs = (
        P("tok", None),
        P("tok", "head"),
        P("tok", "head"),
        P("tok", "head"),
        P(),
        P("head", None),
        P(),
        P("tok", None, None, "head"),
        P("tok", "head", None),
        P(None, None, "head"),
        P("head", None),
        P(),
        P("tok", None),
        P("tok", None),
        P(),
    )
    out_specs = (P("tok", "head"), P("tok", "head", None))
    return jax.shard_map(
        per_device, mesh=mesh, in_specs=in_specs, out_specs=out_specs, check_vma=False
    )
```

```python
import math

import jax
import jax.numpy as jnp
from jax import lax
from jax.experimental import pallas as pl
from jax.experimental.pallas import tpu as pltpu
from jax.sharding import PartitionSpec as P

HD = 128
TOP = 4
EXPERTS = 32
PAGE = 8
CAP = 48
ROW = 4
CORES = 2
CHIPS = 2
BF = jnp.bfloat16
F32 = jnp.float32
BOTH = ("head", "tok")
INTRA = [(0, 1), (1, 0), (2, 3), (3, 2)]
CROSS = [(0, 2), (2, 0), (1, 3), (3, 1)]


def pack_kernel(keys, values, out):
    for i in range(out.shape[0]):
        here = pl.ds(i * HD, HD)
        out[i, :, 0:HD] = keys[:, here]
        out[i, :, HD : 2 * HD] = values[:, here]


def pack_heads(keys, values):
    rows, width = keys.shape
    vmem = pl.BlockSpec(memory_space=pltpu.VMEM)
    heads = width // HD
    return pl.pallas_call(
        pack_kernel,
        out_shape=jax.ShapeDtypeStruct((heads, rows, 2 * HD), BF),
        in_specs=[vmem, vmem],
        out_specs=vmem,
        compiler_params=pltpu.CompilerParams(vmem_limit_bytes=60 << 20),
        cost_estimate=pl.CostEstimate(flops=0, bytes_accessed=1 << 20, transcendentals=0),
        name="pack_heads",
    )(keys, values)


def attention_kernel(
    place, ids_row_hbm, query_hbm, own_hbm, past_hbm, out_hbm,
    ids_row, query_parts, own, past, out, sems, out_sems,
):
    block = out.shape[2] * 2
    pairs = (
        (query_hbm, query_parts),
        (own_hbm, own),
        (past_hbm, past),
        (ids_row_hbm, ids_row),
    )
    copies = [
        pltpu.make_async_copy(source, target, sems.at[i])
        for i, (source, target) in enumerate(pairs)
    ]
    for copy in copies:
        copy.start()
    for copy in copies:
        copy.wait()
    stores = []
    scale = 1.0 / math.sqrt(HD)
    span = ROW * block
    row_pos = lax.broadcasted_iota(jnp.int32, (block, block), 0)
    col_pos = lax.broadcasted_iota(jnp.int32, (block, block), 1)
    causal = col_pos <= row_pos
    same = col_pos == row_pos
    for y in range(ROW):
        query = query_parts[lax.rem(place[0] + (ROW - y), ROW)]
        row_ids = ids_row[0:1, pl.ds(span + y * block, block)]
        query_ids = jnp.sum(jnp.where(same, row_ids, 0), axis=1, keepdims=True)
        pieces = []
        for b in range(y, ROW):
            key = past[b, :, 0:HD]
            key_ids = ids_row[0:1, pl.ds(b * block, block)]
            score = lax.dot_general(
                query, key, (((1,), (1,)), ((), ())), preferred_element_type=F32
            )
            pieces.append(jnp.where(query_ids == key_ids, score, -1e30))
        for b in range(y + 1):
            key = own[b, :, 0:HD]
            key_ids = ids_row[0:1, pl.ds(span + b * block, block)]
            score = lax.dot_general(
                query, key, (((1,), (1,)), ((), ())), preferred_element_type=F32
            )
            allowed = query_ids == key_ids
            if b == y:
                allowed = allowed & causal
            pieces.append(jnp.where(allowed, score, -1e30))
        top = pieces[0].max(-1, keepdims=True)
        for piece in pieces[1:]:
            top = jnp.maximum(top, piece.max(-1, keepdims=True))
        weights = [jnp.exp((piece - top) * scale) for piece in pieces]
        total = weights[0].sum(-1, keepdims=True)
        for weight in weights[1:]:
            total = total + weight.sum(-1, keepdims=True)
        inverse = 1.0 / total
        mixed = jnp.zeros((block, HD), F32)
        index = 0
        for b in range(y, ROW):
            prob = weights[index].astype(BF)
            mixed += jnp.dot(prob, past[b, :, HD : 2 * HD], preferred_element_type=F32)
            index += 1
        for b in range(y + 1):
            prob = weights[index].astype(BF)
            mixed += jnp.dot(prob, own[b, :, HD : 2 * HD], preferred_element_type=F32)
            index += 1
        mixed = mixed * inverse
        half = block // 2
        out[0, y] = mixed[:half].astype(BF)
        out[1, y] = mixed[half:].astype(BF)
        for c in range(2):
            store = pltpu.make_async_copy(out.at[c, y], out_hbm.at[c, y], out_sems.at[c, y])
            store.start()
            stores.append(store)
    for store in stores:
        store.wait()


def attention(place, ids_row, query_parts, own, past):
    block = own.shape[1]
    hbm = pl.BlockSpec(memory_space=pltpu.HBM)
    operands = (ids_row, query_parts, own, past)
    result = jax.ShapeDtypeStruct((2, ROW, block // 2, HD), BF)
    return pl.pallas_call(
        attention_kernel,
        out_shape=result,
        in_specs=[pl.BlockSpec(memory_space=pltpu.SMEM)] + [hbm] * 4,
        out_specs=hbm,
        scratch_shapes=[pltpu.VMEM(o.shape, o.dtype) for o in operands]
        + [
            pltpu.VMEM(result.shape, BF),
            pltpu.SemaphoreType.DMA((4,)),
            pltpu.SemaphoreType.DMA((2, ROW)),
        ],
        compiler_params=pltpu.CompilerParams(vmem_limit_bytes=58 << 20),
        cost_estimate=pl.CostEstimate(
            flops=4 * 5 * ROW * block * block * HD,
            bytes_accessed=3 << 20,
            transcendentals=5 * ROW * block * block,
        ),
        name="row_attention",
    )(place, *operands)


def project_kernel(
    core, att_hbm, own_hbm, peer_hbm, total_hbm, low_hbm,
    att, own, peer, total, total_low, att_sem, sems, out_sems,
):
    width = total.shape[1]
    step = width // 4
    att_copy = pltpu.make_async_copy(att_hbm, att, att_sem)
    att_copy.start()
    copies = []
    for i in range(4):
        cols = pl.ds(i * step, step)
        copies.append(
            (
                pltpu.make_async_copy(own_hbm.at[:, cols], own.at[:, cols], sems.at[0, i]),
                pltpu.make_async_copy(peer_hbm.at[:, cols], peer.at[:, cols], sems.at[1, i]),
            )
        )
    for pair in copies:
        for copy in pair:
            copy.start()
    att_copy.wait()
    c = core[0]
    stores = []
    left = jnp.concatenate([att[c, y] for y in range(ROW)], 1)
    right = jnp.concatenate([att[1 - c, y] for y in range(ROW)], 1)
    for i in range(4):
        cols = pl.ds(i * step, step)
        for copy in copies[i]:
            copy.wait()
        part = jnp.dot(left, own[:, cols], preferred_element_type=F32) + jnp.dot(
            right, peer[:, cols], preferred_element_type=F32
        )
        total_low[:, cols] = part.astype(BF)
        total[:, cols] = part
        for j, (source, target) in enumerate(((total_low, low_hbm), (total, total_hbm))):
            store = pltpu.make_async_copy(
                source.at[:, cols], target.at[:, cols], out_sems.at[j, i]
            )
            store.start()
            stores.append(store)
    for store in stores:
        store.wait()


def project(core, att, out_own, out_peer):
    rows = att.shape[2]
    depth, width = out_own.shape
    hbm = pl.BlockSpec(memory_space=pltpu.HBM)
    return pl.pallas_call(
        project_kernel,
        out_shape=(
            jax.ShapeDtypeStruct((rows, width), F32),
            jax.ShapeDtypeStruct((rows, width), BF),
        ),
        in_specs=[pl.BlockSpec(memory_space=pltpu.SMEM), hbm, hbm, hbm],
        out_specs=(hbm, hbm),
        scratch_shapes=[
            pltpu.VMEM(att.shape, BF),
            pltpu.VMEM((depth, width), BF),
            pltpu.VMEM((depth, width), BF),
            pltpu.VMEM((rows, width), F32),
            pltpu.VMEM((rows, width), BF),
            pltpu.SemaphoreType.DMA,
            pltpu.SemaphoreType.DMA((2, 4)),
            pltpu.SemaphoreType.DMA((2, 4)),
        ],
        compiler_params=pltpu.CompilerParams(vmem_limit_bytes=58 << 20),
        cost_estimate=pl.CostEstimate(
            flops=4 * rows * depth * width, bytes_accessed=6 << 20, transcendentals=0
        ),
        name="project",
    )(core, att, out_own, out_peer)


def norm_kernel(
    core, hidden_hbm, near_hbm, far_hbm, gain_hbm, resid_hbm, normed_hbm,
    hidden, near, far, gain, normed, sems, out_sems,
):
    rows = near.shape[0]
    parts = 2
    block = rows // parts
    start = pl.multiple_of(core[0] * rows, rows)
    gain_copy = pltpu.make_async_copy(gain_hbm, gain, sems.at[3, 0])
    gain_copy.start()
    copies = []
    for i in range(parts):
        here = pl.ds(i * block, block)
        copies.append(
            [
                pltpu.make_async_copy(near_hbm.at[here], near.at[here], sems.at[0, i]),
                pltpu.make_async_copy(far_hbm.at[here], far.at[here], sems.at[1, i]),
                pltpu.make_async_copy(
                    hidden_hbm.at[pl.ds(start + i * block, block)], hidden.at[here], sems.at[2, i]
                ),
            ]
        )
        for copy in copies[i]:
            copy.start()
    gain_copy.wait()
    stores = []
    for i in range(parts):
        here = pl.ds(i * block, block)
        for copy in copies[i]:
            copy.wait()
        value = hidden[here, :].astype(F32) + (near[here, :] + far[here, :].astype(F32))
        mean_square = jnp.mean(value * value, axis=-1, keepdims=True)
        normed[here, :] = (value * lax.rsqrt(mean_square + 1e-06) * gain[...]).astype(BF)
        near[here, :] = value
        for j, (source, target) in enumerate(((normed, normed_hbm), (near, resid_hbm))):
            store = pltpu.make_async_copy(source.at[here], target.at[here], out_sems.at[j, i])
            store.start()
            stores.append(store)
    for store in stores:
        store.wait()


def add_and_norm(core, hidden, near, far, gain):
    rows, width = near.shape
    hbm = pl.BlockSpec(memory_space=pltpu.HBM)
    return pl.pallas_call(
        norm_kernel,
        out_shape=(
            jax.ShapeDtypeStruct((rows, width), F32),
            jax.ShapeDtypeStruct((rows, width), BF),
        ),
        in_specs=[pl.BlockSpec(memory_space=pltpu.SMEM), hbm, hbm, hbm, hbm],
        out_specs=(hbm, hbm),
        scratch_shapes=[
            pltpu.VMEM((rows, width), BF),
            pltpu.VMEM((rows, width), F32),
            pltpu.VMEM((rows, width), BF),
            pltpu.VMEM((1, width), F32),
            pltpu.VMEM((rows, width), BF),
            pltpu.SemaphoreType.DMA((4, 2)),
            pltpu.SemaphoreType.DMA((2, 2)),
        ],
        compiler_params=pltpu.CompilerParams(vmem_limit_bytes=58 << 20),
        cost_estimate=pl.CostEstimate(
            flops=8 * rows * width, bytes_accessed=4 << 20, transcendentals=rows
        ),
        name="add_and_norm",
    )(core, hidden, near, far, gain)


def gather_kernel(
    select_hbm, own_hbm, peer_hbm, out_hbm, select, rows, out, sems, out_sems
):
    half = rows.shape[0] // 2
    total, block = out.shape[0], out.shape[0] // 3
    copies = [
        pltpu.make_async_copy(own_hbm, rows.at[pl.ds(0, half)], sems.at[0]),
        pltpu.make_async_copy(peer_hbm, rows.at[pl.ds(half, half)], sems.at[1]),
        pltpu.make_async_copy(select_hbm, select, sems.at[2]),
    ]
    for copy in copies:
        copy.start()
    for copy in copies:
        copy.wait()
    stores = []
    for i in range(total // block):
        here = pl.ds(i * block, block)
        out[here, :] = jnp.dot(
            select[here, :], rows[...], preferred_element_type=F32
        ).astype(BF)
        store = pltpu.make_async_copy(out.at[here], out_hbm.at[here], out_sems.at[i])
        store.start()
        stores.append(store)
    for store in stores:
        store.wait()


def gather_rows(select, own, peer):
    slots, rows = select.shape
    width = own.shape[1]
    hbm = pl.BlockSpec(memory_space=pltpu.HBM)
    return pl.pallas_call(
        gather_kernel,
        out_shape=jax.ShapeDtypeStruct((slots, width), BF),
        in_specs=[hbm, hbm, hbm],
        out_specs=hbm,
        scratch_shapes=[
            pltpu.VMEM((slots, rows), BF),
            pltpu.VMEM((rows, width), BF),
            pltpu.VMEM((slots, width), BF),
            pltpu.SemaphoreType.DMA((3,)),
            pltpu.SemaphoreType.DMA((3,)),
        ],
        compiler_params=pltpu.CompilerParams(vmem_limit_bytes=58 << 20),
        cost_estimate=pl.CostEstimate(
            flops=2 * slots * rows * width, bytes_accessed=5 << 20, transcendentals=0
        ),
        name="gather_rows",
    )(select, own, peer)


def slot_weight_kernel(rank, weight, high):
    slots = high.shape[1]
    per_core = CAP // CORES
    experts_here = rank.shape[1]
    lane = lax.broadcasted_iota(jnp.int32, (1, slots), 1)
    expert_of = lax.rem(lax.div(lane, per_core), experts_here)
    wanted = lax.rem(lane, per_core) * CORES + lax.div(lane, per_core * experts_here)
    expand = (
        lax.broadcasted_iota(jnp.int32, (experts_here, slots), 0) == expert_of
    ).astype(BF)
    ranks = jnp.dot(rank[...].astype(BF), expand, preferred_element_type=F32)
    hit = ranks.astype(jnp.int32) == wanted
    spread = jnp.dot(weight[...].astype(BF), expand, preferred_element_type=F32)
    high[...] = jnp.where(hit, spread, 0.0).astype(BF)


def slot_weights(rank, weight, slots):
    rows = rank.shape[0]
    vmem = pl.BlockSpec(memory_space=pltpu.VMEM)
    shape = jax.ShapeDtypeStruct((rows, slots), BF)
    return pl.pallas_call(
        slot_weight_kernel,
        out_shape=shape,
        in_specs=[vmem, vmem],
        out_specs=vmem,
        compiler_params=pltpu.CompilerParams(vmem_limit_bytes=16 << 20),
        cost_estimate=pl.CostEstimate(
            flops=6 * rows * slots * 32, bytes_accessed=2 << 20, transcendentals=0
        ),
        name="slot_weights",
    )(rank, weight)


def expert_kernel(
    x_hbm, both_own, both_peer, down_own, down_peer, out_hbm,
    x, gate, up, down, act, out, x_sems, sems, down_sems, out_sems,
):
    hidden = both_own.shape[1]
    rows = x.shape[0]
    groups, _, width = out.shape
    parts = 3
    block = rows // parts
    step = 256
    bounds = [(lo, min(lo + step, 2 * hidden)) for lo in range(0, 2 * hidden, step)]
    x_copies = [
        pltpu.make_async_copy(
            x_hbm.at[pl.ds(m * block, block)], x.at[pl.ds(m * block, block)], x_sems.at[m]
        )
        for m in range(parts)
    ]
    chunks = []
    for n, (lo, hi) in enumerate(bounds):
        copies = []
        for j, (source, start, stop) in enumerate(
            (
                (both_own, lo, min(hi, hidden)),
                (both_peer, max(lo, hidden) - hidden, hi - hidden),
            )
        ):
            if stop <= start:
                continue
            shift = hidden * j
            for k, target in enumerate((gate, up)):
                copies.append(
                    pltpu.make_async_copy(
                        source.at[k, pl.ds(start, stop - start)],
                        target.at[pl.ds(start + shift, stop - start)],
                        sems.at[n, j, k],
                    )
                )
        chunks.append(copies)
    down_copies = [
        pltpu.make_async_copy(source, down.at[pl.ds(j * hidden, hidden)], down_sems.at[j])
        for j, source in enumerate((down_own, down_peer))
    ]
    def begin(copies):
        for copy in copies:
            copy.start()

    def finish(copies):
        for copy in copies:
            copy.wait()

    def halves(n, m):
        lo, hi = bounds[n]
        here = pl.ds(m * block, block)
        left = x[here, :]
        g = lax.dot_general(left, gate[lo:hi, :], contract, preferred_element_type=F32)
        u = lax.dot_general(left, up[lo:hi, :], contract, preferred_element_type=F32)
        act[here, lo:hi] = (g / (1.0 + jnp.exp(-g)) * u).astype(BF)

    contract = (((1,), (1,)), ((), ()))
    begin([x_copies[0]] + chunks[0])
    begin(x_copies[1:])
    finish([x_copies[0]] + chunks[0])
    begin(chunks[1])
    halves(0, 0)
    finish(x_copies[1:])
    begin(chunks[2])
    for m in range(1, parts):
        halves(0, m)
    finish(chunks[1])
    begin(down_copies)
    for m in range(parts):
        halves(1, m)
    finish(chunks[2])
    for m in range(parts):
        halves(2, m)
    finish(down_copies)
    stores = []
    for i in range(groups):
        for m in range(parts):
            here = pl.ds(m * block, block)
            result = jnp.dot(
                act[here, :], down[:, i * width : (i + 1) * width], preferred_element_type=F32
            )
            out[i, here, :] = result.astype(BF)
            store = pltpu.make_async_copy(
                out.at[i, here], out_hbm.at[i, here], out_sems.at[m, i]
            )
            store.start()
            stores.append(store)
    for store in stores:
        store.wait()


def experts(x, both_own, both_peer, down_own, down_peer, groups):
    rows, depth = x.shape
    hidden, width = down_own.shape
    column_width = width // groups
    hbm = pl.BlockSpec(memory_space=pltpu.HBM)
    return pl.pallas_call(
        expert_kernel,
        out_shape=jax.ShapeDtypeStruct((groups, rows, column_width), BF),
        in_specs=[hbm] * 5,
        out_specs=hbm,
        scratch_shapes=[
            pltpu.VMEM((rows, depth), BF),
            pltpu.VMEM((2 * hidden, depth), BF),
            pltpu.VMEM((2 * hidden, depth), BF),
            pltpu.VMEM((2 * hidden, width), BF),
            pltpu.VMEM((rows, 2 * hidden), BF),
            pltpu.VMEM((groups, rows, column_width), BF),
            pltpu.SemaphoreType.DMA((3,)),
            pltpu.SemaphoreType.DMA((pl.cdiv(2 * hidden, 256), 2, 2)),
            pltpu.SemaphoreType.DMA((2,)),
            pltpu.SemaphoreType.DMA((3, groups)),
        ],
        compiler_params=pltpu.CompilerParams(vmem_limit_bytes=60 << 20),
        cost_estimate=pl.CostEstimate(
            flops=12 * rows * depth * hidden,
            bytes_accessed=15 << 20,
            transcendentals=2 * rows * hidden,
        ),
        name="experts",
    )(x, both_own, both_peer, down_own, down_peer)


def combine_kernel(
    core, high_hbm, back_hbm, mine_hbm, peers_hbm, shared_hbm, out,
    high, back, mine, peers, shared, sems,
):
    rows = mine.shape[0]
    chips, depth = back.shape[0], back.shape[1]
    block = depth // CORES
    pieces = [(chip, pl.ds(c * block, block)) for chip in range(chips) for c in range(CORES)]
    copies = [
        pltpu.make_async_copy(back_hbm.at[chip, here], back.at[chip, here], sems.at[i])
        for i, (chip, here) in enumerate(pieces)
    ]
    rest = [
        pltpu.make_async_copy(source, target, sems.at[len(pieces) + i])
        for i, (source, target) in enumerate(
            (
                (high_hbm, high),
                (shared_hbm, shared),
                (mine_hbm, mine),
                (peers_hbm, peers),
            )
        )
    ]
    for copy in [rest[0]] + copies + rest[1:]:
        copy.start()
    total = None
    for i, (copy, (chip, here)) in enumerate(zip(copies, pieces)):
        if i == 0:
            rest[0].wait()
        copy.wait()
        part = jnp.dot(high[:, here], back[chip, here], preferred_element_type=F32)
        total = part if total is None else total + part
    for copy in rest[1:]:
        copy.wait()
    total += shared[...]
    first = core[0] == 0
    low_half = jnp.where(first, mine[...], peers[...])
    high_half = jnp.where(first, peers[...], mine[...])
    out[0:rows, :] = (total[0:rows] + low_half).astype(BF)
    out[rows : 2 * rows, :] = (total[rows:] + high_half).astype(BF)


def combine(core, high, returned, mine, peers, shared):
    hbm = pl.BlockSpec(memory_space=pltpu.HBM)
    vmem = pl.BlockSpec(memory_space=pltpu.VMEM)
    rows, width = shared.shape
    operands = (high, returned, mine, peers, shared)
    return pl.pallas_call(
        combine_kernel,
        out_shape=jax.ShapeDtypeStruct((rows, width), BF),
        in_specs=[pl.BlockSpec(memory_space=pltpu.SMEM)] + [hbm] * 5,
        out_specs=vmem,
        scratch_shapes=[pltpu.VMEM(o.shape, o.dtype) for o in operands]
        + [pltpu.SemaphoreType.DMA((8,))],
        compiler_params=pltpu.CompilerParams(vmem_limit_bytes=60 << 20),
        cost_estimate=pl.CostEstimate(
            flops=8 * rows * width * high.shape[1], bytes_accessed=7 << 20, transcendentals=0
        ),
        name="combine",
    )(core, *operands)


def page_pieces(keys, values, owner_all, tok_count, head_count, tok_index):
    pages_here = owner_all.shape[1]
    tok_rows = keys.shape[0]
    quarter_page = PAGE // head_count
    mine = lax.dynamic_index_in_dim(owner_all, tok_index, 0, keepdims=False)
    row = jnp.arange(tok_rows, dtype=jnp.int32)
    quarter = row // (tok_count * quarter_page)
    owner = row // quarter_page % tok_count
    line = quarter * quarter_page + row % quarter_page
    token_owner = jnp.repeat(mine, PAGE)
    token_line = jnp.arange(tok_rows, dtype=jnp.int32) % PAGE
    pick = (
        (owner[:, None] == token_owner[None, :]) & (line[:, None] == token_line[None, :])
    ).astype(BF)
    parts = [
        jnp.dot(pick, part, preferred_element_type=F32).astype(BF) for part in (keys, values)
    ]
    return jnp.concatenate(parts, 1).reshape(head_count * tok_count, quarter_page, -1)


def place_pages(landed, slots_all, owner_all, tok_count, head_count, tok_index):
    pages_here = owner_all.shape[1]
    quarter_page = PAGE // head_count
    rows = pages_here * quarter_page
    arrival = jnp.sum(jnp.where(owner_all == tok_index, slots_all % pages_here, 0), 1)
    row = jnp.arange(rows, dtype=jnp.int32)
    target = jnp.repeat(arrival, quarter_page) * quarter_page + row % quarter_page
    place = (row[:, None] == target[None, :]).astype(BF)
    landed = landed.reshape(head_count, rows, -1)
    width = landed.shape[2] // 2
    placed = [
        jnp.dot(place, landed[h], preferred_element_type=F32).astype(BF)
        for h in range(head_count)
    ]
    cache = jnp.concatenate(
        [p[:, :width] for p in placed] + [p[:, width:] for p in placed], 1
    )
    return cache.reshape(pages_here, quarter_page, 2 * head_count * width)


def per_device(
    hidden_in,
    queries,
    keys,
    values,
    request_ids,
    out_proj,
    norm_gain,
    expert_gate_up,
    expert_down,
    shared_gate_up,
    shared_down,
    shared_gate,
    routes,
    route_weights,
    page_slots,
):
    tok_rows, model_width = hidden_in.shape
    head_width = queries.shape[1]
    heads_here = head_width // HD
    tok_count = lax.axis_size("tok")
    head_count = lax.axis_size("head")
    tok_index = lax.axis_index("tok")
    head_index = lax.axis_index("head")
    core = head_index % CORES
    column_width = model_width // head_count
    rows_of_blocks = tok_count // ROW
    half = tok_rows // 2
    slots_core = CAP // CORES

    gate_up_own = jnp.transpose(expert_gate_up[0], (1, 2, 0))
    down_own = expert_down[0]
    out_peer = lax.ppermute(out_proj, "head", INTRA)
    gate_up_peer = lax.ppermute(gate_up_own, "head", INTRA)
    down_peer = lax.ppermute(down_own, "head", INTRA)

    packed = pack_heads(keys, values)
    row_groups = [[r * ROW + y for y in range(ROW)] for r in range(rows_of_blocks)]
    own = lax.all_to_all(
        packed, "tok", split_axis=0, concat_axis=0, tiled=True, axis_index_groups=row_groups
    )
    span = ROW * tok_rows
    base = (tok_index // ROW) * span
    padded_ids = jnp.concatenate([jnp.full((span,), -1, jnp.int32), request_ids], 0)
    window_ids = lax.dynamic_slice_in_dim(padded_ids, base, 2 * span, 0)
    ids_row = window_ids[None, :]
    queries, own = lax.optimization_barrier((queries, own))
    place_in_row = tok_index % ROW
    query_parts = []
    for step in range(ROW):
        target = (place_in_row + step) % ROW
        part = lax.dynamic_slice_in_dim(queries, target * HD, HD, 1)
        if step:
            part = lax.ppermute(
                part,
                "tok",
                [
                    (r * ROW + y, r * ROW + (y + step) % ROW)
                    for r in range(rows_of_blocks)
                    for y in range(ROW)
                ],
            )
        query_parts.append(part)
    slots_all = page_slots.reshape(tok_count, tok_rows // PAGE)
    owner_all = slots_all // (tok_rows // PAGE)
    pieces = page_pieces(keys, values, owner_all, tok_count, head_count, tok_index)
    past = lax.ppermute(
        own, "tok", [(s, s + ROW) for s in range(tok_count - ROW)]
    )
    attended = attention(
        place_in_row.reshape(1), ids_row, jnp.stack(query_parts, 0), own, past
    )

    core_groups = [
        [
            (chip * CORES + c) * tok_count + r * ROW + y
            for c in range(CORES)
            for y in range(ROW)
        ]
        for chip in range(CHIPS)
        for r in range(rows_of_blocks)
    ]
    gathered = lax.all_to_all(
        attended.reshape(CORES * ROW, half, HD),
        BOTH,
        split_axis=0,
        concat_axis=0,
        tiled=True,
        axis_index_groups=core_groups,
    ).reshape(CORES, ROW, half, HD)
    expert_ids = jnp.arange(EXPERTS, dtype=jnp.int32)
    named = routes[:, :, None] == expert_ids[None, None, :]
    onehot = jnp.sum(named.astype(F32), 1)
    weight_of = jnp.sum(jnp.where(named, route_weights[:, :, None], 0.0), 1)
    earlier = (
        jnp.arange(tok_rows, dtype=jnp.int32)[None, :] < jnp.arange(tok_rows, dtype=jnp.int32)[:, None]
    ).astype(BF)
    rank = jnp.dot(earlier, onehot.astype(BF), preferred_element_type=F32).astype(jnp.int32)
    rank = jnp.where(onehot > 0, rank, -1)
    rank_t = rank.T
    rank_rel = jnp.where(core == 0, rank_t, jnp.roll(rank_t, half, 1))
    place = jnp.arange(slots_core, dtype=jnp.int32) * CORES
    select = (rank_rel[:, None, :] == (place + core)[None, :, None]).astype(BF)
    select = select.reshape(EXPERTS * slots_core, tok_rows)
    core_ref = core.reshape(1)
    gathered, select, pieces = lax.optimization_barrier((gathered, select, pieces))
    projected, projected_low = project(core_ref, gathered, out_proj, out_peer)
    projected_far = lax.ppermute(projected_low, "head", CROSS)
    pieces, _ = lax.optimization_barrier((pieces, projected_low))
    landed = lax.all_to_all(pieces, BOTH, split_axis=0, concat_axis=0, tiled=True)
    projected_far, landed = lax.optimization_barrier((projected_far, landed))
    resid, normed_own = add_and_norm(
        core_ref, hidden_in, projected, projected_far, norm_gain[None, :]
    )
    normed_peer = lax.ppermute(normed_own, "head", INTRA)

    outgoing = gather_rows(select, normed_own, normed_peer)
    rank, weight_of, _ = lax.optimization_barrier((rank, weight_of, outgoing))
    high = slot_weights(rank, weight_of, CORES * EXPERTS * slots_core)
    late_own, late_peer, _ = lax.optimization_barrier((normed_own, normed_peer, outgoing))
    normed_abs = jnp.where(
        core == 0,
        jnp.concatenate([late_own, late_peer], 0),
        jnp.concatenate([late_peer, late_own], 0),
    )
    arrived = lax.all_to_all(
        outgoing.reshape(tok_count, slots_core, model_width),
        "tok",
        split_axis=0,
        concat_axis=0,
        tiled=True,
    ).reshape(tok_count * slots_core, model_width)
    shared_both = jnp.einsum("td,dgf->tgf", normed_abs, shared_gate_up, preferred_element_type=F32)
    shared_act = (jax.nn.silu(shared_both[:, 0, :]) * shared_both[:, 1, :]).astype(BF)
    shared_scale = jax.nn.sigmoid(jnp.dot(normed_abs, shared_gate, preferred_element_type=F32))
    shared_term = shared_scale[:, None] * jnp.dot(
        shared_act, shared_down, preferred_element_type=F32
    )
    chip = head_index // CORES
    chip_width = CORES * column_width
    shared_near = lax.dynamic_slice_in_dim(shared_term, chip * chip_width, chip_width, 1)
    shared_send = lax.dynamic_slice_in_dim(
        shared_term, (1 - chip) * chip_width, chip_width, 1
    ).astype(BF)
    shared_near, shared_send, arrived = lax.optimization_barrier(
        (shared_near, shared_send, arrived)
    )
    shared_far = lax.ppermute(shared_send, "head", CROSS)

    partial = experts(arrived, gate_up_own, gate_up_peer, down_own, down_peer, head_count)
    partial = partial.reshape(head_count * tok_count, slots_core, column_width)
    partial, shared_far = lax.optimization_barrier((partial, shared_far))
    returned = lax.all_to_all(partial, BOTH, split_axis=0, concat_axis=0, tiled=True)
    returned = returned.reshape(CHIPS, CORES * EXPERTS * slots_core, column_width)

    shared_chip = shared_near + shared_far.astype(F32)
    shared_own = lax.dynamic_slice_in_dim(shared_chip, core * column_width, column_width, 1)
    shared_peer = lax.dynamic_slice_in_dim(
        shared_chip, (1 - core) * column_width, column_width, 1
    ).astype(BF)
    shared_cols = shared_own + lax.ppermute(shared_peer, "head", INTRA).astype(F32)
    own_cols = lax.dynamic_slice_in_dim(resid, head_index * column_width, column_width, 1)
    peer_cols = lax.dynamic_slice_in_dim(
        resid, (head_index + 1 - 2 * core) * column_width, column_width, 1
    )
    from_peer = lax.ppermute(peer_cols, "head", INTRA)
    layer_out = combine(core_ref, high, returned, own_cols, from_peer, shared_cols)
    decode_cache = place_pages(landed, slots_all, owner_all, tok_count, head_count, tok_index)
    return (layer_out, decode_cache)


def solution(mesh):
    in_specs = (
        P("tok", None),
        P("tok", "head"),
        P("tok", "head"),
        P("tok", "head"),
        P(),
        P("head", None),
        P(),
        P("tok", None, None, "head"),
        P("tok", "head", None),
        P(None, None, "head"),
        P("head", None),
        P(),
        P("tok", None),
        P("tok", None),
        P(),
    )
    out_specs = (P("tok", "head"), P("tok", "head", None))
    return jax.shard_map(
        per_device, mesh=mesh, in_specs=in_specs, out_specs=out_specs, check_vma=False
    )
```

```python
import math

import jax
import jax.numpy as jnp
from jax import lax
from jax.experimental import pallas as pl
from jax.experimental.pallas import tpu as pltpu
from jax.sharding import PartitionSpec as P

HD = 128
TOP = 4
EXPERTS = 32
PAGE = 8
CAP = 48
ROW = 4
CORES = 2
CHIPS = 2
BF = jnp.bfloat16
F32 = jnp.float32
BOTH = ("head", "tok")
INTRA = [(0, 1), (1, 0), (2, 3), (3, 2)]
CROSS = [(0, 2), (2, 0), (1, 3), (3, 1)]


def pack_kernel(keys, values, out):
    for i in range(out.shape[0]):
        here = pl.ds(i * HD, HD)
        out[i, :, 0:HD] = keys[:, here]
        out[i, :, HD : 2 * HD] = values[:, here]


def pack_heads(keys, values):
    rows, width = keys.shape
    vmem = pl.BlockSpec(memory_space=pltpu.VMEM)
    heads = width // HD
    return pl.pallas_call(
        pack_kernel,
        out_shape=jax.ShapeDtypeStruct((heads, rows, 2 * HD), BF),
        in_specs=[vmem, vmem],
        out_specs=vmem,
        compiler_params=pltpu.CompilerParams(vmem_limit_bytes=60 << 20),
        cost_estimate=pl.CostEstimate(flops=0, bytes_accessed=1 << 20, transcendentals=0),
        name="pack_heads",
    )(keys, values)


def attention_kernel(
    place, ids_row_hbm, query_hbm, own_hbm, past_hbm, out_hbm,
    ids_row, query_parts, own, past, out, sems, out_sems,
):
    block = out.shape[2] * 2
    pairs = (
        (query_hbm, query_parts),
        (own_hbm, own),
        (past_hbm, past),
        (ids_row_hbm, ids_row),
    )
    copies = [
        pltpu.make_async_copy(source, target, sems.at[i])
        for i, (source, target) in enumerate(pairs)
    ]
    for copy in copies:
        copy.start()
    for copy in copies:
        copy.wait()
    stores = []
    scale = 1.0 / math.sqrt(HD)
    span = ROW * block
    row_pos = lax.broadcasted_iota(jnp.int32, (block, block), 0)
    col_pos = lax.broadcasted_iota(jnp.int32, (block, block), 1)
    causal = col_pos <= row_pos
    same = col_pos == row_pos
    for y in range(ROW):
        query = query_parts[lax.rem(place[0] + (ROW - y), ROW)]
        row_ids = ids_row[0:1, pl.ds(span + y * block, block)]
        query_ids = jnp.sum(jnp.where(same, row_ids, 0), axis=1, keepdims=True)
        pieces = []
        for b in range(y, ROW):
            key = past[b, :, 0:HD]
            key_ids = ids_row[0:1, pl.ds(b * block, block)]
            score = lax.dot_general(
                query, key, (((1,), (1,)), ((), ())), preferred_element_type=F32
            )
            pieces.append(jnp.where(query_ids == key_ids, score, -1e30))
        for b in range(y + 1):
            key = own[b, :, 0:HD]
            key_ids = ids_row[0:1, pl.ds(span + b * block, block)]
            score = lax.dot_general(
                query, key, (((1,), (1,)), ((), ())), preferred_element_type=F32
            )
            allowed = query_ids == key_ids
            if b == y:
                allowed = allowed & causal
            pieces.append(jnp.where(allowed, score, -1e30))
        top = pieces[0].max(-1, keepdims=True)
        for piece in pieces[1:]:
            top = jnp.maximum(top, piece.max(-1, keepdims=True))
        weights = [jnp.exp((piece - top) * scale) for piece in pieces]
        total = weights[0].sum(-1, keepdims=True)
        for weight in weights[1:]:
            total = total + weight.sum(-1, keepdims=True)
        inverse = 1.0 / total
        mixed = jnp.zeros((block, HD), F32)
        index = 0
        for b in range(y, ROW):
            prob = weights[index].astype(BF)
            mixed += jnp.dot(prob, past[b, :, HD : 2 * HD], preferred_element_type=F32)
            index += 1
        for b in range(y + 1):
            prob = weights[index].astype(BF)
            mixed += jnp.dot(prob, own[b, :, HD : 2 * HD], preferred_element_type=F32)
            index += 1
        mixed = mixed * inverse
        half = block // 2
        out[0, y] = mixed[:half].astype(BF)
        out[1, y] = mixed[half:].astype(BF)
        for c in range(2):
            store = pltpu.make_async_copy(out.at[c, y], out_hbm.at[c, y], out_sems.at[c, y])
            store.start()
            stores.append(store)
    for store in stores:
        store.wait()


def attention(place, ids_row, query_parts, own, past):
    block = own.shape[1]
    hbm = pl.BlockSpec(memory_space=pltpu.HBM)
    operands = (ids_row, query_parts, own, past)
    result = jax.ShapeDtypeStruct((2, ROW, block // 2, HD), BF)
    return pl.pallas_call(
        attention_kernel,
        out_shape=result,
        in_specs=[pl.BlockSpec(memory_space=pltpu.SMEM)] + [hbm] * 4,
        out_specs=hbm,
        scratch_shapes=[pltpu.VMEM(o.shape, o.dtype) for o in operands]
        + [
            pltpu.VMEM(result.shape, BF),
            pltpu.SemaphoreType.DMA((4,)),
            pltpu.SemaphoreType.DMA((2, ROW)),
        ],
        compiler_params=pltpu.CompilerParams(vmem_limit_bytes=58 << 20),
        cost_estimate=pl.CostEstimate(
            flops=4 * 5 * ROW * block * block * HD,
            bytes_accessed=3 << 20,
            transcendentals=5 * ROW * block * block,
        ),
        name="row_attention",
    )(place, *operands)


def project_kernel(
    core, att_hbm, own_hbm, peer_hbm, low_hbm, att, own, peer, total_low, att_sem, sems, out_sems,
):
    width = total_low.shape[1]
    step = width // 4
    att_copy = pltpu.make_async_copy(att_hbm, att, att_sem)
    att_copy.start()
    copies = []
    for i in range(4):
        cols = pl.ds(i * step, step)
        copies.append(
            (
                pltpu.make_async_copy(own_hbm.at[:, cols], own.at[:, cols], sems.at[0, i]),
                pltpu.make_async_copy(peer_hbm.at[:, cols], peer.at[:, cols], sems.at[1, i]),
            )
        )
    for pair in copies:
        for copy in pair:
            copy.start()
    att_copy.wait()
    c = core[0]
    stores = []
    left = jnp.concatenate([att[c, y] for y in range(ROW)], 1)
    right = jnp.concatenate([att[1 - c, y] for y in range(ROW)], 1)
    for i in range(4):
        cols = pl.ds(i * step, step)
        for copy in copies[i]:
            copy.wait()
        part = jnp.dot(left, own[:, cols], preferred_element_type=F32) + jnp.dot(
            right, peer[:, cols], preferred_element_type=F32
        )
        total_low[:, cols] = part.astype(BF)
        store = pltpu.make_async_copy(total_low.at[:, cols], low_hbm.at[:, cols], out_sems.at[i])
        store.start()
        stores.append(store)
    for store in stores:
        store.wait()


def project(core, att, out_own, out_peer):
    rows = att.shape[2]
    depth, width = out_own.shape
    hbm = pl.BlockSpec(memory_space=pltpu.HBM)
    return pl.pallas_call(
        project_kernel,
        out_shape=jax.ShapeDtypeStruct((rows, width), BF),
        in_specs=[pl.BlockSpec(memory_space=pltpu.SMEM), hbm, hbm, hbm],
        out_specs=hbm,
        scratch_shapes=[
            pltpu.VMEM(att.shape, BF),
            pltpu.VMEM((depth, width), BF),
            pltpu.VMEM((depth, width), BF),
            pltpu.VMEM((rows, width), BF),
            pltpu.SemaphoreType.DMA,
            pltpu.SemaphoreType.DMA((2, 4)),
            pltpu.SemaphoreType.DMA((4,)),
        ],
        compiler_params=pltpu.CompilerParams(vmem_limit_bytes=58 << 20),
        cost_estimate=pl.CostEstimate(
            flops=4 * rows * depth * width, bytes_accessed=6 << 20, transcendentals=0
        ),
        name="project",
    )(core, att, out_own, out_peer)


def norm_kernel(
    core, hidden_hbm, near_hbm, far_hbm, gain_hbm, resid_hbm, normed_hbm,
    hidden, near, far, gain, resid, normed, sems, out_sems,
):
    rows = near.shape[0]
    parts = 2
    block = rows // parts
    start = pl.multiple_of(core[0] * rows, rows)
    gain_copy = pltpu.make_async_copy(gain_hbm, gain, sems.at[3, 0])
    gain_copy.start()
    copies = []
    for i in range(parts):
        here = pl.ds(i * block, block)
        copies.append(
            [
                pltpu.make_async_copy(near_hbm.at[here], near.at[here], sems.at[0, i]),
                pltpu.make_async_copy(far_hbm.at[here], far.at[here], sems.at[1, i]),
                pltpu.make_async_copy(
                    hidden_hbm.at[pl.ds(start + i * block, block)], hidden.at[here], sems.at[2, i]
                ),
            ]
        )
        for copy in copies[i]:
            copy.start()
    gain_copy.wait()
    stores = []
    for i in range(parts):
        here = pl.ds(i * block, block)
        for copy in copies[i]:
            copy.wait()
        value = hidden[here, :].astype(F32) + (
            near[here, :].astype(F32) + far[here, :].astype(F32)
        )
        mean_square = jnp.mean(value * value, axis=-1, keepdims=True)
        normed[here, :] = (value * lax.rsqrt(mean_square + 1e-06) * gain[...]).astype(BF)
        resid[here, :] = value
        for j, (source, target) in enumerate(((normed, normed_hbm), (resid, resid_hbm))):
            store = pltpu.make_async_copy(source.at[here], target.at[here], out_sems.at[j, i])
            store.start()
            stores.append(store)
    for store in stores:
        store.wait()


def add_and_norm(core, hidden, near, far, gain):
    rows, width = near.shape
    hbm = pl.BlockSpec(memory_space=pltpu.HBM)
    return pl.pallas_call(
        norm_kernel,
        out_shape=(
            jax.ShapeDtypeStruct((rows, width), F32),
            jax.ShapeDtypeStruct((rows, width), BF),
        ),
        in_specs=[pl.BlockSpec(memory_space=pltpu.SMEM), hbm, hbm, hbm, hbm],
        out_specs=(hbm, hbm),
        scratch_shapes=[
            pltpu.VMEM((rows, width), BF),
            pltpu.VMEM((rows, width), BF),
            pltpu.VMEM((rows, width), BF),
            pltpu.VMEM((1, width), F32),
            pltpu.VMEM((rows, width), F32),
            pltpu.VMEM((rows, width), BF),
            pltpu.SemaphoreType.DMA((4, 2)),
            pltpu.SemaphoreType.DMA((2, 2)),
        ],
        compiler_params=pltpu.CompilerParams(vmem_limit_bytes=58 << 20),
        cost_estimate=pl.CostEstimate(
            flops=8 * rows * width, bytes_accessed=4 << 20, transcendentals=rows
        ),
        name="add_and_norm",
    )(core, hidden, near, far, gain)


def gather_kernel(
    select_hbm, own_hbm, peer_hbm, out_hbm, select, rows, out, sems, out_sems
):
    half = rows.shape[0] // 2
    total, block = out.shape[0], out.shape[0] // 3
    copies = [
        pltpu.make_async_copy(own_hbm, rows.at[pl.ds(0, half)], sems.at[0]),
        pltpu.make_async_copy(peer_hbm, rows.at[pl.ds(half, half)], sems.at[1]),
        pltpu.make_async_copy(select_hbm, select, sems.at[2]),
    ]
    for copy in copies:
        copy.start()
    for copy in copies:
        copy.wait()
    stores = []
    for i in range(total // block):
        here = pl.ds(i * block, block)
        out[here, :] = jnp.dot(
            select[here, :], rows[...], preferred_element_type=F32
        ).astype(BF)
        store = pltpu.make_async_copy(out.at[here], out_hbm.at[here], out_sems.at[i])
        store.start()
        stores.append(store)
    for store in stores:
        store.wait()


def gather_rows(select, own, peer):
    slots, rows = select.shape
    width = own.shape[1]
    hbm = pl.BlockSpec(memory_space=pltpu.HBM)
    return pl.pallas_call(
        gather_kernel,
        out_shape=jax.ShapeDtypeStruct((slots, width), BF),
        in_specs=[hbm, hbm, hbm],
        out_specs=hbm,
        scratch_shapes=[
            pltpu.VMEM((slots, rows), BF),
            pltpu.VMEM((rows, width), BF),
            pltpu.VMEM((slots, width), BF),
            pltpu.SemaphoreType.DMA((3,)),
            pltpu.SemaphoreType.DMA((3,)),
        ],
        compiler_params=pltpu.CompilerParams(vmem_limit_bytes=58 << 20),
        cost_estimate=pl.CostEstimate(
            flops=2 * slots * rows * width, bytes_accessed=5 << 20, transcendentals=0
        ),
        name="gather_rows",
    )(select, own, peer)


def slot_weight_kernel(rank, weight, high):
    slots = high.shape[1]
    per_core = CAP // CORES
    experts_here = rank.shape[1]
    lane = lax.broadcasted_iota(jnp.int32, (1, slots), 1)
    expert_of = lax.rem(lax.div(lane, per_core), experts_here)
    wanted = lax.rem(lane, per_core) * CORES + lax.div(lane, per_core * experts_here)
    expand = (
        lax.broadcasted_iota(jnp.int32, (experts_here, slots), 0) == expert_of
    ).astype(BF)
    ranks = jnp.dot(rank[...].astype(BF), expand, preferred_element_type=F32)
    hit = ranks.astype(jnp.int32) == wanted
    spread = jnp.dot(weight[...].astype(BF), expand, preferred_element_type=F32)
    high[...] = jnp.where(hit, spread, 0.0).astype(BF)


def slot_weights(rank, weight, slots):
    rows = rank.shape[0]
    vmem = pl.BlockSpec(memory_space=pltpu.VMEM)
    shape = jax.ShapeDtypeStruct((rows, slots), BF)
    return pl.pallas_call(
        slot_weight_kernel,
        out_shape=shape,
        in_specs=[vmem, vmem],
        out_specs=vmem,
        compiler_params=pltpu.CompilerParams(vmem_limit_bytes=16 << 20),
        cost_estimate=pl.CostEstimate(
            flops=6 * rows * slots * 32, bytes_accessed=2 << 20, transcendentals=0
        ),
        name="slot_weights",
    )(rank, weight)


def expert_kernel(
    x_hbm, both_own, both_peer, down_own, down_peer, out_hbm,
    x, gate, up, down, act, out, x_sems, sems, down_sems, out_sems,
):
    hidden = both_own.shape[1]
    rows = x.shape[0]
    groups, _, width = out.shape
    parts = 3
    block = rows // parts
    step = 256
    bounds = [(lo, min(lo + step, 2 * hidden)) for lo in range(0, 2 * hidden, step)]
    x_copies = [
        pltpu.make_async_copy(
            x_hbm.at[pl.ds(m * block, block)], x.at[pl.ds(m * block, block)], x_sems.at[m]
        )
        for m in range(parts)
    ]
    chunks = []
    for n, (lo, hi) in enumerate(bounds):
        copies = []
        for j, (source, start, stop) in enumerate(
            (
                (both_own, lo, min(hi, hidden)),
                (both_peer, max(lo, hidden) - hidden, hi - hidden),
            )
        ):
            if stop <= start:
                continue
            shift = hidden * j
            for k, target in enumerate((gate, up)):
                copies.append(
                    pltpu.make_async_copy(
                        source.at[k, pl.ds(start, stop - start)],
                        target.at[pl.ds(start + shift, stop - start)],
                        sems.at[n, j, k],
                    )
                )
        chunks.append(copies)
    down_copies = [
        pltpu.make_async_copy(source, down.at[pl.ds(j * hidden, hidden)], down_sems.at[j])
        for j, source in enumerate((down_own, down_peer))
    ]
    def begin(copies):
        for copy in copies:
            copy.start()

    def finish(copies):
        for copy in copies:
            copy.wait()

    def halves(n, start, count):
        lo, hi = bounds[n]
        here = pl.ds(start * block, count * block)
        left = x[here, :]
        g = lax.dot_general(left, gate[lo:hi, :], contract, preferred_element_type=F32)
        u = lax.dot_general(left, up[lo:hi, :], contract, preferred_element_type=F32)
        act[here, lo:hi] = (g / (1.0 + jnp.exp(-g)) * u).astype(BF)

    contract = (((1,), (1,)), ((), ()))
    begin([x_copies[0]] + chunks[0])
    begin(x_copies[1:])
    finish([x_copies[0]] + chunks[0])
    begin(chunks[1])
    halves(0, 0, 1)
    finish(x_copies[1:])
    begin(chunks[2])
    halves(0, 1, parts - 1)
    finish(chunks[1])
    begin(down_copies)
    halves(1, 0, parts)
    finish(chunks[2])
    halves(2, 0, parts)
    finish(down_copies)
    stores = []
    for i in range(groups):
        result = jnp.dot(
            act[...], down[:, i * width : (i + 1) * width], preferred_element_type=F32
        )
        out[i] = result.astype(BF)
        store = pltpu.make_async_copy(out.at[i], out_hbm.at[i], out_sems.at[i])
        store.start()
        stores.append(store)
    for store in stores:
        store.wait()


def experts(x, both_own, both_peer, down_own, down_peer, groups):
    rows, depth = x.shape
    hidden, width = down_own.shape
    column_width = width // groups
    hbm = pl.BlockSpec(memory_space=pltpu.HBM)
    return pl.pallas_call(
        expert_kernel,
        out_shape=jax.ShapeDtypeStruct((groups, rows, column_width), BF),
        in_specs=[hbm] * 5,
        out_specs=hbm,
        scratch_shapes=[
            pltpu.VMEM((rows, depth), BF),
            pltpu.VMEM((2 * hidden, depth), BF),
            pltpu.VMEM((2 * hidden, depth), BF),
            pltpu.VMEM((2 * hidden, width), BF),
            pltpu.VMEM((rows, 2 * hidden), BF),
            pltpu.VMEM((groups, rows, column_width), BF),
            pltpu.SemaphoreType.DMA((3,)),
            pltpu.SemaphoreType.DMA((pl.cdiv(2 * hidden, 256), 2, 2)),
            pltpu.SemaphoreType.DMA((2,)),
            pltpu.SemaphoreType.DMA((groups,)),
        ],
        compiler_params=pltpu.CompilerParams(vmem_limit_bytes=60 << 20),
        cost_estimate=pl.CostEstimate(
            flops=12 * rows * depth * hidden,
            bytes_accessed=15 << 20,
            transcendentals=2 * rows * hidden,
        ),
        name="experts",
    )(x, both_own, both_peer, down_own, down_peer)


def combine_kernel(
    core, high_hbm, back_hbm, mine_hbm, peers_hbm, shared_hbm, out,
    high, back, mine, peers, shared, sems,
):
    rows = mine.shape[0]
    chips, depth = back.shape[0], back.shape[1]
    block = depth // CORES
    pieces = [(chip, pl.ds(c * block, block)) for chip in range(chips) for c in range(CORES)]
    copies = [
        pltpu.make_async_copy(back_hbm.at[chip, here], back.at[chip, here], sems.at[i])
        for i, (chip, here) in enumerate(pieces)
    ]
    rest = [
        pltpu.make_async_copy(source, target, sems.at[len(pieces) + i])
        for i, (source, target) in enumerate(
            (
                (high_hbm, high),
                (shared_hbm, shared),
                (mine_hbm, mine),
                (peers_hbm, peers),
            )
        )
    ]
    for copy in [rest[0]] + copies + rest[1:]:
        copy.start()
    total = None
    for i, (copy, (chip, here)) in enumerate(zip(copies, pieces)):
        if i == 0:
            rest[0].wait()
        copy.wait()
        part = jnp.dot(high[:, here], back[chip, here], preferred_element_type=F32)
        total = part if total is None else total + part
    for copy in rest[1:]:
        copy.wait()
    total += shared[...]
    first = core[0] == 0
    low_half = jnp.where(first, mine[...], peers[...])
    high_half = jnp.where(first, peers[...], mine[...])
    out[0:rows, :] = (total[0:rows] + low_half).astype(BF)
    out[rows : 2 * rows, :] = (total[rows:] + high_half).astype(BF)


def combine(core, high, returned, mine, peers, shared):
    hbm = pl.BlockSpec(memory_space=pltpu.HBM)
    vmem = pl.BlockSpec(memory_space=pltpu.VMEM)
    rows, width = shared.shape
    operands = (high, returned, mine, peers, shared)
    return pl.pallas_call(
        combine_kernel,
        out_shape=jax.ShapeDtypeStruct((rows, width), BF),
        in_specs=[pl.BlockSpec(memory_space=pltpu.SMEM)] + [hbm] * 5,
        out_specs=vmem,
        scratch_shapes=[pltpu.VMEM(o.shape, o.dtype) for o in operands]
        + [pltpu.SemaphoreType.DMA((8,))],
        compiler_params=pltpu.CompilerParams(vmem_limit_bytes=60 << 20),
        cost_estimate=pl.CostEstimate(
            flops=8 * rows * width * high.shape[1], bytes_accessed=7 << 20, transcendentals=0
        ),
        name="combine",
    )(core, *operands)


def page_pieces(keys, values, owner_all, tok_count, head_count, tok_index):
    pages_here = owner_all.shape[1]
    tok_rows = keys.shape[0]
    quarter_page = PAGE // head_count
    mine = lax.dynamic_index_in_dim(owner_all, tok_index, 0, keepdims=False)
    row = jnp.arange(tok_rows, dtype=jnp.int32)
    quarter = row // (tok_count * quarter_page)
    owner = row // quarter_page % tok_count
    line = quarter * quarter_page + row % quarter_page
    token_owner = jnp.repeat(mine, PAGE)
    token_line = jnp.arange(tok_rows, dtype=jnp.int32) % PAGE
    pick = (
        (owner[:, None] == token_owner[None, :]) & (line[:, None] == token_line[None, :])
    ).astype(BF)
    parts = [
        jnp.dot(pick, part, preferred_element_type=F32).astype(BF) for part in (keys, values)
    ]
    return jnp.concatenate(parts, 1).reshape(head_count * tok_count, quarter_page, -1)


def place_pages(landed, slots_all, owner_all, tok_count, head_count, tok_index):
    pages_here = owner_all.shape[1]
    quarter_page = PAGE // head_count
    rows = pages_here * quarter_page
    arrival = jnp.sum(jnp.where(owner_all == tok_index, slots_all % pages_here, 0), 1)
    row = jnp.arange(rows, dtype=jnp.int32)
    target = jnp.repeat(arrival, quarter_page) * quarter_page + row % quarter_page
    place = (row[:, None] == target[None, :]).astype(BF)
    landed = landed.reshape(head_count, rows, -1)
    width = landed.shape[2] // 2
    placed = [
        jnp.dot(place, landed[h], preferred_element_type=F32).astype(BF)
        for h in range(head_count)
    ]
    cache = jnp.concatenate(
        [p[:, :width] for p in placed] + [p[:, width:] for p in placed], 1
    )
    return cache.reshape(pages_here, quarter_page, 2 * head_count * width)


def per_device(
    hidden_in,
    queries,
    keys,
    values,
    request_ids,
    out_proj,
    norm_gain,
    expert_gate_up,
    expert_down,
    shared_gate_up,
    shared_down,
    shared_gate,
    routes,
    route_weights,
    page_slots,
):
    tok_rows, model_width = hidden_in.shape
    head_width = queries.shape[1]
    heads_here = head_width // HD
    tok_count = lax.axis_size("tok")
    head_count = lax.axis_size("head")
    tok_index = lax.axis_index("tok")
    head_index = lax.axis_index("head")
    core = head_index % CORES
    column_width = model_width // head_count
    rows_of_blocks = tok_count // ROW
    half = tok_rows // 2
    slots_core = CAP // CORES

    gate_up_own = jnp.transpose(expert_gate_up[0], (1, 2, 0))
    down_own = expert_down[0]
    out_peer = lax.ppermute(out_proj, "head", INTRA)
    gate_up_peer = lax.ppermute(gate_up_own, "head", INTRA)
    down_peer = lax.ppermute(down_own, "head", INTRA)

    packed = pack_heads(keys, values)
    row_groups = [[r * ROW + y for y in range(ROW)] for r in range(rows_of_blocks)]
    own = lax.all_to_all(
        packed, "tok", split_axis=0, concat_axis=0, tiled=True, axis_index_groups=row_groups
    )
    span = ROW * tok_rows
    base = (tok_index // ROW) * span
    padded_ids = jnp.concatenate([jnp.full((span,), -1, jnp.int32), request_ids], 0)
    window_ids = lax.dynamic_slice_in_dim(padded_ids, base, 2 * span, 0)
    ids_row = window_ids[None, :]
    queries, own = lax.optimization_barrier((queries, own))
    place_in_row = tok_index % ROW
    query_parts = []
    for step in range(ROW):
        target = (place_in_row + step) % ROW
        part = lax.dynamic_slice_in_dim(queries, target * HD, HD, 1)
        if step:
            part = lax.ppermute(
                part,
                "tok",
                [
                    (r * ROW + y, r * ROW + (y + step) % ROW)
                    for r in range(rows_of_blocks)
                    for y in range(ROW)
                ],
            )
        query_parts.append(part)
    slots_all = page_slots.reshape(tok_count, tok_rows // PAGE)
    owner_all = slots_all // (tok_rows // PAGE)
    pieces = page_pieces(keys, values, owner_all, tok_count, head_count, tok_index)
    past = lax.ppermute(
        own, "tok", [(s, s + ROW) for s in range(tok_count - ROW)]
    )
    attended = attention(
        place_in_row.reshape(1), ids_row, jnp.stack(query_parts, 0), own, past
    )

    core_groups = [
        [
            (chip * CORES + c) * tok_count + r * ROW + y
            for c in range(CORES)
            for y in range(ROW)
        ]
        for chip in range(CHIPS)
        for r in range(rows_of_blocks)
    ]
    gathered = lax.all_to_all(
        attended.reshape(CORES * ROW, half, HD),
        BOTH,
        split_axis=0,
        concat_axis=0,
        tiled=True,
        axis_index_groups=core_groups,
    ).reshape(CORES, ROW, half, HD)
    expert_ids = jnp.arange(EXPERTS, dtype=jnp.int32)
    named = routes[:, :, None] == expert_ids[None, None, :]
    onehot = jnp.sum(named.astype(F32), 1)
    weight_of = jnp.sum(jnp.where(named, route_weights[:, :, None], 0.0), 1)
    earlier = (
        jnp.arange(tok_rows, dtype=jnp.int32)[None, :] < jnp.arange(tok_rows, dtype=jnp.int32)[:, None]
    ).astype(BF)
    rank = jnp.dot(earlier, onehot.astype(BF), preferred_element_type=F32).astype(jnp.int32)
    rank = jnp.where(onehot > 0, rank, -1)
    rank_t = rank.T
    rank_rel = jnp.where(core == 0, rank_t, jnp.roll(rank_t, half, 1))
    place = jnp.arange(slots_core, dtype=jnp.int32) * CORES
    select = (rank_rel[:, None, :] == (place + core)[None, :, None]).astype(BF)
    select = select.reshape(EXPERTS * slots_core, tok_rows)
    core_ref = core.reshape(1)
    gathered, select, pieces = lax.optimization_barrier((gathered, select, pieces))
    projected_low = project(core_ref, gathered, out_proj, out_peer)
    projected_far = lax.ppermute(projected_low, "head", CROSS)
    pieces, _ = lax.optimization_barrier((pieces, projected_low))
    landed = lax.all_to_all(pieces, BOTH, split_axis=0, concat_axis=0, tiled=True)
    resid, normed_own = add_and_norm(
        core_ref, hidden_in, projected_low, projected_far, norm_gain[None, :]
    )
    normed_own, landed = lax.optimization_barrier((normed_own, landed))
    normed_peer = lax.ppermute(normed_own, "head", INTRA)

    outgoing = gather_rows(select, normed_own, normed_peer)
    rank, weight_of, _ = lax.optimization_barrier((rank, weight_of, outgoing))
    high = slot_weights(rank, weight_of, CORES * EXPERTS * slots_core)
    late_own, late_peer, _ = lax.optimization_barrier((normed_own, normed_peer, outgoing))
    normed_abs = jnp.where(
        core == 0,
        jnp.concatenate([late_own, late_peer], 0),
        jnp.concatenate([late_peer, late_own], 0),
    )
    arrived = lax.all_to_all(
        outgoing.reshape(tok_count, slots_core, model_width),
        "tok",
        split_axis=0,
        concat_axis=0,
        tiled=True,
    ).reshape(tok_count * slots_core, model_width)
    shared_both = jnp.einsum("td,dgf->tgf", normed_abs, shared_gate_up, preferred_element_type=F32)
    shared_act = (jax.nn.silu(shared_both[:, 0, :]) * shared_both[:, 1, :]).astype(BF)
    shared_scale = jax.nn.sigmoid(jnp.dot(normed_abs, shared_gate, preferred_element_type=F32))
    shared_term = shared_scale[:, None] * jnp.dot(
        shared_act, shared_down, preferred_element_type=F32
    )
    chip = head_index // CORES
    chip_width = CORES * column_width
    shared_near = lax.dynamic_slice_in_dim(shared_term, chip * chip_width, chip_width, 1)
    shared_send = lax.dynamic_slice_in_dim(
        shared_term, (1 - chip) * chip_width, chip_width, 1
    ).astype(BF)
    shared_near, shared_send, arrived = lax.optimization_barrier(
        (shared_near, shared_send, arrived)
    )
    shared_far = lax.ppermute(shared_send, "head", CROSS)

    partial = experts(arrived, gate_up_own, gate_up_peer, down_own, down_peer, head_count)
    partial = partial.reshape(head_count * tok_count, slots_core, column_width)
    partial, shared_far = lax.optimization_barrier((partial, shared_far))
    returned = lax.all_to_all(partial, BOTH, split_axis=0, concat_axis=0, tiled=True)
    returned = returned.reshape(CHIPS, CORES * EXPERTS * slots_core, column_width)

    shared_chip = shared_near + shared_far.astype(F32)
    shared_own = lax.dynamic_slice_in_dim(shared_chip, core * column_width, column_width, 1)
    shared_peer = lax.dynamic_slice_in_dim(
        shared_chip, (1 - core) * column_width, column_width, 1
    ).astype(BF)
    shared_cols = shared_own + lax.ppermute(shared_peer, "head", INTRA).astype(F32)
    own_cols = lax.dynamic_slice_in_dim(resid, head_index * column_width, column_width, 1)
    peer_cols = lax.dynamic_slice_in_dim(
        resid, (head_index + 1 - 2 * core) * column_width, column_width, 1
    )
    from_peer = lax.ppermute(peer_cols, "head", INTRA)
    layer_out = combine(core_ref, high, returned, own_cols, from_peer, shared_cols)
    decode_cache = place_pages(landed, slots_all, owner_all, tok_count, head_count, tok_index)
    return (layer_out, decode_cache)


def solution(mesh):
    in_specs = (
        P("tok", None),
        P("tok", "head"),
        P("tok", "head"),
        P("tok", "head"),
        P(),
        P("head", None),
        P(),
        P("tok", None, None, "head"),
        P("tok", "head", None),
        P(None, None, "head"),
        P("head", None),
        P(),
        P("tok", None),
        P("tok", None),
        P(),
    )
    out_specs = (P("tok", "head"), P("tok", "head", None))
    return jax.shard_map(
        per_device, mesh=mesh, in_specs=in_specs, out_specs=out_specs, check_vma=False
    )
```

```python
import math

import jax
import jax.numpy as jnp
from jax import lax
from jax.experimental import pallas as pl
from jax.experimental.pallas import tpu as pltpu
from jax.sharding import PartitionSpec as P

HD = 128
TOP = 4
EXPERTS = 32
PAGE = 8
CAP = 48
ROW = 4
CORES = 2
CHIPS = 2
BF = jnp.bfloat16
F32 = jnp.float32
BOTH = ("head", "tok")
INTRA = [(0, 1), (1, 0), (2, 3), (3, 2)]
CROSS = [(0, 2), (2, 0), (1, 3), (3, 1)]


def pack_kernel(keys, values, out):
    for i in range(out.shape[0]):
        here = pl.ds(i * HD, HD)
        out[i, :, 0:HD] = keys[:, here]
        out[i, :, HD : 2 * HD] = values[:, here]


def pack_heads(keys, values):
    rows, width = keys.shape
    vmem = pl.BlockSpec(memory_space=pltpu.VMEM)
    heads = width // HD
    return pl.pallas_call(
        pack_kernel,
        out_shape=jax.ShapeDtypeStruct((heads, rows, 2 * HD), BF),
        in_specs=[vmem, vmem],
        out_specs=vmem,
        compiler_params=pltpu.CompilerParams(vmem_limit_bytes=60 << 20),
        cost_estimate=pl.CostEstimate(flops=0, bytes_accessed=1 << 20, transcendentals=0),
        name="pack_heads",
    )(keys, values)


def attention_kernel(
    place, ids_row_hbm, query_hbm, own_hbm, past_hbm, out_hbm,
    ids_row, query_parts, own, past, out, sems, out_sems,
):
    block = out.shape[2] * 2
    pairs = (
        (query_hbm, query_parts),
        (own_hbm, own),
        (past_hbm, past),
        (ids_row_hbm, ids_row),
    )
    copies = [
        pltpu.make_async_copy(source, target, sems.at[i])
        for i, (source, target) in enumerate(pairs)
    ]
    for copy in copies:
        copy.start()
    for copy in copies[:2] + copies[3:]:
        copy.wait()
    stores = []
    scale = 1.0 / math.sqrt(HD)
    span = ROW * block
    row_pos = lax.broadcasted_iota(jnp.int32, (block, block), 0)
    col_pos = lax.broadcasted_iota(jnp.int32, (block, block), 1)
    causal = col_pos <= row_pos
    same = col_pos == row_pos
    for y in range(ROW):
        query = query_parts[lax.rem(place[0] + (ROW - y), ROW)]
        row_ids = ids_row[0:1, pl.ds(span + y * block, block)]
        query_ids = jnp.sum(jnp.where(same, row_ids, 0), axis=1, keepdims=True)
        pieces = []
        for b in range(y + 1):
            key = own[b, :, 0:HD]
            key_ids = ids_row[0:1, pl.ds(span + b * block, block)]
            score = lax.dot_general(
                query, key, (((1,), (1,)), ((), ())), preferred_element_type=F32
            )
            allowed = query_ids == key_ids
            if b == y:
                allowed = allowed & causal
            pieces.append(jnp.where(allowed, score, -1e30))
        if y == 0:
            copies[2].wait()
        for b in range(y, ROW):
            key = past[b, :, 0:HD]
            key_ids = ids_row[0:1, pl.ds(b * block, block)]
            score = lax.dot_general(
                query, key, (((1,), (1,)), ((), ())), preferred_element_type=F32
            )
            pieces.append(jnp.where(query_ids == key_ids, score, -1e30))
        top = pieces[0].max(-1, keepdims=True)
        for piece in pieces[1:]:
            top = jnp.maximum(top, piece.max(-1, keepdims=True))
        weights = [jnp.exp((piece - top) * scale) for piece in pieces]
        total = weights[0].sum(-1, keepdims=True)
        for weight in weights[1:]:
            total = total + weight.sum(-1, keepdims=True)
        inverse = 1.0 / total
        mixed = jnp.zeros((block, HD), F32)
        index = 0
        for b in range(y + 1):
            prob = weights[index].astype(BF)
            mixed += jnp.dot(prob, own[b, :, HD : 2 * HD], preferred_element_type=F32)
            index += 1
        for b in range(y, ROW):
            prob = weights[index].astype(BF)
            mixed += jnp.dot(prob, past[b, :, HD : 2 * HD], preferred_element_type=F32)
            index += 1
        mixed = mixed * inverse
        half = block // 2
        out[0, y] = mixed[:half].astype(BF)
        out[1, y] = mixed[half:].astype(BF)
        for c in range(2):
            store = pltpu.make_async_copy(out.at[c, y], out_hbm.at[c, y], out_sems.at[c, y])
            store.start()
            stores.append(store)
    for store in stores:
        store.wait()


def attention(place, ids_row, query_parts, own, past):
    block = own.shape[1]
    hbm = pl.BlockSpec(memory_space=pltpu.HBM)
    operands = (ids_row, query_parts, own, past)
    result = jax.ShapeDtypeStruct((2, ROW, block // 2, HD), BF)
    return pl.pallas_call(
        attention_kernel,
        out_shape=result,
        in_specs=[pl.BlockSpec(memory_space=pltpu.SMEM)] + [hbm] * 4,
        out_specs=hbm,
        scratch_shapes=[pltpu.VMEM(o.shape, o.dtype) for o in operands]
        + [
            pltpu.VMEM(result.shape, BF),
            pltpu.SemaphoreType.DMA((4,)),
            pltpu.SemaphoreType.DMA((2, ROW)),
        ],
        compiler_params=pltpu.CompilerParams(vmem_limit_bytes=58 << 20),
        cost_estimate=pl.CostEstimate(
            flops=4 * 5 * ROW * block * block * HD,
            bytes_accessed=3 << 20,
            transcendentals=5 * ROW * block * block,
        ),
        name="row_attention",
    )(place, *operands)


def project_kernel(
    core, att_hbm, own_hbm, peer_hbm, low_hbm, att, own, peer, total_low, att_sem, sems, out_sems,
):
    width = total_low.shape[1]
    step = width // 4
    att_copy = pltpu.make_async_copy(att_hbm, att, att_sem)
    att_copy.start()
    copies = []
    for i in range(4):
        cols = pl.ds(i * step, step)
        copies.append(
            (
                pltpu.make_async_copy(own_hbm.at[:, cols], own.at[:, cols], sems.at[0, i]),
                pltpu.make_async_copy(peer_hbm.at[:, cols], peer.at[:, cols], sems.at[1, i]),
            )
        )
    for pair in copies:
        for copy in pair:
            copy.start()
    att_copy.wait()
    c = core[0]
    stores = []
    left = jnp.concatenate([att[c, y] for y in range(ROW)], 1)
    right = jnp.concatenate([att[1 - c, y] for y in range(ROW)], 1)
    for i in range(4):
        cols = pl.ds(i * step, step)
        for copy in copies[i]:
            copy.wait()
        part = jnp.dot(left, own[:, cols], preferred_element_type=F32) + jnp.dot(
            right, peer[:, cols], preferred_element_type=F32
        )
        total_low[:, cols] = part.astype(BF)
        store = pltpu.make_async_copy(total_low.at[:, cols], low_hbm.at[:, cols], out_sems.at[i])
        store.start()
        stores.append(store)
    for store in stores:
        store.wait()


def project(core, att, out_own, out_peer):
    rows = att.shape[2]
    depth, width = out_own.shape
    hbm = pl.BlockSpec(memory_space=pltpu.HBM)
    return pl.pallas_call(
        project_kernel,
        out_shape=jax.ShapeDtypeStruct((rows, width), BF),
        in_specs=[pl.BlockSpec(memory_space=pltpu.SMEM), hbm, hbm, hbm],
        out_specs=hbm,
        scratch_shapes=[
            pltpu.VMEM(att.shape, BF),
            pltpu.VMEM((depth, width), BF),
            pltpu.VMEM((depth, width), BF),
            pltpu.VMEM((rows, width), BF),
            pltpu.SemaphoreType.DMA,
            pltpu.SemaphoreType.DMA((2, 4)),
            pltpu.SemaphoreType.DMA((4,)),
        ],
        compiler_params=pltpu.CompilerParams(vmem_limit_bytes=58 << 20),
        cost_estimate=pl.CostEstimate(
            flops=4 * rows * depth * width, bytes_accessed=6 << 20, transcendentals=0
        ),
        name="project",
    )(core, att, out_own, out_peer)


def norm_kernel(
    core, hidden_hbm, near_hbm, far_hbm, gain_hbm, resid_hbm, normed_hbm,
    hidden, near, far, gain, resid, normed, sems, out_sems,
):
    rows = near.shape[0]
    parts = 2
    block = rows // parts
    start = pl.multiple_of(core[0] * rows, rows)
    gain_copy = pltpu.make_async_copy(gain_hbm, gain, sems.at[3, 0])
    gain_copy.start()
    copies = []
    for i in range(parts):
        here = pl.ds(i * block, block)
        copies.append(
            [
                pltpu.make_async_copy(near_hbm.at[here], near.at[here], sems.at[0, i]),
                pltpu.make_async_copy(far_hbm.at[here], far.at[here], sems.at[1, i]),
                pltpu.make_async_copy(
                    hidden_hbm.at[pl.ds(start + i * block, block)], hidden.at[here], sems.at[2, i]
                ),
            ]
        )
        for copy in copies[i]:
            copy.start()
    gain_copy.wait()
    stores = []
    for i in range(parts):
        here = pl.ds(i * block, block)
        for copy in copies[i]:
            copy.wait()
        value = hidden[here, :].astype(F32) + (
            near[here, :].astype(F32) + far[here, :].astype(F32)
        )
        mean_square = jnp.mean(value * value, axis=-1, keepdims=True)
        normed[here, :] = (value * lax.rsqrt(mean_square + 1e-06) * gain[...]).astype(BF)
        resid[here, :] = value
        for j, (source, target) in enumerate(((normed, normed_hbm), (resid, resid_hbm))):
            store = pltpu.make_async_copy(source.at[here], target.at[here], out_sems.at[j, i])
            store.start()
            stores.append(store)
    for store in stores:
        store.wait()


def add_and_norm(core, hidden, near, far, gain):
    rows, width = near.shape
    hbm = pl.BlockSpec(memory_space=pltpu.HBM)
    return pl.pallas_call(
        norm_kernel,
        out_shape=(
            jax.ShapeDtypeStruct((rows, width), F32),
            jax.ShapeDtypeStruct((rows, width), BF),
        ),
        in_specs=[pl.BlockSpec(memory_space=pltpu.SMEM), hbm, hbm, hbm, hbm],
        out_specs=(hbm, hbm),
        scratch_shapes=[
            pltpu.VMEM((rows, width), BF),
            pltpu.VMEM((rows, width), BF),
            pltpu.VMEM((rows, width), BF),
            pltpu.VMEM((1, width), F32),
            pltpu.VMEM((rows, width), F32),
            pltpu.VMEM((rows, width), BF),
            pltpu.SemaphoreType.DMA((4, 2)),
            pltpu.SemaphoreType.DMA((2, 2)),
        ],
        compiler_params=pltpu.CompilerParams(vmem_limit_bytes=58 << 20),
        cost_estimate=pl.CostEstimate(
            flops=8 * rows * width, bytes_accessed=4 << 20, transcendentals=rows
        ),
        name="add_and_norm",
    )(core, hidden, near, far, gain)


def gather_kernel(
    core, select_hbm, own_hbm, peer_hbm, out_hbm, both_hbm, select, rows, out, sems, out_sems, both_sems
):
    half = rows.shape[0] // 2
    total = out.shape[0]
    block = total // out_sems.shape[0]
    own, peer = pl.ds(0, half), pl.ds(half, half)
    copies = [
        pltpu.make_async_copy(own_hbm, rows.at[own], sems.at[0]),
        pltpu.make_async_copy(peer_hbm, rows.at[peer], sems.at[1]),
        pltpu.make_async_copy(select_hbm, select, sems.at[2]),
    ]
    for copy in copies:
        copy.start()
    for copy in copies:
        copy.wait()
    stores = []
    for i in range(total // block):
        here = pl.ds(i * block, block)
        out[here, :] = jnp.dot(
            select[here, :], rows[...], preferred_element_type=F32
        ).astype(BF)
        store = pltpu.make_async_copy(out.at[here], out_hbm.at[here], out_sems.at[i])
        store.start()
        stores.append(store)
    for j, (source, place) in enumerate(((own, core[0]), (peer, 1 - core[0]))):
        target = pl.ds(pl.multiple_of(place * half, half), half)
        store = pltpu.make_async_copy(rows.at[source], both_hbm.at[target], both_sems.at[j])
        store.start()
        stores.append(store)
    for store in stores:
        store.wait()


def gather_rows(core, select, own, peer):
    slots, rows = select.shape
    width = own.shape[1]
    hbm = pl.BlockSpec(memory_space=pltpu.HBM)
    return pl.pallas_call(
        gather_kernel,
        out_shape=(
            jax.ShapeDtypeStruct((slots, width), BF),
            jax.ShapeDtypeStruct((rows, width), BF),
        ),
        in_specs=[pl.BlockSpec(memory_space=pltpu.SMEM), hbm, hbm, hbm],
        out_specs=(hbm, hbm),
        scratch_shapes=[
            pltpu.VMEM((slots, rows), BF),
            pltpu.VMEM((rows, width), BF),
            pltpu.VMEM((slots, width), BF),
            pltpu.SemaphoreType.DMA((3,)),
            pltpu.SemaphoreType.DMA((6,)),
            pltpu.SemaphoreType.DMA((2,)),
        ],
        compiler_params=pltpu.CompilerParams(vmem_limit_bytes=58 << 20),
        cost_estimate=pl.CostEstimate(
            flops=2 * slots * rows * width, bytes_accessed=7 << 20, transcendentals=0
        ),
        name="gather_rows",
    )(core, select, own, peer)


def slot_weight_kernel(rank, weight, high):
    slots = high.shape[1]
    per_core = CAP // CORES
    experts_here = rank.shape[1]
    lane = lax.broadcasted_iota(jnp.int32, (1, slots), 1)
    expert_of = lax.rem(lax.div(lane, per_core), experts_here)
    wanted = lax.rem(lane, per_core) * CORES + lax.div(lane, per_core * experts_here)
    expand = (
        lax.broadcasted_iota(jnp.int32, (experts_here, slots), 0) == expert_of
    ).astype(BF)
    ranks = jnp.dot(rank[...].astype(BF), expand, preferred_element_type=F32)
    hit = ranks.astype(jnp.int32) == wanted
    spread = jnp.dot(weight[...].astype(BF), expand, preferred_element_type=F32)
    high[...] = jnp.where(hit, spread, 0.0).astype(BF)


def slot_weights(rank, weight, slots):
    rows = rank.shape[0]
    vmem = pl.BlockSpec(memory_space=pltpu.VMEM)
    shape = jax.ShapeDtypeStruct((rows, slots), BF)
    return pl.pallas_call(
        slot_weight_kernel,
        out_shape=shape,
        in_specs=[vmem, vmem],
        out_specs=vmem,
        compiler_params=pltpu.CompilerParams(vmem_limit_bytes=16 << 20),
        cost_estimate=pl.CostEstimate(
            flops=6 * rows * slots * 32, bytes_accessed=2 << 20, transcendentals=0
        ),
        name="slot_weights",
    )(rank, weight)


def expert_kernel(
    x_hbm, both_own, both_peer, down_own, down_peer, out_hbm,
    x, gate, up, down, act, out, x_sems, sems, down_sems, out_sems,
):
    hidden = both_own.shape[1]
    rows = x.shape[0]
    groups, _, width = out.shape
    parts = 3
    block = rows // parts
    step = 256
    bounds = [(lo, min(lo + step, 2 * hidden)) for lo in range(0, 2 * hidden, step)]
    x_copies = [
        pltpu.make_async_copy(
            x_hbm.at[pl.ds(m * block, block)], x.at[pl.ds(m * block, block)], x_sems.at[m]
        )
        for m in range(parts)
    ]
    chunks = []
    for n, (lo, hi) in enumerate(bounds):
        copies = []
        for j, (source, start, stop) in enumerate(
            (
                (both_own, lo, min(hi, hidden)),
                (both_peer, max(lo, hidden) - hidden, hi - hidden),
            )
        ):
            if stop <= start:
                continue
            shift = hidden * j
            for k, target in enumerate((gate, up)):
                copies.append(
                    pltpu.make_async_copy(
                        source.at[k, pl.ds(start, stop - start)],
                        target.at[pl.ds(start + shift, stop - start)],
                        sems.at[n, j, k],
                    )
                )
        chunks.append(copies)
    down_copies = [
        pltpu.make_async_copy(source, down.at[pl.ds(j * hidden, hidden)], down_sems.at[j])
        for j, source in enumerate((down_own, down_peer))
    ]
    def begin(copies):
        for copy in copies:
            copy.start()

    def finish(copies):
        for copy in copies:
            copy.wait()

    def halves(n, start, count):
        lo, hi = bounds[n]
        here = pl.ds(start * block, count * block)
        left = x[here, :]
        g = lax.dot_general(left, gate[lo:hi, :], contract, preferred_element_type=F32)
        u = lax.dot_general(left, up[lo:hi, :], contract, preferred_element_type=F32)
        act[here, lo:hi] = (g / (1.0 + jnp.exp(-g)) * u).astype(BF)

    contract = (((1,), (1,)), ((), ()))
    begin([x_copies[0]] + chunks[0])
    begin(x_copies[1:])
    finish([x_copies[0]] + chunks[0])
    begin(chunks[1])
    halves(0, 0, 1)
    finish(x_copies[1:])
    begin(chunks[2])
    halves(0, 1, parts - 1)
    finish(chunks[1])
    begin(down_copies)
    halves(1, 0, parts)
    finish(chunks[2])
    halves(2, 0, parts)
    finish(down_copies)
    stores = []
    for i in range(groups):
        result = jnp.dot(
            act[...], down[:, i * width : (i + 1) * width], preferred_element_type=F32
        )
        out[i] = result.astype(BF)
        store = pltpu.make_async_copy(out.at[i], out_hbm.at[i], out_sems.at[i])
        store.start()
        stores.append(store)
    for store in stores:
        store.wait()


def experts(x, both_own, both_peer, down_own, down_peer, groups):
    rows, depth = x.shape
    hidden, width = down_own.shape
    column_width = width // groups
    hbm = pl.BlockSpec(memory_space=pltpu.HBM)
    return pl.pallas_call(
        expert_kernel,
        out_shape=jax.ShapeDtypeStruct((groups, rows, column_width), BF),
        in_specs=[hbm] * 5,
        out_specs=hbm,
        scratch_shapes=[
            pltpu.VMEM((rows, depth), BF),
            pltpu.VMEM((2 * hidden, depth), BF),
            pltpu.VMEM((2 * hidden, depth), BF),
            pltpu.VMEM((2 * hidden, width), BF),
            pltpu.VMEM((rows, 2 * hidden), BF),
            pltpu.VMEM((groups, rows, column_width), BF),
            pltpu.SemaphoreType.DMA((3,)),
            pltpu.SemaphoreType.DMA((pl.cdiv(2 * hidden, 256), 2, 2)),
            pltpu.SemaphoreType.DMA((2,)),
            pltpu.SemaphoreType.DMA((groups,)),
        ],
        compiler_params=pltpu.CompilerParams(vmem_limit_bytes=60 << 20),
        cost_estimate=pl.CostEstimate(
            flops=12 * rows * depth * hidden,
            bytes_accessed=15 << 20,
            transcendentals=2 * rows * hidden,
        ),
        name="experts",
    )(x, both_own, both_peer, down_own, down_peer)


def combine_kernel(
    core, high_hbm, back_hbm, mine_hbm, peers_hbm, shared_hbm, out,
    high, back, mine, peers, shared, sems,
):
    rows = mine.shape[0]
    chips, depth = back.shape[0], back.shape[1]
    block = depth // CORES
    pieces = [(chip, pl.ds(c * block, block)) for chip in range(chips) for c in range(CORES)]
    copies = [
        pltpu.make_async_copy(back_hbm.at[chip, here], back.at[chip, here], sems.at[i])
        for i, (chip, here) in enumerate(pieces)
    ]
    rest = [
        pltpu.make_async_copy(source, target, sems.at[len(pieces) + i])
        for i, (source, target) in enumerate(
            (
                (high_hbm, high),
                (shared_hbm, shared),
                (mine_hbm, mine),
                (peers_hbm, peers),
            )
        )
    ]
    for copy in [rest[0]] + copies + rest[1:]:
        copy.start()
    total = None
    for i, (copy, (chip, here)) in enumerate(zip(copies, pieces)):
        if i == 0:
            rest[0].wait()
        copy.wait()
        part = jnp.dot(high[:, here], back[chip, here], preferred_element_type=F32)
        total = part if total is None else total + part
    for copy in rest[1:]:
        copy.wait()
    total += shared[...]
    first = core[0] == 0
    low_half = jnp.where(first, mine[...], peers[...])
    high_half = jnp.where(first, peers[...], mine[...])
    out[0:rows, :] = (total[0:rows] + low_half).astype(BF)
    out[rows : 2 * rows, :] = (total[rows:] + high_half).astype(BF)


def combine(core, high, returned, mine, peers, shared):
    hbm = pl.BlockSpec(memory_space=pltpu.HBM)
    vmem = pl.BlockSpec(memory_space=pltpu.VMEM)
    rows, width = shared.shape
    operands = (high, returned, mine, peers, shared)
    return pl.pallas_call(
        combine_kernel,
        out_shape=jax.ShapeDtypeStruct((rows, width), BF),
        in_specs=[pl.BlockSpec(memory_space=pltpu.SMEM)] + [hbm] * 5,
        out_specs=vmem,
        scratch_shapes=[pltpu.VMEM(o.shape, o.dtype) for o in operands]
        + [pltpu.SemaphoreType.DMA((8,))],
        compiler_params=pltpu.CompilerParams(vmem_limit_bytes=60 << 20),
        cost_estimate=pl.CostEstimate(
            flops=8 * rows * width * high.shape[1], bytes_accessed=7 << 20, transcendentals=0
        ),
        name="combine",
    )(core, *operands)


def page_pieces(keys, values, owner_all, tok_count, head_count, tok_index):
    pages_here = owner_all.shape[1]
    tok_rows = keys.shape[0]
    quarter_page = PAGE // head_count
    mine = lax.dynamic_index_in_dim(owner_all, tok_index, 0, keepdims=False)
    row = jnp.arange(tok_rows, dtype=jnp.int32)
    quarter = row // (tok_count * quarter_page)
    owner = row // quarter_page % tok_count
    line = quarter * quarter_page + row % quarter_page
    token_owner = jnp.repeat(mine, PAGE)
    token_line = jnp.arange(tok_rows, dtype=jnp.int32) % PAGE
    pick = (
        (owner[:, None] == token_owner[None, :]) & (line[:, None] == token_line[None, :])
    ).astype(BF)
    parts = [
        jnp.dot(pick, part, preferred_element_type=F32).astype(BF) for part in (keys, values)
    ]
    return jnp.concatenate(parts, 1).reshape(head_count * tok_count, quarter_page, -1)


def place_pages(landed, slots_all, owner_all, tok_count, head_count, tok_index):
    pages_here = owner_all.shape[1]
    quarter_page = PAGE // head_count
    rows = pages_here * quarter_page
    arrival = jnp.sum(jnp.where(owner_all == tok_index, slots_all % pages_here, 0), 1)
    row = jnp.arange(rows, dtype=jnp.int32)
    target = jnp.repeat(arrival, quarter_page) * quarter_page + row % quarter_page
    place = (row[:, None] == target[None, :]).astype(BF)
    landed = landed.reshape(head_count, rows, -1)
    width = landed.shape[2] // 2
    placed = [
        jnp.dot(place, landed[h], preferred_element_type=F32).astype(BF)
        for h in range(head_count)
    ]
    cache = jnp.concatenate(
        [p[:, :width] for p in placed] + [p[:, width:] for p in placed], 1
    )
    return cache.reshape(pages_here, quarter_page, 2 * head_count * width)


def per_device(
    hidden_in,
    queries,
    keys,
    values,
    request_ids,
    out_proj,
    norm_gain,
    expert_gate_up,
    expert_down,
    shared_gate_up,
    shared_down,
    shared_gate,
    routes,
    route_weights,
    page_slots,
):
    tok_rows, model_width = hidden_in.shape
    head_width = queries.shape[1]
    heads_here = head_width // HD
    tok_count = lax.axis_size("tok")
    head_count = lax.axis_size("head")
    tok_index = lax.axis_index("tok")
    head_index = lax.axis_index("head")
    core = head_index % CORES
    column_width = model_width // head_count
    rows_of_blocks = tok_count // ROW
    half = tok_rows // 2
    slots_core = CAP // CORES

    gate_up_own = jnp.transpose(expert_gate_up[0], (1, 2, 0))
    down_own = expert_down[0]
    out_peer = lax.ppermute(out_proj, "head", INTRA)
    gate_up_peer = lax.ppermute(gate_up_own, "head", INTRA)
    down_peer = lax.ppermute(down_own, "head", INTRA)

    packed = pack_heads(keys, values)
    row_groups = [[r * ROW + y for y in range(ROW)] for r in range(rows_of_blocks)]
    own = lax.all_to_all(
        packed, "tok", split_axis=0, concat_axis=0, tiled=True, axis_index_groups=row_groups
    )
    span = ROW * tok_rows
    base = (tok_index // ROW) * span
    padded_ids = jnp.concatenate([jnp.full((span,), -1, jnp.int32), request_ids], 0)
    window_ids = lax.dynamic_slice_in_dim(padded_ids, base, 2 * span, 0)
    ids_row = window_ids[None, :]
    queries, own = lax.optimization_barrier((queries, own))
    place_in_row = tok_index % ROW
    query_parts = []
    for step in range(ROW):
        target = (place_in_row + step) % ROW
        part = lax.dynamic_slice_in_dim(queries, target * HD, HD, 1)
        if step:
            part = lax.ppermute(
                part,
                "tok",
                [
                    (r * ROW + y, r * ROW + (y + step) % ROW)
                    for r in range(rows_of_blocks)
                    for y in range(ROW)
                ],
            )
        query_parts.append(part)
    slots_all = page_slots.reshape(tok_count, tok_rows // PAGE)
    owner_all = slots_all // (tok_rows // PAGE)
    pieces = page_pieces(keys, values, owner_all, tok_count, head_count, tok_index)
    past = lax.ppermute(
        own, "tok", [(s, s + ROW) for s in range(tok_count - ROW)]
    )
    expert_ids = jnp.arange(EXPERTS, dtype=jnp.int32)
    named = routes[:, :, None] == expert_ids[None, None, :]
    onehot = jnp.sum(named.astype(F32), 1)
    weight_of = jnp.sum(jnp.where(named, route_weights[:, :, None], 0.0), 1)
    earlier = (
        jnp.arange(tok_rows, dtype=jnp.int32)[None, :] < jnp.arange(tok_rows, dtype=jnp.int32)[:, None]
    ).astype(BF)
    rank = jnp.dot(earlier, onehot.astype(BF), preferred_element_type=F32).astype(jnp.int32)
    rank = jnp.where(onehot > 0, rank, -1)
    rank_t = rank.T
    rank_rel = jnp.where(core == 0, rank_t, jnp.roll(rank_t, half, 1))
    place = jnp.arange(slots_core, dtype=jnp.int32) * CORES
    select = (rank_rel[:, None, :] == (place + core)[None, :, None]).astype(BF)
    select = select.reshape(EXPERTS * slots_core, tok_rows)
    past, select = lax.optimization_barrier((past, select))
    attended = attention(
        place_in_row.reshape(1), ids_row, jnp.stack(query_parts, 0), own, past
    )

    core_groups = [
        [
            (chip * CORES + c) * tok_count + r * ROW + y
            for c in range(CORES)
            for y in range(ROW)
        ]
        for chip in range(CHIPS)
        for r in range(rows_of_blocks)
    ]
    gathered = lax.all_to_all(
        attended.reshape(CORES * ROW, half, HD),
        BOTH,
        split_axis=0,
        concat_axis=0,
        tiled=True,
        axis_index_groups=core_groups,
    ).reshape(CORES, ROW, half, HD)
    core_ref = core.reshape(1)
    gathered, pieces = lax.optimization_barrier((gathered, pieces))
    projected_low = project(core_ref, gathered, out_proj, out_peer)
    projected_far = lax.ppermute(projected_low, "head", CROSS)
    pieces, _ = lax.optimization_barrier((pieces, projected_low))
    landed = lax.all_to_all(pieces, BOTH, split_axis=0, concat_axis=0, tiled=True)
    resid, normed_own = add_and_norm(
        core_ref, hidden_in, projected_low, projected_far, norm_gain[None, :]
    )
    normed_own, landed = lax.optimization_barrier((normed_own, landed))
    normed_peer = lax.ppermute(normed_own, "head", INTRA)

    outgoing, normed_abs = gather_rows(core_ref, select, normed_own, normed_peer)
    rank, weight_of, _ = lax.optimization_barrier((rank, weight_of, outgoing))
    high = slot_weights(rank, weight_of, CORES * EXPERTS * slots_core)
    arrived = lax.all_to_all(
        outgoing.reshape(tok_count, slots_core, model_width),
        "tok",
        split_axis=0,
        concat_axis=0,
        tiled=True,
    ).reshape(tok_count * slots_core, model_width)
    shared_both = jnp.einsum("td,dgf->tgf", normed_abs, shared_gate_up, preferred_element_type=F32)
    shared_act = (jax.nn.silu(shared_both[:, 0, :]) * shared_both[:, 1, :]).astype(BF)
    shared_scale = jax.nn.sigmoid(jnp.dot(normed_abs, shared_gate, preferred_element_type=F32))
    shared_term = shared_scale[:, None] * jnp.dot(
        shared_act, shared_down, preferred_element_type=F32
    )
    chip = head_index // CORES
    chip_width = CORES * column_width
    shared_near = lax.dynamic_slice_in_dim(shared_term, chip * chip_width, chip_width, 1)
    shared_send = lax.dynamic_slice_in_dim(
        shared_term, (1 - chip) * chip_width, chip_width, 1
    ).astype(BF)
    shared_near, shared_send, arrived = lax.optimization_barrier(
        (shared_near, shared_send, arrived)
    )
    shared_far = lax.ppermute(shared_send, "head", CROSS)

    partial = experts(arrived, gate_up_own, gate_up_peer, down_own, down_peer, head_count)
    partial = partial.reshape(head_count * tok_count, slots_core, column_width)
    partial, shared_far = lax.optimization_barrier((partial, shared_far))
    returned = lax.all_to_all(partial, BOTH, split_axis=0, concat_axis=0, tiled=True)
    returned = returned.reshape(CHIPS, CORES * EXPERTS * slots_core, column_width)

    shared_chip = shared_near + shared_far.astype(F32)
    shared_own = lax.dynamic_slice_in_dim(shared_chip, core * column_width, column_width, 1)
    shared_peer = lax.dynamic_slice_in_dim(
        shared_chip, (1 - core) * column_width, column_width, 1
    ).astype(BF)
    shared_cols = shared_own + lax.ppermute(shared_peer, "head", INTRA).astype(F32)
    own_cols = lax.dynamic_slice_in_dim(resid, head_index * column_width, column_width, 1)
    peer_cols = lax.dynamic_slice_in_dim(
        resid, (head_index + 1 - 2 * core) * column_width, column_width, 1
    )
    from_peer = lax.ppermute(peer_cols, "head", INTRA)
    layer_out = combine(core_ref, high, returned, own_cols, from_peer, shared_cols)
    decode_cache = place_pages(landed, slots_all, owner_all, tok_count, head_count, tok_index)
    return (layer_out, decode_cache)


def solution(mesh):
    in_specs = (
        P("tok", None),
        P("tok", "head"),
        P("tok", "head"),
        P("tok", "head"),
        P(),
        P("head", None),
        P(),
        P("tok", None, None, "head"),
        P("tok", "head", None),
        P(None, None, "head"),
        P("head", None),
        P(),
        P("tok", None),
        P("tok", None),
        P(),
    )
    out_specs = (P("tok", "head"), P("tok", "head", None))
    return jax.shard_map(
        per_device, mesh=mesh, in_specs=in_specs, out_specs=out_specs, check_vma=False
    )
```

```python
import math

import jax
import jax.numpy as jnp
from jax import lax
from jax.experimental import pallas as pl
from jax.experimental.pallas import tpu as pltpu
from jax.sharding import PartitionSpec as P

HD = 128
TOP = 4
EXPERTS = 32
PAGE = 8
CAP = 48
ROW = 4
CORES = 2
CHIPS = 2
BF = jnp.bfloat16
F32 = jnp.float32
BOTH = ("head", "tok")
INTRA = [(0, 1), (1, 0), (2, 3), (3, 2)]
CROSS = [(0, 2), (2, 0), (1, 3), (3, 1)]


def pack_kernel(place, keys, values, *outs):
    for step, out in enumerate(outs):
        head = lax.rem(place[0] + step, ROW)
        here = pl.ds(pl.multiple_of(head * HD, HD), HD)
        out[:, 0:HD] = keys[:, here]
        out[:, HD : 2 * HD] = values[:, here]


def pack_heads(place, keys, values):
    rows, width = keys.shape
    vmem = pl.BlockSpec(memory_space=pltpu.VMEM)
    heads = width // HD
    return pl.pallas_call(
        pack_kernel,
        out_shape=(jax.ShapeDtypeStruct((rows, 2 * HD), BF),) * heads,
        in_specs=[pl.BlockSpec(memory_space=pltpu.SMEM), vmem, vmem],
        out_specs=(vmem,) * heads,
        compiler_params=pltpu.CompilerParams(vmem_limit_bytes=60 << 20),
        cost_estimate=pl.CostEstimate(flops=0, bytes_accessed=1 << 20, transcendentals=0),
        name="pack_heads",
    )(place, keys, values)


def attention_kernel(
    place, ids_row_hbm, query_hbm, own_hbm, past_hbm, out_hbm,
    ids_row, query_parts, own, past, out, sems, out_sems,
):
    block = out.shape[2] * 2
    pairs = (
        (query_hbm, query_parts),
        (own_hbm, own),
        (past_hbm, past),
        (ids_row_hbm, ids_row),
    )
    copies = [
        pltpu.make_async_copy(source, target, sems.at[i])
        for i, (source, target) in enumerate(pairs)
    ]
    for copy in copies:
        copy.start()
    for copy in copies:
        copy.wait()
    stores = []

    def slot(b):
        return lax.rem(place[0] + (ROW - b), ROW)

    scale = 1.0 / math.sqrt(HD)
    span = ROW * block
    row_pos = lax.broadcasted_iota(jnp.int32, (block, block), 0)
    col_pos = lax.broadcasted_iota(jnp.int32, (block, block), 1)
    causal = col_pos <= row_pos
    same = col_pos == row_pos
    for y in range(ROW):
        query = query_parts[lax.rem(place[0] + (ROW - y), ROW)]
        row_ids = ids_row[0:1, pl.ds(span + y * block, block)]
        query_ids = jnp.sum(jnp.where(same, row_ids, 0), axis=1, keepdims=True)
        pieces = []
        for b in range(y, ROW):
            key = past[slot(b), :, 0:HD]
            key_ids = ids_row[0:1, pl.ds(b * block, block)]
            score = lax.dot_general(
                query, key, (((1,), (1,)), ((), ())), preferred_element_type=F32
            )
            pieces.append(jnp.where(query_ids == key_ids, score, -1e30))
        for b in range(y + 1):
            key = own[slot(b), :, 0:HD]
            key_ids = ids_row[0:1, pl.ds(span + b * block, block)]
            score = lax.dot_general(
                query, key, (((1,), (1,)), ((), ())), preferred_element_type=F32
            )
            allowed = query_ids == key_ids
            if b == y:
                allowed = allowed & causal
            pieces.append(jnp.where(allowed, score, -1e30))
        top = pieces[0].max(-1, keepdims=True)
        for piece in pieces[1:]:
            top = jnp.maximum(top, piece.max(-1, keepdims=True))
        weights = [jnp.exp((piece - top) * scale) for piece in pieces]
        total = weights[0].sum(-1, keepdims=True)
        for weight in weights[1:]:
            total = total + weight.sum(-1, keepdims=True)
        inverse = 1.0 / total
        mixed = jnp.zeros((block, HD), F32)
        index = 0
        for b in range(y, ROW):
            prob = weights[index].astype(BF)
            mixed += jnp.dot(prob, past[slot(b), :, HD : 2 * HD], preferred_element_type=F32)
            index += 1
        for b in range(y + 1):
            prob = weights[index].astype(BF)
            mixed += jnp.dot(prob, own[slot(b), :, HD : 2 * HD], preferred_element_type=F32)
            index += 1
        mixed = mixed * inverse
        half = block // 2
        out[0, y] = mixed[:half].astype(BF)
        out[1, y] = mixed[half:].astype(BF)
        for c in range(2):
            store = pltpu.make_async_copy(out.at[c, y], out_hbm.at[c, y], out_sems.at[c, y])
            store.start()
            stores.append(store)
    for store in stores:
        store.wait()


def attention(place, ids_row, query_parts, own, past):
    block = own.shape[1]
    hbm = pl.BlockSpec(memory_space=pltpu.HBM)
    operands = (ids_row, query_parts, own, past)
    result = jax.ShapeDtypeStruct((2, ROW, block // 2, HD), BF)
    return pl.pallas_call(
        attention_kernel,
        out_shape=result,
        in_specs=[pl.BlockSpec(memory_space=pltpu.SMEM)] + [hbm] * 4,
        out_specs=hbm,
        scratch_shapes=[pltpu.VMEM(o.shape, o.dtype) for o in operands]
        + [
            pltpu.VMEM(result.shape, BF),
            pltpu.SemaphoreType.DMA((4,)),
            pltpu.SemaphoreType.DMA((2, ROW)),
        ],
        compiler_params=pltpu.CompilerParams(vmem_limit_bytes=58 << 20),
        cost_estimate=pl.CostEstimate(
            flops=4 * 5 * ROW * block * block * HD,
            bytes_accessed=3 << 20,
            transcendentals=5 * ROW * block * block,
        ),
        name="row_attention",
    )(place, *operands)


def project_kernel(
    core, att_hbm, own_hbm, peer_hbm, low_hbm, att, own, peer, total_low, att_sem, sems, out_sems,
):
    width = total_low.shape[1]
    step = width // 4
    att_copy = pltpu.make_async_copy(att_hbm, att, att_sem)
    att_copy.start()
    copies = []
    for i in range(4):
        cols = pl.ds(i * step, step)
        copies.append(
            (
                pltpu.make_async_copy(own_hbm.at[:, cols], own.at[:, cols], sems.at[0, i]),
                pltpu.make_async_copy(peer_hbm.at[:, cols], peer.at[:, cols], sems.at[1, i]),
            )
        )
    for pair in copies:
        for copy in pair:
            copy.start()
    att_copy.wait()
    c = core[0]
    stores = []
    left = jnp.concatenate([att[c, y] for y in range(ROW)], 1)
    right = jnp.concatenate([att[1 - c, y] for y in range(ROW)], 1)
    for i in range(4):
        cols = pl.ds(i * step, step)
        for copy in copies[i]:
            copy.wait()
        part = jnp.dot(left, own[:, cols], preferred_element_type=F32) + jnp.dot(
            right, peer[:, cols], preferred_element_type=F32
        )
        total_low[:, cols] = part.astype(BF)
        store = pltpu.make_async_copy(total_low.at[:, cols], low_hbm.at[:, cols], out_sems.at[i])
        store.start()
        stores.append(store)
    for store in stores:
        store.wait()


def project(core, att, out_own, out_peer):
    rows = att.shape[2]
    depth, width = out_own.shape
    hbm = pl.BlockSpec(memory_space=pltpu.HBM)
    return pl.pallas_call(
        project_kernel,
        out_shape=jax.ShapeDtypeStruct((rows, width), BF),
        in_specs=[pl.BlockSpec(memory_space=pltpu.SMEM), hbm, hbm, hbm],
        out_specs=hbm,
        scratch_shapes=[
            pltpu.VMEM(att.shape, BF),
            pltpu.VMEM((depth, width), BF),
            pltpu.VMEM((depth, width), BF),
            pltpu.VMEM((rows, width), BF),
            pltpu.SemaphoreType.DMA,
            pltpu.SemaphoreType.DMA((2, 4)),
            pltpu.SemaphoreType.DMA((4,)),
        ],
        compiler_params=pltpu.CompilerParams(vmem_limit_bytes=58 << 20),
        cost_estimate=pl.CostEstimate(
            flops=4 * rows * depth * width, bytes_accessed=6 << 20, transcendentals=0
        ),
        name="project",
    )(core, att, out_own, out_peer)


def norm_kernel(
    core, hidden_hbm, near_hbm, far_hbm, gain_hbm, resid_hbm, normed_hbm,
    hidden, near, far, gain, resid, normed, sems, out_sems,
):
    rows = near.shape[0]
    parts = 2
    block = rows // parts
    start = pl.multiple_of(core[0] * rows, rows)
    gain_copy = pltpu.make_async_copy(gain_hbm, gain, sems.at[3, 0])
    gain_copy.start()
    copies = []
    for i in range(parts):
        here = pl.ds(i * block, block)
        copies.append(
            [
                pltpu.make_async_copy(near_hbm.at[here], near.at[here], sems.at[0, i]),
                pltpu.make_async_copy(far_hbm.at[here], far.at[here], sems.at[1, i]),
                pltpu.make_async_copy(
                    hidden_hbm.at[pl.ds(start + i * block, block)], hidden.at[here], sems.at[2, i]
                ),
            ]
        )
        for copy in copies[i]:
            copy.start()
    gain_copy.wait()
    stores = []
    for i in range(parts):
        here = pl.ds(i * block, block)
        for copy in copies[i]:
            copy.wait()
        value = hidden[here, :].astype(F32) + (
            near[here, :].astype(F32) + far[here, :].astype(F32)
        )
        mean_square = jnp.mean(value * value, axis=-1, keepdims=True)
        normed[here, :] = (value * lax.rsqrt(mean_square + 1e-06) * gain[...]).astype(BF)
        resid[here, :] = value
        for j, (source, target) in enumerate(((normed, normed_hbm), (resid, resid_hbm))):
            store = pltpu.make_async_copy(source.at[here], target.at[here], out_sems.at[j, i])
            store.start()
            stores.append(store)
    for store in stores:
        store.wait()


def add_and_norm(core, hidden, near, far, gain):
    rows, width = near.shape
    hbm = pl.BlockSpec(memory_space=pltpu.HBM)
    return pl.pallas_call(
        norm_kernel,
        out_shape=(
            jax.ShapeDtypeStruct((rows, width), F32),
            jax.ShapeDtypeStruct((rows, width), BF),
        ),
        in_specs=[pl.BlockSpec(memory_space=pltpu.SMEM), hbm, hbm, hbm, hbm],
        out_specs=(hbm, hbm),
        scratch_shapes=[
            pltpu.VMEM((rows, width), BF),
            pltpu.VMEM((rows, width), BF),
            pltpu.VMEM((rows, width), BF),
            pltpu.VMEM((1, width), F32),
            pltpu.VMEM((rows, width), F32),
            pltpu.VMEM((rows, width), BF),
            pltpu.SemaphoreType.DMA((4, 2)),
            pltpu.SemaphoreType.DMA((2, 2)),
        ],
        compiler_params=pltpu.CompilerParams(vmem_limit_bytes=58 << 20),
        cost_estimate=pl.CostEstimate(
            flops=8 * rows * width, bytes_accessed=4 << 20, transcendentals=rows
        ),
        name="add_and_norm",
    )(core, hidden, near, far, gain)


def gather_kernel(
    select_hbm, own_hbm, peer_hbm, out_hbm, select, rows, out, sems, out_sems
):
    half = rows.shape[0] // 2
    total, block = out.shape[0], out.shape[0] // 3
    copies = [
        pltpu.make_async_copy(own_hbm, rows.at[pl.ds(0, half)], sems.at[0]),
        pltpu.make_async_copy(peer_hbm, rows.at[pl.ds(half, half)], sems.at[1]),
        pltpu.make_async_copy(select_hbm, select, sems.at[2]),
    ]
    for copy in copies:
        copy.start()
    for copy in copies:
        copy.wait()
    stores = []
    for i in range(total // block):
        here = pl.ds(i * block, block)
        out[here, :] = jnp.dot(
            select[here, :], rows[...], preferred_element_type=F32
        ).astype(BF)
        store = pltpu.make_async_copy(out.at[here], out_hbm.at[here], out_sems.at[i])
        store.start()
        stores.append(store)
    for store in stores:
        store.wait()


def gather_rows(select, own, peer):
    slots, rows = select.shape
    width = own.shape[1]
    hbm = pl.BlockSpec(memory_space=pltpu.HBM)
    return pl.pallas_call(
        gather_kernel,
        out_shape=jax.ShapeDtypeStruct((slots, width), BF),
        in_specs=[hbm, hbm, hbm],
        out_specs=hbm,
        scratch_shapes=[
            pltpu.VMEM((slots, rows), BF),
            pltpu.VMEM((rows, width), BF),
            pltpu.VMEM((slots, width), BF),
            pltpu.SemaphoreType.DMA((3,)),
            pltpu.SemaphoreType.DMA((3,)),
        ],
        compiler_params=pltpu.CompilerParams(vmem_limit_bytes=58 << 20),
        cost_estimate=pl.CostEstimate(
            flops=2 * slots * rows * width, bytes_accessed=5 << 20, transcendentals=0
        ),
        name="gather_rows",
    )(select, own, peer)


def slot_weight_kernel(rank, weight, high):
    slots = high.shape[1]
    per_core = CAP // CORES
    experts_here = rank.shape[1]
    lane = lax.broadcasted_iota(jnp.int32, (1, slots), 1)
    expert_of = lax.rem(lax.div(lane, per_core), experts_here)
    wanted = lax.rem(lane, per_core) * CORES + lax.div(lane, per_core * experts_here)
    expand = (
        lax.broadcasted_iota(jnp.int32, (experts_here, slots), 0) == expert_of
    ).astype(BF)
    ranks = jnp.dot(rank[...].astype(BF), expand, preferred_element_type=F32)
    hit = ranks.astype(jnp.int32) == wanted
    spread = jnp.dot(weight[...].astype(BF), expand, preferred_element_type=F32)
    high[...] = jnp.where(hit, spread, 0.0).astype(BF)


def slot_weights(rank, weight, slots):
    rows = rank.shape[0]
    vmem = pl.BlockSpec(memory_space=pltpu.VMEM)
    shape = jax.ShapeDtypeStruct((rows, slots), BF)
    return pl.pallas_call(
        slot_weight_kernel,
        out_shape=shape,
        in_specs=[vmem, vmem],
        out_specs=vmem,
        compiler_params=pltpu.CompilerParams(vmem_limit_bytes=16 << 20),
        cost_estimate=pl.CostEstimate(
            flops=6 * rows * slots * 32, bytes_accessed=2 << 20, transcendentals=0
        ),
        name="slot_weights",
    )(rank, weight)


def expert_kernel(
    x_hbm, both_own, both_peer, down_own, down_peer, out_hbm,
    x, gate, up, down, act, out, x_sems, sems, down_sems, out_sems,
):
    hidden = both_own.shape[1]
    rows = x.shape[0]
    groups, _, width = out.shape
    parts = 3
    block = rows // parts
    step = 256
    bounds = [(lo, min(lo + step, 2 * hidden)) for lo in range(0, 2 * hidden, step)]
    x_copies = [
        pltpu.make_async_copy(
            x_hbm.at[pl.ds(m * block, block)], x.at[pl.ds(m * block, block)], x_sems.at[m]
        )
        for m in range(parts)
    ]
    chunks = []
    for n, (lo, hi) in enumerate(bounds):
        copies = []
        for j, (source, start, stop) in enumerate(
            (
                (both_own, lo, min(hi, hidden)),
                (both_peer, max(lo, hidden) - hidden, hi - hidden),
            )
        ):
            if stop <= start:
                continue
            shift = hidden * j
            for k, target in enumerate((gate, up)):
                copies.append(
                    pltpu.make_async_copy(
                        source.at[k, pl.ds(start, stop - start)],
                        target.at[pl.ds(start + shift, stop - start)],
                        sems.at[n, j, k],
                    )
                )
        chunks.append(copies)
    down_copies = [
        pltpu.make_async_copy(source, down.at[pl.ds(j * hidden, hidden)], down_sems.at[j])
        for j, source in enumerate((down_own, down_peer))
    ]
    def begin(copies):
        for copy in copies:
            copy.start()

    def finish(copies):
        for copy in copies:
            copy.wait()

    def halves(n, start, count):
        lo, hi = bounds[n]
        here = pl.ds(start * block, count * block)
        left = x[here, :]
        g = lax.dot_general(left, gate[lo:hi, :], contract, preferred_element_type=F32)
        u = lax.dot_general(left, up[lo:hi, :], contract, preferred_element_type=F32)
        act[here, lo:hi] = (g / (1.0 + jnp.exp(-g)) * u).astype(BF)

    contract = (((1,), (1,)), ((), ()))
    begin([x_copies[0]] + chunks[0])
    begin(x_copies[1:])
    finish([x_copies[0]] + chunks[0])
    begin(chunks[1])
    halves(0, 0, 1)
    finish(x_copies[1:])
    begin(chunks[2])
    halves(0, 1, parts - 1)
    finish(chunks[1])
    begin(down_copies)
    halves(1, 0, parts)
    finish(chunks[2])
    halves(2, 0, parts)
    finish(down_copies)
    stores = []
    for i in range(groups):
        result = jnp.dot(
            act[...], down[:, i * width : (i + 1) * width], preferred_element_type=F32
        )
        out[i] = result.astype(BF)
        store = pltpu.make_async_copy(out.at[i], out_hbm.at[i], out_sems.at[i])
        store.start()
        stores.append(store)
    for store in stores:
        store.wait()


def experts(x, both_own, both_peer, down_own, down_peer, groups):
    rows, depth = x.shape
    hidden, width = down_own.shape
    column_width = width // groups
    hbm = pl.BlockSpec(memory_space=pltpu.HBM)
    return pl.pallas_call(
        expert_kernel,
        out_shape=jax.ShapeDtypeStruct((groups, rows, column_width), BF),
        in_specs=[hbm] * 5,
        out_specs=hbm,
        scratch_shapes=[
            pltpu.VMEM((rows, depth), BF),
            pltpu.VMEM((2 * hidden, depth), BF),
            pltpu.VMEM((2 * hidden, depth), BF),
            pltpu.VMEM((2 * hidden, width), BF),
            pltpu.VMEM((rows, 2 * hidden), BF),
            pltpu.VMEM((groups, rows, column_width), BF),
            pltpu.SemaphoreType.DMA((3,)),
            pltpu.SemaphoreType.DMA((pl.cdiv(2 * hidden, 256), 2, 2)),
            pltpu.SemaphoreType.DMA((2,)),
            pltpu.SemaphoreType.DMA((groups,)),
        ],
        compiler_params=pltpu.CompilerParams(vmem_limit_bytes=60 << 20),
        cost_estimate=pl.CostEstimate(
            flops=12 * rows * depth * hidden,
            bytes_accessed=15 << 20,
            transcendentals=2 * rows * hidden,
        ),
        name="experts",
    )(x, both_own, both_peer, down_own, down_peer)


def combine_kernel(
    core, high_hbm, back_hbm, mine_hbm, peers_hbm, shared_hbm, out,
    high, back, mine, peers, shared, sems,
):
    rows = mine.shape[0]
    chips, depth = back.shape[0], back.shape[1]
    block = depth // CORES
    pieces = [(chip, pl.ds(c * block, block)) for chip in range(chips) for c in range(CORES)]
    copies = [
        pltpu.make_async_copy(back_hbm.at[chip, here], back.at[chip, here], sems.at[i])
        for i, (chip, here) in enumerate(pieces)
    ]
    rest = [
        pltpu.make_async_copy(source, target, sems.at[len(pieces) + i])
        for i, (source, target) in enumerate(
            (
                (high_hbm, high),
                (shared_hbm, shared),
                (mine_hbm, mine),
                (peers_hbm, peers),
            )
        )
    ]
    for copy in [rest[0]] + copies + rest[1:]:
        copy.start()
    total = None
    for i, (copy, (chip, here)) in enumerate(zip(copies, pieces)):
        if i == 0:
            rest[0].wait()
        copy.wait()
        part = jnp.dot(high[:, here], back[chip, here], preferred_element_type=F32)
        total = part if total is None else total + part
    for copy in rest[1:]:
        copy.wait()
    total += shared[...]
    first = core[0] == 0
    low_half = jnp.where(first, mine[...], peers[...])
    high_half = jnp.where(first, peers[...], mine[...])
    out[0:rows, :] = (total[0:rows] + low_half).astype(BF)
    out[rows : 2 * rows, :] = (total[rows:] + high_half).astype(BF)


def combine(core, high, returned, mine, peers, shared):
    hbm = pl.BlockSpec(memory_space=pltpu.HBM)
    vmem = pl.BlockSpec(memory_space=pltpu.VMEM)
    rows, width = shared.shape
    operands = (high, returned, mine, peers, shared)
    return pl.pallas_call(
        combine_kernel,
        out_shape=jax.ShapeDtypeStruct((rows, width), BF),
        in_specs=[pl.BlockSpec(memory_space=pltpu.SMEM)] + [hbm] * 5,
        out_specs=vmem,
        scratch_shapes=[pltpu.VMEM(o.shape, o.dtype) for o in operands]
        + [pltpu.SemaphoreType.DMA((8,))],
        compiler_params=pltpu.CompilerParams(vmem_limit_bytes=60 << 20),
        cost_estimate=pl.CostEstimate(
            flops=8 * rows * width * high.shape[1], bytes_accessed=7 << 20, transcendentals=0
        ),
        name="combine",
    )(core, *operands)


def page_pieces(keys, values, owner_all, tok_count, head_count, tok_index):
    pages_here = owner_all.shape[1]
    tok_rows = keys.shape[0]
    quarter_page = PAGE // head_count
    mine = lax.dynamic_index_in_dim(owner_all, tok_index, 0, keepdims=False)
    row = jnp.arange(tok_rows, dtype=jnp.int32)
    quarter = row // (tok_count * quarter_page)
    owner = row // quarter_page % tok_count
    line = quarter * quarter_page + row % quarter_page
    token_owner = jnp.repeat(mine, PAGE)
    token_line = jnp.arange(tok_rows, dtype=jnp.int32) % PAGE
    pick = (
        (owner[:, None] == token_owner[None, :]) & (line[:, None] == token_line[None, :])
    ).astype(BF)
    parts = [
        jnp.dot(pick, part, preferred_element_type=F32).astype(BF) for part in (keys, values)
    ]
    return jnp.concatenate(parts, 1).reshape(head_count * tok_count, quarter_page, -1)


def place_pages(landed, slots_all, owner_all, tok_count, head_count, tok_index):
    pages_here = owner_all.shape[1]
    quarter_page = PAGE // head_count
    rows = pages_here * quarter_page
    arrival = jnp.sum(jnp.where(owner_all == tok_index, slots_all % pages_here, 0), 1)
    row = jnp.arange(rows, dtype=jnp.int32)
    target = jnp.repeat(arrival, quarter_page) * quarter_page + row % quarter_page
    place = (row[:, None] == target[None, :]).astype(BF)
    landed = landed.reshape(head_count, rows, -1)
    width = landed.shape[2] // 2
    placed = [
        jnp.dot(place, landed[h], preferred_element_type=F32).astype(BF)
        for h in range(head_count)
    ]
    cache = jnp.concatenate(
        [p[:, :width] for p in placed] + [p[:, width:] for p in placed], 1
    )
    return cache.reshape(pages_here, quarter_page, 2 * head_count * width)


def per_device(
    hidden_in,
    queries,
    keys,
    values,
    request_ids,
    out_proj,
    norm_gain,
    expert_gate_up,
    expert_down,
    shared_gate_up,
    shared_down,
    shared_gate,
    routes,
    route_weights,
    page_slots,
):
    tok_rows, model_width = hidden_in.shape
    head_width = queries.shape[1]
    heads_here = head_width // HD
    tok_count = lax.axis_size("tok")
    head_count = lax.axis_size("head")
    tok_index = lax.axis_index("tok")
    head_index = lax.axis_index("head")
    core = head_index % CORES
    column_width = model_width // head_count
    rows_of_blocks = tok_count // ROW
    half = tok_rows // 2
    slots_core = CAP // CORES

    gate_up_own = jnp.transpose(expert_gate_up[0], (1, 2, 0))
    down_own = expert_down[0]
    out_peer = lax.ppermute(out_proj, "head", INTRA)
    gate_up_peer = lax.ppermute(gate_up_own, "head", INTRA)
    down_peer = lax.ppermute(down_own, "head", INTRA)

    place_in_row = tok_index % ROW
    own = []
    for step, part in enumerate(pack_heads(place_in_row.reshape(1), keys, values)):
        if step:
            part = lax.ppermute(
                part,
                "tok",
                [
                    (r * ROW + y, r * ROW + (y + step) % ROW)
                    for r in range(rows_of_blocks)
                    for y in range(ROW)
                ],
            )
        own.append(part)
    own = jnp.stack(own, 0)
    span = ROW * tok_rows
    base = (tok_index // ROW) * span
    padded_ids = jnp.concatenate([jnp.full((span,), -1, jnp.int32), request_ids], 0)
    window_ids = lax.dynamic_slice_in_dim(padded_ids, base, 2 * span, 0)
    ids_row = window_ids[None, :]
    queries, own = lax.optimization_barrier((queries, own))
    place_in_row = tok_index % ROW
    query_parts = []
    for step in range(ROW):
        target = (place_in_row + step) % ROW
        part = lax.dynamic_slice_in_dim(queries, target * HD, HD, 1)
        if step:
            part = lax.ppermute(
                part,
                "tok",
                [
                    (r * ROW + y, r * ROW + (y + step) % ROW)
                    for r in range(rows_of_blocks)
                    for y in range(ROW)
                ],
            )
        query_parts.append(part)
    slots_all = page_slots.reshape(tok_count, tok_rows // PAGE)
    owner_all = slots_all // (tok_rows // PAGE)
    pieces = page_pieces(keys, values, owner_all, tok_count, head_count, tok_index)
    past = lax.ppermute(
        own, "tok", [(s, s + ROW) for s in range(tok_count - ROW)]
    )
    attended = attention(
        place_in_row.reshape(1), ids_row, jnp.stack(query_parts, 0), own, past
    )

    core_groups = [
        [
            (chip * CORES + c) * tok_count + r * ROW + y
            for c in range(CORES)
            for y in range(ROW)
        ]
        for chip in range(CHIPS)
        for r in range(rows_of_blocks)
    ]
    gathered = lax.all_to_all(
        attended.reshape(CORES * ROW, half, HD),
        BOTH,
        split_axis=0,
        concat_axis=0,
        tiled=True,
        axis_index_groups=core_groups,
    ).reshape(CORES, ROW, half, HD)
    expert_ids = jnp.arange(EXPERTS, dtype=jnp.int32)
    named = routes[:, :, None] == expert_ids[None, None, :]
    onehot = jnp.sum(named.astype(F32), 1)
    weight_of = jnp.sum(jnp.where(named, route_weights[:, :, None], 0.0), 1)
    earlier = (
        jnp.arange(tok_rows, dtype=jnp.int32)[None, :] < jnp.arange(tok_rows, dtype=jnp.int32)[:, None]
    ).astype(BF)
    rank = jnp.dot(earlier, onehot.astype(BF), preferred_element_type=F32).astype(jnp.int32)
    rank = jnp.where(onehot > 0, rank, -1)
    rank_t = rank.T
    rank_rel = jnp.where(core == 0, rank_t, jnp.roll(rank_t, half, 1))
    place = jnp.arange(slots_core, dtype=jnp.int32) * CORES
    select = (rank_rel[:, None, :] == (place + core)[None, :, None]).astype(BF)
    select = select.reshape(EXPERTS * slots_core, tok_rows)
    core_ref = core.reshape(1)
    gathered, select, pieces = lax.optimization_barrier((gathered, select, pieces))
    projected_low = project(core_ref, gathered, out_proj, out_peer)
    projected_far = lax.ppermute(projected_low, "head", CROSS)
    pieces, _ = lax.optimization_barrier((pieces, projected_low))
    landed = lax.all_to_all(pieces, BOTH, split_axis=0, concat_axis=0, tiled=True)
    resid, normed_own = add_and_norm(
        core_ref, hidden_in, projected_low, projected_far, norm_gain[None, :]
    )
    normed_own, landed = lax.optimization_barrier((normed_own, landed))
    normed_peer = lax.ppermute(normed_own, "head", INTRA)

    outgoing = gather_rows(select, normed_own, normed_peer)
    rank, weight_of, _ = lax.optimization_barrier((rank, weight_of, outgoing))
    high = slot_weights(rank, weight_of, CORES * EXPERTS * slots_core)
    late_own, late_peer, _ = lax.optimization_barrier((normed_own, normed_peer, outgoing))
    normed_abs = jnp.where(
        core == 0,
        jnp.concatenate([late_own, late_peer], 0),
        jnp.concatenate([late_peer, late_own], 0),
    )
    arrived = lax.all_to_all(
        outgoing.reshape(tok_count, slots_core, model_width),
        "tok",
        split_axis=0,
        concat_axis=0,
        tiled=True,
    ).reshape(tok_count * slots_core, model_width)
    shared_both = jnp.einsum("td,dgf->tgf", normed_abs, shared_gate_up, preferred_element_type=F32)
    shared_act = (jax.nn.silu(shared_both[:, 0, :]) * shared_both[:, 1, :]).astype(BF)
    shared_scale = jax.nn.sigmoid(jnp.dot(normed_abs, shared_gate, preferred_element_type=F32))
    shared_term = shared_scale[:, None] * jnp.dot(
        shared_act, shared_down, preferred_element_type=F32
    )
    chip = head_index // CORES
    chip_width = CORES * column_width
    shared_near = lax.dynamic_slice_in_dim(shared_term, chip * chip_width, chip_width, 1)
    shared_send = lax.dynamic_slice_in_dim(
        shared_term, (1 - chip) * chip_width, chip_width, 1
    ).astype(BF)
    shared_near, shared_send, arrived = lax.optimization_barrier(
        (shared_near, shared_send, arrived)
    )
    shared_far = lax.ppermute(shared_send, "head", CROSS)

    partial = experts(arrived, gate_up_own, gate_up_peer, down_own, down_peer, head_count)
    partial = partial.reshape(head_count * tok_count, slots_core, column_width)
    partial, shared_far = lax.optimization_barrier((partial, shared_far))
    returned = lax.all_to_all(partial, BOTH, split_axis=0, concat_axis=0, tiled=True)
    returned = returned.reshape(CHIPS, CORES * EXPERTS * slots_core, column_width)

    shared_chip = shared_near + shared_far.astype(F32)
    shared_own = lax.dynamic_slice_in_dim(shared_chip, core * column_width, column_width, 1)
    shared_peer = lax.dynamic_slice_in_dim(
        shared_chip, (1 - core) * column_width, column_width, 1
    ).astype(BF)
    shared_cols = shared_own + lax.ppermute(shared_peer, "head", INTRA).astype(F32)
    own_cols = lax.dynamic_slice_in_dim(resid, head_index * column_width, column_width, 1)
    peer_cols = lax.dynamic_slice_in_dim(
        resid, (head_index + 1 - 2 * core) * column_width, column_width, 1
    )
    from_peer = lax.ppermute(peer_cols, "head", INTRA)
    layer_out = combine(core_ref, high, returned, own_cols, from_peer, shared_cols)
    decode_cache = place_pages(landed, slots_all, owner_all, tok_count, head_count, tok_index)
    return (layer_out, decode_cache)


def solution(mesh):
    in_specs = (
        P("tok", None),
        P("tok", "head"),
        P("tok", "head"),
        P("tok", "head"),
        P(),
        P("head", None),
        P(),
        P("tok", None, None, "head"),
        P("tok", "head", None),
        P(None, None, "head"),
        P("head", None),
        P(),
        P("tok", None),
        P("tok", None),
        P(),
    )
    out_specs = (P("tok", "head"), P("tok", "head", None))
    return jax.shard_map(
        per_device, mesh=mesh, in_specs=in_specs, out_specs=out_specs, check_vma=False
    )
```

```python
import math

import jax
import jax.numpy as jnp
from jax import lax
from jax.experimental import pallas as pl
from jax.experimental.pallas import tpu as pltpu
from jax.sharding import PartitionSpec as P

HD = 128
TOP = 4
EXPERTS = 32
PAGE = 8
CAP = 48
ROW = 4
CORES = 2
CHIPS = 2
BF = jnp.bfloat16
F32 = jnp.float32
BOTH = ("head", "tok")
INTRA = [(0, 1), (1, 0), (2, 3), (3, 2)]
CROSS = [(0, 2), (2, 0), (1, 3), (3, 1)]


def pack_kernel(place, keys, values, *outs):
    for step, out in enumerate(outs):
        head = lax.rem(place[0] + step, ROW)
        here = pl.ds(pl.multiple_of(head * HD, HD), HD)
        out[:, 0:HD] = keys[:, here]
        out[:, HD : 2 * HD] = values[:, here]


def pack_heads(place, keys, values):
    rows, width = keys.shape
    vmem = pl.BlockSpec(memory_space=pltpu.VMEM)
    heads = width // HD
    return pl.pallas_call(
        pack_kernel,
        out_shape=(jax.ShapeDtypeStruct((rows, 2 * HD), BF),) * heads,
        in_specs=[pl.BlockSpec(memory_space=pltpu.SMEM), vmem, vmem],
        out_specs=(vmem,) * heads,
        compiler_params=pltpu.CompilerParams(vmem_limit_bytes=60 << 20),
        cost_estimate=pl.CostEstimate(flops=0, bytes_accessed=1 << 20, transcendentals=0),
        name="pack_heads",
    )(place, keys, values)


def attention_kernel(
    place, ids_row_hbm, query_hbm, own_hbm, past_hbm, out_hbm,
    ids_row, query_parts, own, past, out, sems, out_sems,
):
    block = out.shape[2] * 2
    pairs = (
        (query_hbm, query_parts),
        (own_hbm, own),
        (past_hbm, past),
        (ids_row_hbm, ids_row),
    )
    copies = [
        pltpu.make_async_copy(source, target, sems.at[i])
        for i, (source, target) in enumerate(pairs)
    ]
    for copy in copies:
        copy.start()
    for copy in copies:
        copy.wait()
    stores = []

    def slot(b):
        return lax.rem(place[0] + (ROW - b), ROW)

    scale = 1.0 / math.sqrt(HD)
    span = ROW * block
    row_pos = lax.broadcasted_iota(jnp.int32, (block, block), 0)
    col_pos = lax.broadcasted_iota(jnp.int32, (block, block), 1)
    causal = col_pos <= row_pos
    same = col_pos == row_pos
    for y in range(ROW):
        query = query_parts[lax.rem(place[0] + (ROW - y), ROW)]
        row_ids = ids_row[0:1, pl.ds(span + y * block, block)]
        query_ids = jnp.sum(jnp.where(same, row_ids, 0), axis=1, keepdims=True)
        pieces = []
        for b in range(y, ROW):
            key = past[slot(b), :, 0:HD]
            key_ids = ids_row[0:1, pl.ds(b * block, block)]
            score = lax.dot_general(
                query, key, (((1,), (1,)), ((), ())), preferred_element_type=F32
            )
            pieces.append(jnp.where(query_ids == key_ids, score, -1e30))
        for b in range(y + 1):
            key = own[slot(b), :, 0:HD]
            key_ids = ids_row[0:1, pl.ds(span + b * block, block)]
            score = lax.dot_general(
                query, key, (((1,), (1,)), ((), ())), preferred_element_type=F32
            )
            allowed = query_ids == key_ids
            if b == y:
                allowed = allowed & causal
            pieces.append(jnp.where(allowed, score, -1e30))
        top = pieces[0].max(-1, keepdims=True)
        for piece in pieces[1:]:
            top = jnp.maximum(top, piece.max(-1, keepdims=True))
        weights = [jnp.exp((piece - top) * scale) for piece in pieces]
        total = weights[0].sum(-1, keepdims=True)
        for weight in weights[1:]:
            total = total + weight.sum(-1, keepdims=True)
        inverse = 1.0 / total
        mixed = jnp.zeros((block, HD), F32)
        index = 0
        for b in range(y, ROW):
            prob = weights[index].astype(BF)
            mixed += jnp.dot(prob, past[slot(b), :, HD : 2 * HD], preferred_element_type=F32)
            index += 1
        for b in range(y + 1):
            prob = weights[index].astype(BF)
            mixed += jnp.dot(prob, own[slot(b), :, HD : 2 * HD], preferred_element_type=F32)
            index += 1
        mixed = mixed * inverse
        half = block // 2
        out[0, y] = mixed[:half].astype(BF)
        out[1, y] = mixed[half:].astype(BF)
        for c in range(2):
            store = pltpu.make_async_copy(out.at[c, y], out_hbm.at[c, y], out_sems.at[c, y])
            store.start()
            stores.append(store)
    for store in stores:
        store.wait()


def attention(place, ids_row, query_parts, own, past):
    block = own.shape[1]
    hbm = pl.BlockSpec(memory_space=pltpu.HBM)
    operands = (ids_row, query_parts, own, past)
    result = jax.ShapeDtypeStruct((2, ROW, block // 2, HD), BF)
    return pl.pallas_call(
        attention_kernel,
        out_shape=result,
        in_specs=[pl.BlockSpec(memory_space=pltpu.SMEM)] + [hbm] * 4,
        out_specs=hbm,
        scratch_shapes=[pltpu.VMEM(o.shape, o.dtype) for o in operands]
        + [
            pltpu.VMEM(result.shape, BF),
            pltpu.SemaphoreType.DMA((4,)),
            pltpu.SemaphoreType.DMA((2, ROW)),
        ],
        compiler_params=pltpu.CompilerParams(vmem_limit_bytes=58 << 20),
        cost_estimate=pl.CostEstimate(
            flops=4 * 5 * ROW * block * block * HD,
            bytes_accessed=3 << 20,
            transcendentals=5 * ROW * block * block,
        ),
        name="row_attention",
    )(place, *operands)


def project_kernel(
    core, att_hbm, own_hbm, peer_hbm, low_hbm, att, own, peer, total_low, att_sem, sems, out_sems,
):
    width = total_low.shape[1]
    step = width // 4
    att_copy = pltpu.make_async_copy(att_hbm, att, att_sem)
    att_copy.start()
    copies = []
    for i in range(4):
        cols = pl.ds(i * step, step)
        copies.append(
            (
                pltpu.make_async_copy(own_hbm.at[:, cols], own.at[:, cols], sems.at[0, i]),
                pltpu.make_async_copy(peer_hbm.at[:, cols], peer.at[:, cols], sems.at[1, i]),
            )
        )
    for pair in copies:
        for copy in pair:
            copy.start()
    att_copy.wait()
    c = core[0]
    stores = []
    left = jnp.concatenate([att[c, y] for y in range(ROW)], 1)
    right = jnp.concatenate([att[1 - c, y] for y in range(ROW)], 1)
    for i in range(4):
        cols = pl.ds(i * step, step)
        for copy in copies[i]:
            copy.wait()
        part = jnp.dot(left, own[:, cols], preferred_element_type=F32) + jnp.dot(
            right, peer[:, cols], preferred_element_type=F32
        )
        total_low[:, cols] = part.astype(BF)
        store = pltpu.make_async_copy(total_low.at[:, cols], low_hbm.at[:, cols], out_sems.at[i])
        store.start()
        stores.append(store)
    for store in stores:
        store.wait()


def project(core, att, out_own, out_peer):
    rows = att.shape[2]
    depth, width = out_own.shape
    hbm = pl.BlockSpec(memory_space=pltpu.HBM)
    return pl.pallas_call(
        project_kernel,
        out_shape=jax.ShapeDtypeStruct((rows, width), BF),
        in_specs=[pl.BlockSpec(memory_space=pltpu.SMEM), hbm, hbm, hbm],
        out_specs=hbm,
        scratch_shapes=[
            pltpu.VMEM(att.shape, BF),
            pltpu.VMEM((depth, width), BF),
            pltpu.VMEM((depth, width), BF),
            pltpu.VMEM((rows, width), BF),
            pltpu.SemaphoreType.DMA,
            pltpu.SemaphoreType.DMA((2, 4)),
            pltpu.SemaphoreType.DMA((4,)),
        ],
        compiler_params=pltpu.CompilerParams(vmem_limit_bytes=58 << 20),
        cost_estimate=pl.CostEstimate(
            flops=4 * rows * depth * width, bytes_accessed=6 << 20, transcendentals=0
        ),
        name="project",
    )(core, att, out_own, out_peer)


def norm_kernel(
    core, hidden_hbm, near_hbm, far_hbm, gain_hbm, resid_hbm, normed_hbm,
    hidden, near, far, gain, resid, normed, sems, out_sems,
):
    rows = near.shape[0]
    parts = 2
    block = rows // parts
    start = pl.multiple_of(core[0] * rows, rows)
    gain_copy = pltpu.make_async_copy(gain_hbm, gain, sems.at[3, 0])
    gain_copy.start()
    copies = []
    for i in range(parts):
        here = pl.ds(i * block, block)
        copies.append(
            [
                pltpu.make_async_copy(near_hbm.at[here], near.at[here], sems.at[0, i]),
                pltpu.make_async_copy(far_hbm.at[here], far.at[here], sems.at[1, i]),
                pltpu.make_async_copy(
                    hidden_hbm.at[pl.ds(start + i * block, block)], hidden.at[here], sems.at[2, i]
                ),
            ]
        )
        for copy in copies[i]:
            copy.start()
    gain_copy.wait()
    stores = []
    for i in range(parts):
        here = pl.ds(i * block, block)
        for copy in copies[i]:
            copy.wait()
        value = hidden[here, :].astype(F32) + (
            near[here, :].astype(F32) + far[here, :].astype(F32)
        )
        mean_square = jnp.mean(value * value, axis=-1, keepdims=True)
        normed[here, :] = (value * lax.rsqrt(mean_square + 1e-06) * gain[...]).astype(BF)
        resid[here, :] = value
        for j, (source, target) in enumerate(((normed, normed_hbm), (resid, resid_hbm))):
            store = pltpu.make_async_copy(source.at[here], target.at[here], out_sems.at[j, i])
            store.start()
            stores.append(store)
    for store in stores:
        store.wait()


def add_and_norm(core, hidden, near, far, gain):
    rows, width = near.shape
    hbm = pl.BlockSpec(memory_space=pltpu.HBM)
    return pl.pallas_call(
        norm_kernel,
        out_shape=(
            jax.ShapeDtypeStruct((rows, width), F32),
            jax.ShapeDtypeStruct((rows, width), BF),
        ),
        in_specs=[pl.BlockSpec(memory_space=pltpu.SMEM), hbm, hbm, hbm, hbm],
        out_specs=(hbm, hbm),
        scratch_shapes=[
            pltpu.VMEM((rows, width), BF),
            pltpu.VMEM((rows, width), BF),
            pltpu.VMEM((rows, width), BF),
            pltpu.VMEM((1, width), F32),
            pltpu.VMEM((rows, width), F32),
            pltpu.VMEM((rows, width), BF),
            pltpu.SemaphoreType.DMA((4, 2)),
            pltpu.SemaphoreType.DMA((2, 2)),
        ],
        compiler_params=pltpu.CompilerParams(vmem_limit_bytes=58 << 20),
        cost_estimate=pl.CostEstimate(
            flops=8 * rows * width, bytes_accessed=4 << 20, transcendentals=rows
        ),
        name="add_and_norm",
    )(core, hidden, near, far, gain)


def gather_kernel(
    select_hbm, own_hbm, peer_hbm, out_hbm, select, rows, out, sems, out_sems
):
    half = rows.shape[0] // 2
    total, block = out.shape[0], out.shape[0] // 3
    copies = [
        pltpu.make_async_copy(own_hbm, rows.at[pl.ds(0, half)], sems.at[0]),
        pltpu.make_async_copy(peer_hbm, rows.at[pl.ds(half, half)], sems.at[1]),
        pltpu.make_async_copy(select_hbm, select, sems.at[2]),
    ]
    for copy in copies:
        copy.start()
    for copy in copies:
        copy.wait()
    stores = []
    for i in range(total // block):
        here = pl.ds(i * block, block)
        out[here, :] = jnp.dot(
            select[here, :], rows[...], preferred_element_type=F32
        ).astype(BF)
        store = pltpu.make_async_copy(out.at[here], out_hbm.at[here], out_sems.at[i])
        store.start()
        stores.append(store)
    for store in stores:
        store.wait()


def gather_rows(select, own, peer):
    slots, rows = select.shape
    width = own.shape[1]
    hbm = pl.BlockSpec(memory_space=pltpu.HBM)
    return pl.pallas_call(
        gather_kernel,
        out_shape=jax.ShapeDtypeStruct((slots, width), BF),
        in_specs=[hbm, hbm, hbm],
        out_specs=hbm,
        scratch_shapes=[
            pltpu.VMEM((slots, rows), BF),
            pltpu.VMEM((rows, width), BF),
            pltpu.VMEM((slots, width), BF),
            pltpu.SemaphoreType.DMA((3,)),
            pltpu.SemaphoreType.DMA((3,)),
        ],
        compiler_params=pltpu.CompilerParams(vmem_limit_bytes=58 << 20),
        cost_estimate=pl.CostEstimate(
            flops=2 * slots * rows * width, bytes_accessed=5 << 20, transcendentals=0
        ),
        name="gather_rows",
    )(select, own, peer)


def slot_weight_kernel(rank, weight, high):
    slots = high.shape[1]
    per_core = CAP // CORES
    experts_here = rank.shape[1]
    lane = lax.broadcasted_iota(jnp.int32, (1, slots), 1)
    expert_of = lax.rem(lax.div(lane, per_core), experts_here)
    wanted = lax.rem(lane, per_core) * CORES + lax.div(lane, per_core * experts_here)
    expand = (
        lax.broadcasted_iota(jnp.int32, (experts_here, slots), 0) == expert_of
    ).astype(BF)
    ranks = jnp.dot(rank[...].astype(BF), expand, preferred_element_type=F32)
    hit = ranks.astype(jnp.int32) == wanted
    spread = jnp.dot(weight[...].astype(BF), expand, preferred_element_type=F32)
    high[...] = jnp.where(hit, spread, 0.0).astype(BF)


def slot_weights(rank, weight, slots):
    rows = rank.shape[0]
    vmem = pl.BlockSpec(memory_space=pltpu.VMEM)
    shape = jax.ShapeDtypeStruct((rows, slots), BF)
    return pl.pallas_call(
        slot_weight_kernel,
        out_shape=shape,
        in_specs=[vmem, vmem],
        out_specs=vmem,
        compiler_params=pltpu.CompilerParams(vmem_limit_bytes=16 << 20),
        cost_estimate=pl.CostEstimate(
            flops=6 * rows * slots * 32, bytes_accessed=2 << 20, transcendentals=0
        ),
        name="slot_weights",
    )(rank, weight)


def expert_kernel(
    x_hbm, both_own, both_peer, down_own, down_peer, out_hbm,
    x, gate, up, down, act, out, x_sems, sems, down_sems, out_sems,
):
    hidden = both_own.shape[1]
    rows = x.shape[0]
    groups, _, width = out.shape
    parts = 3
    block = rows // parts
    step = 256
    bounds = [(lo, min(lo + step, 2 * hidden)) for lo in range(0, 2 * hidden, step)]
    x_copies = [
        pltpu.make_async_copy(
            x_hbm.at[pl.ds(m * block, block)], x.at[pl.ds(m * block, block)], x_sems.at[m]
        )
        for m in range(parts)
    ]
    chunks = []
    for n, (lo, hi) in enumerate(bounds):
        copies = []
        for j, (source, start, stop) in enumerate(
            (
                (both_own, lo, min(hi, hidden)),
                (both_peer, max(lo, hidden) - hidden, hi - hidden),
            )
        ):
            if stop <= start:
                continue
            shift = hidden * j
            for k, target in enumerate((gate, up)):
                copies.append(
                    pltpu.make_async_copy(
                        source.at[k, pl.ds(start, stop - start)],
                        target.at[pl.ds(start + shift, stop - start)],
                        sems.at[n, j, k],
                    )
                )
        chunks.append(copies)
    down_copies = [
        pltpu.make_async_copy(source, down.at[pl.ds(j * hidden, hidden)], down_sems.at[j])
        for j, source in enumerate((down_own, down_peer))
    ]
    def begin(copies):
        for copy in copies:
            copy.start()

    def finish(copies):
        for copy in copies:
            copy.wait()

    def halves(n, start, count):
        lo, hi = bounds[n]
        here = pl.ds(start * block, count * block)
        left = x[here, :]
        g = lax.dot_general(left, gate[lo:hi, :], contract, preferred_element_type=F32)
        u = lax.dot_general(left, up[lo:hi, :], contract, preferred_element_type=F32)
        act[here, lo:hi] = (g / (1.0 + jnp.exp(-g)) * u).astype(BF)

    contract = (((1,), (1,)), ((), ()))
    begin([x_copies[0]] + chunks[0])
    begin(x_copies[1:])
    finish([x_copies[0]] + chunks[0])
    begin(chunks[1])
    halves(0, 0, 1)
    finish(x_copies[1:])
    begin(chunks[2])
    halves(0, 1, parts - 1)
    finish(chunks[1])
    begin(down_copies)
    halves(1, 0, parts)
    finish(chunks[2])
    halves(2, 0, parts)
    finish(down_copies)
    stores = []
    for i in range(groups):
        result = jnp.dot(
            act[...], down[:, i * width : (i + 1) * width], preferred_element_type=F32
        )
        out[i] = result.astype(BF)
        store = pltpu.make_async_copy(out.at[i], out_hbm.at[i], out_sems.at[i])
        store.start()
        stores.append(store)
    for store in stores:
        store.wait()


def experts(x, both_own, both_peer, down_own, down_peer, groups):
    rows, depth = x.shape
    hidden, width = down_own.shape
    column_width = width // groups
    hbm = pl.BlockSpec(memory_space=pltpu.HBM)
    return pl.pallas_call(
        expert_kernel,
        out_shape=jax.ShapeDtypeStruct((groups, rows, column_width), BF),
        in_specs=[hbm] * 5,
        out_specs=hbm,
        scratch_shapes=[
            pltpu.VMEM((rows, depth), BF),
            pltpu.VMEM((2 * hidden, depth), BF),
            pltpu.VMEM((2 * hidden, depth), BF),
            pltpu.VMEM((2 * hidden, width), BF),
            pltpu.VMEM((rows, 2 * hidden), BF),
            pltpu.VMEM((groups, rows, column_width), BF),
            pltpu.SemaphoreType.DMA((3,)),
            pltpu.SemaphoreType.DMA((pl.cdiv(2 * hidden, 256), 2, 2)),
            pltpu.SemaphoreType.DMA((2,)),
            pltpu.SemaphoreType.DMA((groups,)),
        ],
        compiler_params=pltpu.CompilerParams(vmem_limit_bytes=60 << 20),
        cost_estimate=pl.CostEstimate(
            flops=12 * rows * depth * hidden,
            bytes_accessed=15 << 20,
            transcendentals=2 * rows * hidden,
        ),
        name="experts",
    )(x, both_own, both_peer, down_own, down_peer)


def combine_kernel(
    core, high_hbm, back_hbm, mine_hbm, peers_hbm, shared_hbm, out,
    high, back, mine, peers, shared, sems,
):
    rows = mine.shape[0]
    chips, depth = back.shape[0], back.shape[1]
    block = depth // CORES
    pieces = [(chip, pl.ds(c * block, block)) for chip in range(chips) for c in range(CORES)]
    copies = [
        pltpu.make_async_copy(back_hbm.at[chip, here], back.at[chip, here], sems.at[i])
        for i, (chip, here) in enumerate(pieces)
    ]
    rest = [
        pltpu.make_async_copy(source, target, sems.at[len(pieces) + i])
        for i, (source, target) in enumerate(
            (
                (high_hbm, high),
                (shared_hbm, shared),
                (mine_hbm, mine),
                (peers_hbm, peers),
            )
        )
    ]
    for copy in [rest[0]] + copies + rest[1:]:
        copy.start()
    total = None
    for i, (copy, (chip, here)) in enumerate(zip(copies, pieces)):
        if i == 0:
            rest[0].wait()
        copy.wait()
        part = jnp.dot(high[:, here], back[chip, here], preferred_element_type=F32)
        total = part if total is None else total + part
    for copy in rest[1:]:
        copy.wait()
    total += shared[...]
    first = core[0] == 0
    low_half = jnp.where(first, mine[...], peers[...])
    high_half = jnp.where(first, peers[...], mine[...])
    out[0:rows, :] = (total[0:rows] + low_half).astype(BF)
    out[rows : 2 * rows, :] = (total[rows:] + high_half).astype(BF)


def combine(core, high, returned, mine, peers, shared):
    hbm = pl.BlockSpec(memory_space=pltpu.HBM)
    vmem = pl.BlockSpec(memory_space=pltpu.VMEM)
    rows, width = shared.shape
    operands = (high, returned, mine, peers, shared)
    return pl.pallas_call(
        combine_kernel,
        out_shape=jax.ShapeDtypeStruct((rows, width), BF),
        in_specs=[pl.BlockSpec(memory_space=pltpu.SMEM)] + [hbm] * 5,
        out_specs=vmem,
        scratch_shapes=[pltpu.VMEM(o.shape, o.dtype) for o in operands]
        + [pltpu.SemaphoreType.DMA((8,))],
        compiler_params=pltpu.CompilerParams(vmem_limit_bytes=60 << 20),
        cost_estimate=pl.CostEstimate(
            flops=8 * rows * width * high.shape[1], bytes_accessed=7 << 20, transcendentals=0
        ),
        name="combine",
    )(core, *operands)


def page_pieces(keys, values, owner_all, tok_count, head_count, tok_index):
    pages_here = owner_all.shape[1]
    tok_rows = keys.shape[0]
    quarter_page = PAGE // head_count
    mine = lax.dynamic_index_in_dim(owner_all, tok_index, 0, keepdims=False)
    row = jnp.arange(tok_rows, dtype=jnp.int32)
    quarter = row // (tok_count * quarter_page)
    owner = row // quarter_page % tok_count
    line = quarter * quarter_page + row % quarter_page
    token_owner = jnp.repeat(mine, PAGE)
    token_line = jnp.arange(tok_rows, dtype=jnp.int32) % PAGE
    pick = (
        (owner[:, None] == token_owner[None, :]) & (line[:, None] == token_line[None, :])
    ).astype(BF)
    parts = [
        jnp.dot(pick, part, preferred_element_type=F32).astype(BF) for part in (keys, values)
    ]
    return jnp.concatenate(parts, 1).reshape(head_count * tok_count, quarter_page, -1)


def place_pages(landed, slots_all, owner_all, tok_count, head_count, tok_index):
    pages_here = owner_all.shape[1]
    quarter_page = PAGE // head_count
    rows = pages_here * quarter_page
    arrival = jnp.sum(jnp.where(owner_all == tok_index, slots_all % pages_here, 0), 1)
    row = jnp.arange(rows, dtype=jnp.int32)
    target = jnp.repeat(arrival, quarter_page) * quarter_page + row % quarter_page
    place = (row[:, None] == target[None, :]).astype(BF)
    landed = landed.reshape(head_count, rows, -1)
    width = landed.shape[2] // 2
    placed = [
        jnp.dot(place, landed[h], preferred_element_type=F32).astype(BF)
        for h in range(head_count)
    ]
    cache = jnp.concatenate(
        [p[:, :width] for p in placed] + [p[:, width:] for p in placed], 1
    )
    return cache.reshape(pages_here, quarter_page, 2 * head_count * width)


def per_device(
    hidden_in,
    queries,
    keys,
    values,
    request_ids,
    out_proj,
    norm_gain,
    expert_gate_up,
    expert_down,
    shared_gate_up,
    shared_down,
    shared_gate,
    routes,
    route_weights,
    page_slots,
):
    tok_rows, model_width = hidden_in.shape
    head_width = queries.shape[1]
    heads_here = head_width // HD
    tok_count = lax.axis_size("tok")
    head_count = lax.axis_size("head")
    tok_index = lax.axis_index("tok")
    head_index = lax.axis_index("head")
    core = head_index % CORES
    column_width = model_width // head_count
    rows_of_blocks = tok_count // ROW
    half = tok_rows // 2
    slots_core = CAP // CORES

    gate_up_own = jnp.transpose(expert_gate_up[0], (1, 2, 0))
    down_own = expert_down[0]
    out_peer = lax.ppermute(out_proj, "head", INTRA)
    gate_up_peer = lax.ppermute(gate_up_own, "head", INTRA)
    down_peer = lax.ppermute(down_own, "head", INTRA)

    place_in_row = tok_index % ROW
    own = []
    for step, part in enumerate(pack_heads(place_in_row.reshape(1), keys, values)):
        if step:
            part = lax.ppermute(
                part,
                "tok",
                [
                    (r * ROW + y, r * ROW + (y + step) % ROW)
                    for r in range(rows_of_blocks)
                    for y in range(ROW)
                ],
            )
        own.append(part)
    own = jnp.stack(own, 0)
    span = ROW * tok_rows
    base = (tok_index // ROW) * span
    padded_ids = jnp.concatenate([jnp.full((span,), -1, jnp.int32), request_ids], 0)
    window_ids = lax.dynamic_slice_in_dim(padded_ids, base, 2 * span, 0)
    ids_row = window_ids[None, :]
    queries, own, page_keys, page_values = lax.optimization_barrier((queries, own, keys, values))
    place_in_row = tok_index % ROW
    query_parts = []
    for step in range(ROW):
        target = (place_in_row + step) % ROW
        part = lax.dynamic_slice_in_dim(queries, target * HD, HD, 1)
        if step:
            part = lax.ppermute(
                part,
                "tok",
                [
                    (r * ROW + y, r * ROW + (y + step) % ROW)
                    for r in range(rows_of_blocks)
                    for y in range(ROW)
                ],
            )
        query_parts.append(part)
    slots_all = page_slots.reshape(tok_count, tok_rows // PAGE)
    owner_all = slots_all // (tok_rows // PAGE)
    pieces = page_pieces(page_keys, page_values, owner_all, tok_count, head_count, tok_index)
    past = lax.ppermute(
        own, "tok", [(s, s + ROW) for s in range(tok_count - ROW)]
    )
    attended = attention(
        place_in_row.reshape(1), ids_row, jnp.stack(query_parts, 0), own, past
    )

    core_groups = [
        [
            (chip * CORES + c) * tok_count + r * ROW + y
            for c in range(CORES)
            for y in range(ROW)
        ]
        for chip in range(CHIPS)
        for r in range(rows_of_blocks)
    ]
    gathered = lax.all_to_all(
        attended.reshape(CORES * ROW, half, HD),
        BOTH,
        split_axis=0,
        concat_axis=0,
        tiled=True,
        axis_index_groups=core_groups,
    ).reshape(CORES, ROW, half, HD)
    expert_ids = jnp.arange(EXPERTS, dtype=jnp.int32)
    named = routes[:, :, None] == expert_ids[None, None, :]
    onehot = jnp.sum(named.astype(F32), 1)
    weight_of = jnp.sum(jnp.where(named, route_weights[:, :, None], 0.0), 1)
    earlier = (
        jnp.arange(tok_rows, dtype=jnp.int32)[None, :] < jnp.arange(tok_rows, dtype=jnp.int32)[:, None]
    ).astype(BF)
    rank = jnp.dot(earlier, onehot.astype(BF), preferred_element_type=F32).astype(jnp.int32)
    rank = jnp.where(onehot > 0, rank, -1)
    rank_t = rank.T
    rank_rel = jnp.where(core == 0, rank_t, jnp.roll(rank_t, half, 1))
    place = jnp.arange(slots_core, dtype=jnp.int32) * CORES
    select = (rank_rel[:, None, :] == (place + core)[None, :, None]).astype(BF)
    select = select.reshape(EXPERTS * slots_core, tok_rows)
    core_ref = core.reshape(1)
    gathered, select, pieces = lax.optimization_barrier((gathered, select, pieces))
    projected_low = project(core_ref, gathered, out_proj, out_peer)
    projected_far = lax.ppermute(projected_low, "head", CROSS)
    pieces, _ = lax.optimization_barrier((pieces, projected_low))
    landed = lax.all_to_all(pieces, BOTH, split_axis=0, concat_axis=0, tiled=True)
    resid, normed_own = add_and_norm(
        core_ref, hidden_in, projected_low, projected_far, norm_gain[None, :]
    )
    normed_own, landed = lax.optimization_barrier((normed_own, landed))
    normed_peer = lax.ppermute(normed_own, "head", INTRA)

    outgoing = gather_rows(select, normed_own, normed_peer)
    rank, weight_of, _ = lax.optimization_barrier((rank, weight_of, outgoing))
    high = slot_weights(rank, weight_of, CORES * EXPERTS * slots_core)
    late_own, late_peer, _ = lax.optimization_barrier((normed_own, normed_peer, outgoing))
    normed_abs = jnp.where(
        core == 0,
        jnp.concatenate([late_own, late_peer], 0),
        jnp.concatenate([late_peer, late_own], 0),
    )
    arrived = lax.all_to_all(
        outgoing.reshape(tok_count, slots_core, model_width),
        "tok",
        split_axis=0,
        concat_axis=0,
        tiled=True,
    ).reshape(tok_count * slots_core, model_width)
    shared_both = jnp.einsum("td,dgf->tgf", normed_abs, shared_gate_up, preferred_element_type=F32)
    shared_act = (jax.nn.silu(shared_both[:, 0, :]) * shared_both[:, 1, :]).astype(BF)
    shared_scale = jax.nn.sigmoid(jnp.dot(normed_abs, shared_gate, preferred_element_type=F32))
    shared_term = shared_scale[:, None] * jnp.dot(
        shared_act, shared_down, preferred_element_type=F32
    )
    chip = head_index // CORES
    chip_width = CORES * column_width
    shared_near = lax.dynamic_slice_in_dim(shared_term, chip * chip_width, chip_width, 1)
    shared_send = lax.dynamic_slice_in_dim(
        shared_term, (1 - chip) * chip_width, chip_width, 1
    ).astype(BF)
    shared_near, shared_send, arrived = lax.optimization_barrier(
        (shared_near, shared_send, arrived)
    )
    shared_far = lax.ppermute(shared_send, "head", CROSS)

    partial = experts(arrived, gate_up_own, gate_up_peer, down_own, down_peer, head_count)
    partial = partial.reshape(head_count * tok_count, slots_core, column_width)
    partial, shared_far = lax.optimization_barrier((partial, shared_far))
    returned = lax.all_to_all(partial, BOTH, split_axis=0, concat_axis=0, tiled=True)
    returned = returned.reshape(CHIPS, CORES * EXPERTS * slots_core, column_width)

    shared_chip = shared_near + shared_far.astype(F32)
    shared_own = lax.dynamic_slice_in_dim(shared_chip, core * column_width, column_width, 1)
    shared_peer = lax.dynamic_slice_in_dim(
        shared_chip, (1 - core) * column_width, column_width, 1
    ).astype(BF)
    shared_cols = shared_own + lax.ppermute(shared_peer, "head", INTRA).astype(F32)
    own_cols = lax.dynamic_slice_in_dim(resid, head_index * column_width, column_width, 1)
    peer_cols = lax.dynamic_slice_in_dim(
        resid, (head_index + 1 - 2 * core) * column_width, column_width, 1
    )
    from_peer = lax.ppermute(peer_cols, "head", INTRA)
    layer_out = combine(core_ref, high, returned, own_cols, from_peer, shared_cols)
    decode_cache = place_pages(landed, slots_all, owner_all, tok_count, head_count, tok_index)
    return (layer_out, decode_cache)


def solution(mesh):
    in_specs = (
        P("tok", None),
        P("tok", "head"),
        P("tok", "head"),
        P("tok", "head"),
        P(),
        P("head", None),
        P(),
        P("tok", None, None, "head"),
        P("tok", "head", None),
        P(None, None, "head"),
        P("head", None),
        P(),
        P("tok", None),
        P("tok", None),
        P(),
    )
    out_specs = (P("tok", "head"), P("tok", "head", None))
    return jax.shard_map(
        per_device, mesh=mesh, in_specs=in_specs, out_specs=out_specs, check_vma=False
    )
```

```python
import math

import jax
import jax.numpy as jnp
from jax import lax
from jax.experimental import pallas as pl
from jax.experimental.pallas import tpu as pltpu
from jax.sharding import PartitionSpec as P

HD = 128
TOP = 4
EXPERTS = 32
PAGE = 8
CAP = 48
ROW = 4
CORES = 2
CHIPS = 2
BF = jnp.bfloat16
F32 = jnp.float32
BOTH = ("head", "tok")
INTRA = [(0, 1), (1, 0), (2, 3), (3, 2)]
CROSS = [(0, 2), (2, 0), (1, 3), (3, 1)]


def pack_kernel(place, keys, values, *outs):
    for step, out in enumerate(outs):
        head = lax.rem(place[0] + step, ROW)
        here = pl.ds(pl.multiple_of(head * HD, HD), HD)
        out[:, 0:HD] = keys[:, here]
        out[:, HD : 2 * HD] = values[:, here]


def pack_heads(place, keys, values):
    rows, width = keys.shape
    vmem = pl.BlockSpec(memory_space=pltpu.VMEM)
    heads = width // HD
    return pl.pallas_call(
        pack_kernel,
        out_shape=(jax.ShapeDtypeStruct((rows, 2 * HD), BF),) * heads,
        in_specs=[pl.BlockSpec(memory_space=pltpu.SMEM), vmem, vmem],
        out_specs=(vmem,) * heads,
        compiler_params=pltpu.CompilerParams(vmem_limit_bytes=60 << 20),
        cost_estimate=pl.CostEstimate(flops=0, bytes_accessed=1 << 20, transcendentals=0),
        name="pack_heads",
    )(place, keys, values)


def attention_kernel(
    place, ids_row_hbm, query_hbm, own_hbm, past_hbm, out_hbm,
    ids_row, query_parts, own, past, out, sems, out_sems,
):
    block = out.shape[2] * 2
    pairs = (
        (query_hbm, query_parts),
        (own_hbm, own),
        (past_hbm, past),
        (ids_row_hbm, ids_row),
    )
    copies = [
        pltpu.make_async_copy(source, target, sems.at[i])
        for i, (source, target) in enumerate(pairs)
    ]
    for copy in copies:
        copy.start()
    for copy in copies:
        copy.wait()
    stores = []

    def slot(b):
        return lax.rem(place[0] + (ROW - b), ROW)

    scale = 1.0 / math.sqrt(HD)
    span = ROW * block
    row_pos = lax.broadcasted_iota(jnp.int32, (block, block), 0)
    col_pos = lax.broadcasted_iota(jnp.int32, (block, block), 1)
    causal = col_pos <= row_pos
    same = col_pos == row_pos
    for y in range(ROW):
        query = query_parts[lax.rem(place[0] + (ROW - y), ROW)]
        row_ids = ids_row[0:1, pl.ds(span + y * block, block)]
        query_ids = jnp.sum(jnp.where(same, row_ids, 0), axis=1, keepdims=True)
        pieces = []
        for b in range(y, ROW):
            key = past[slot(b), :, 0:HD]
            key_ids = ids_row[0:1, pl.ds(b * block, block)]
            score = lax.dot_general(
                query, key, (((1,), (1,)), ((), ())), preferred_element_type=F32
            )
            pieces.append(jnp.where(query_ids == key_ids, score, -1e30))
        for b in range(y + 1):
            key = own[slot(b), :, 0:HD]
            key_ids = ids_row[0:1, pl.ds(span + b * block, block)]
            score = lax.dot_general(
                query, key, (((1,), (1,)), ((), ())), preferred_element_type=F32
            )
            allowed = query_ids == key_ids
            if b == y:
                allowed = allowed & causal
            pieces.append(jnp.where(allowed, score, -1e30))
        top = pieces[0].max(-1, keepdims=True)
        for piece in pieces[1:]:
            top = jnp.maximum(top, piece.max(-1, keepdims=True))
        weights = [jnp.exp((piece - top) * scale) for piece in pieces]
        total = weights[0].sum(-1, keepdims=True)
        for weight in weights[1:]:
            total = total + weight.sum(-1, keepdims=True)
        inverse = 1.0 / total
        mixed = jnp.zeros((block, HD), F32)
        index = 0
        for b in range(y, ROW):
            prob = weights[index].astype(BF)
            mixed += jnp.dot(prob, past[slot(b), :, HD : 2 * HD], preferred_element_type=F32)
            index += 1
        for b in range(y + 1):
            prob = weights[index].astype(BF)
            mixed += jnp.dot(prob, own[slot(b), :, HD : 2 * HD], preferred_element_type=F32)
            index += 1
        mixed = mixed * inverse
        half = block // 2
        out[0, y] = mixed[:half].astype(BF)
        out[1, y] = mixed[half:].astype(BF)
        for c in range(2):
            store = pltpu.make_async_copy(out.at[c, y], out_hbm.at[c, y], out_sems.at[c, y])
            store.start()
            stores.append(store)
    for store in stores:
        store.wait()


def attention(place, ids_row, query_parts, own, past):
    block = own.shape[1]
    hbm = pl.BlockSpec(memory_space=pltpu.HBM)
    operands = (ids_row, query_parts, own, past)
    result = jax.ShapeDtypeStruct((2, ROW, block // 2, HD), BF)
    return pl.pallas_call(
        attention_kernel,
        out_shape=result,
        in_specs=[pl.BlockSpec(memory_space=pltpu.SMEM)] + [hbm] * 4,
        out_specs=hbm,
        scratch_shapes=[pltpu.VMEM(o.shape, o.dtype) for o in operands]
        + [
            pltpu.VMEM(result.shape, BF),
            pltpu.SemaphoreType.DMA((4,)),
            pltpu.SemaphoreType.DMA((2, ROW)),
        ],
        compiler_params=pltpu.CompilerParams(vmem_limit_bytes=58 << 20),
        cost_estimate=pl.CostEstimate(
            flops=4 * 5 * ROW * block * block * HD,
            bytes_accessed=3 << 20,
            transcendentals=5 * ROW * block * block,
        ),
        name="row_attention",
    )(place, *operands)


def project_kernel(
    core, att_hbm, own_hbm, peer_hbm, low_hbm, att, own, peer, total_low, att_sem, sems, out_sems,
):
    width = total_low.shape[1]
    step = width // 4
    att_copy = pltpu.make_async_copy(att_hbm, att, att_sem)
    att_copy.start()
    copies = []
    for i in range(4):
        cols = pl.ds(i * step, step)
        copies.append(
            (
                pltpu.make_async_copy(own_hbm.at[:, cols], own.at[:, cols], sems.at[0, i]),
                pltpu.make_async_copy(peer_hbm.at[:, cols], peer.at[:, cols], sems.at[1, i]),
            )
        )
    for pair in copies:
        for copy in pair:
            copy.start()
    att_copy.wait()
    c = core[0]
    stores = []
    left = jnp.concatenate([att[c, y] for y in range(ROW)], 1)
    right = jnp.concatenate([att[1 - c, y] for y in range(ROW)], 1)
    for i in range(4):
        cols = pl.ds(i * step, step)
        for copy in copies[i]:
            copy.wait()
        part = jnp.dot(left, own[:, cols], preferred_element_type=F32) + jnp.dot(
            right, peer[:, cols], preferred_element_type=F32
        )
        total_low[:, cols] = part.astype(BF)
        store = pltpu.make_async_copy(total_low.at[:, cols], low_hbm.at[:, cols], out_sems.at[i])
        store.start()
        stores.append(store)
    for store in stores:
        store.wait()


def project(core, att, out_own, out_peer):
    rows = att.shape[2]
    depth, width = out_own.shape
    hbm = pl.BlockSpec(memory_space=pltpu.HBM)
    return pl.pallas_call(
        project_kernel,
        out_shape=jax.ShapeDtypeStruct((rows, width), BF),
        in_specs=[pl.BlockSpec(memory_space=pltpu.SMEM), hbm, hbm, hbm],
        out_specs=hbm,
        scratch_shapes=[
            pltpu.VMEM(att.shape, BF),
            pltpu.VMEM((depth, width), BF),
            pltpu.VMEM((depth, width), BF),
            pltpu.VMEM((rows, width), BF),
            pltpu.SemaphoreType.DMA,
            pltpu.SemaphoreType.DMA((2, 4)),
            pltpu.SemaphoreType.DMA((4,)),
        ],
        compiler_params=pltpu.CompilerParams(vmem_limit_bytes=58 << 20),
        cost_estimate=pl.CostEstimate(
            flops=4 * rows * depth * width, bytes_accessed=6 << 20, transcendentals=0
        ),
        name="project",
    )(core, att, out_own, out_peer)


def norm_kernel(
    core, hidden_hbm, near_hbm, far_hbm, gain_hbm, resid_hbm, normed_hbm,
    hidden, near, far, gain, resid, normed, sems, out_sems,
):
    rows = near.shape[0]
    parts = 2
    block = rows // parts
    start = pl.multiple_of(core[0] * rows, rows)
    gain_copy = pltpu.make_async_copy(gain_hbm, gain, sems.at[3, 0])
    gain_copy.start()
    copies = []
    for i in range(parts):
        here = pl.ds(i * block, block)
        copies.append(
            [
                pltpu.make_async_copy(near_hbm.at[here], near.at[here], sems.at[0, i]),
                pltpu.make_async_copy(far_hbm.at[here], far.at[here], sems.at[1, i]),
                pltpu.make_async_copy(
                    hidden_hbm.at[pl.ds(start + i * block, block)], hidden.at[here], sems.at[2, i]
                ),
            ]
        )
        for copy in copies[i]:
            copy.start()
    gain_copy.wait()
    stores = []
    for i in range(parts):
        here = pl.ds(i * block, block)
        for copy in copies[i]:
            copy.wait()
        value = hidden[here, :].astype(F32) + (
            near[here, :].astype(F32) + far[here, :].astype(F32)
        )
        mean_square = jnp.mean(value * value, axis=-1, keepdims=True)
        normed[here, :] = (value * lax.rsqrt(mean_square + 1e-06) * gain[...]).astype(BF)
        resid[here, :] = value
        for j, (source, target) in enumerate(((normed, normed_hbm), (resid, resid_hbm))):
            store = pltpu.make_async_copy(source.at[here], target.at[here], out_sems.at[j, i])
            store.start()
            stores.append(store)
    for store in stores:
        store.wait()


def add_and_norm(core, hidden, near, far, gain):
    rows, width = near.shape
    hbm = pl.BlockSpec(memory_space=pltpu.HBM)
    return pl.pallas_call(
        norm_kernel,
        out_shape=(
            jax.ShapeDtypeStruct((rows, width), F32),
            jax.ShapeDtypeStruct((rows, width), BF),
        ),
        in_specs=[pl.BlockSpec(memory_space=pltpu.SMEM), hbm, hbm, hbm, hbm],
        out_specs=(hbm, hbm),
        scratch_shapes=[
            pltpu.VMEM((rows, width), BF),
            pltpu.VMEM((rows, width), BF),
            pltpu.VMEM((rows, width), BF),
            pltpu.VMEM((1, width), F32),
            pltpu.VMEM((rows, width), F32),
            pltpu.VMEM((rows, width), BF),
            pltpu.SemaphoreType.DMA((4, 2)),
            pltpu.SemaphoreType.DMA((2, 2)),
        ],
        compiler_params=pltpu.CompilerParams(vmem_limit_bytes=58 << 20),
        cost_estimate=pl.CostEstimate(
            flops=8 * rows * width, bytes_accessed=4 << 20, transcendentals=rows
        ),
        name="add_and_norm",
    )(core, hidden, near, far, gain)


def gather_kernel(
    select_hbm, own_hbm, peer_hbm, out_hbm, select, rows, out, sems, out_sems
):
    half = rows.shape[0] // 2
    total, block = out.shape[0], out.shape[0] // 6
    copies = [
        pltpu.make_async_copy(own_hbm, rows.at[pl.ds(0, half)], sems.at[0]),
        pltpu.make_async_copy(peer_hbm, rows.at[pl.ds(half, half)], sems.at[1]),
        pltpu.make_async_copy(select_hbm, select, sems.at[2]),
    ]
    for copy in copies:
        copy.start()
    for copy in copies:
        copy.wait()
    stores = []
    for i in range(total // block):
        here = pl.ds(i * block, block)
        out[here, :] = jnp.dot(
            select[here, :], rows[...], preferred_element_type=F32
        ).astype(BF)
        store = pltpu.make_async_copy(out.at[here], out_hbm.at[here], out_sems.at[i])
        store.start()
        stores.append(store)
    for store in stores:
        store.wait()


def gather_rows(select, own, peer):
    slots, rows = select.shape
    width = own.shape[1]
    hbm = pl.BlockSpec(memory_space=pltpu.HBM)
    return pl.pallas_call(
        gather_kernel,
        out_shape=jax.ShapeDtypeStruct((slots, width), BF),
        in_specs=[hbm, hbm, hbm],
        out_specs=hbm,
        scratch_shapes=[
            pltpu.VMEM((slots, rows), BF),
            pltpu.VMEM((rows, width), BF),
            pltpu.VMEM((slots, width), BF),
            pltpu.SemaphoreType.DMA((3,)),
            pltpu.SemaphoreType.DMA((6,)),
        ],
        compiler_params=pltpu.CompilerParams(vmem_limit_bytes=58 << 20),
        cost_estimate=pl.CostEstimate(
            flops=2 * slots * rows * width, bytes_accessed=5 << 20, transcendentals=0
        ),
        name="gather_rows",
    )(select, own, peer)


def slot_weight_kernel(rank, weight, high):
    slots = high.shape[1]
    per_core = CAP // CORES
    experts_here = rank.shape[1]
    lane = lax.broadcasted_iota(jnp.int32, (1, slots), 1)
    expert_of = lax.rem(lax.div(lane, per_core), experts_here)
    wanted = lax.rem(lane, per_core) * CORES + lax.div(lane, per_core * experts_here)
    expand = (
        lax.broadcasted_iota(jnp.int32, (experts_here, slots), 0) == expert_of
    ).astype(BF)
    ranks = jnp.dot(rank[...].astype(BF), expand, preferred_element_type=F32)
    hit = ranks.astype(jnp.int32) == wanted
    spread = jnp.dot(weight[...].astype(BF), expand, preferred_element_type=F32)
    high[...] = jnp.where(hit, spread, 0.0).astype(BF)


def slot_weights(rank, weight, slots):
    rows = rank.shape[0]
    vmem = pl.BlockSpec(memory_space=pltpu.VMEM)
    shape = jax.ShapeDtypeStruct((rows, slots), BF)
    return pl.pallas_call(
        slot_weight_kernel,
        out_shape=shape,
        in_specs=[vmem, vmem],
        out_specs=vmem,
        compiler_params=pltpu.CompilerParams(vmem_limit_bytes=16 << 20),
        cost_estimate=pl.CostEstimate(
            flops=6 * rows * slots * 32, bytes_accessed=2 << 20, transcendentals=0
        ),
        name="slot_weights",
    )(rank, weight)


def expert_kernel(
    x_hbm, both_own, both_peer, down_own, down_peer, out_hbm,
    x, gate, up, down, act, out, x_sems, sems, down_sems, out_sems,
):
    hidden = both_own.shape[1]
    rows = x.shape[0]
    groups, _, width = out.shape
    parts = 3
    block = rows // parts
    step = 256
    bounds = [(lo, min(lo + step, 2 * hidden)) for lo in range(0, 2 * hidden, step)]
    x_copies = [
        pltpu.make_async_copy(
            x_hbm.at[pl.ds(m * block, block)], x.at[pl.ds(m * block, block)], x_sems.at[m]
        )
        for m in range(parts)
    ]
    chunks = []
    for n, (lo, hi) in enumerate(bounds):
        copies = []
        for j, (source, start, stop) in enumerate(
            (
                (both_own, lo, min(hi, hidden)),
                (both_peer, max(lo, hidden) - hidden, hi - hidden),
            )
        ):
            if stop <= start:
                continue
            shift = hidden * j
            for k, target in enumerate((gate, up)):
                copies.append(
                    pltpu.make_async_copy(
                        source.at[k, pl.ds(start, stop - start)],
                        target.at[pl.ds(start + shift, stop - start)],
                        sems.at[n, j, k],
                    )
                )
        chunks.append(copies)
    down_copies = [
        pltpu.make_async_copy(source, down.at[pl.ds(j * hidden, hidden)], down_sems.at[j])
        for j, source in enumerate((down_own, down_peer))
    ]
    def begin(copies):
        for copy in copies:
            copy.start()

    def finish(copies):
        for copy in copies:
            copy.wait()

    def halves(n, start, count):
        lo, hi = bounds[n]
        here = pl.ds(start * block, count * block)
        left = x[here, :]
        g = lax.dot_general(left, gate[lo:hi, :], contract, preferred_element_type=F32)
        u = lax.dot_general(left, up[lo:hi, :], contract, preferred_element_type=F32)
        act[here, lo:hi] = (g / (1.0 + jnp.exp(-g)) * u).astype(BF)

    contract = (((1,), (1,)), ((), ()))
    begin([x_copies[0]] + chunks[0])
    begin(x_copies[1:])
    finish([x_copies[0]] + chunks[0])
    begin(chunks[1])
    halves(0, 0, 1)
    finish(x_copies[1:])
    begin(chunks[2])
    halves(0, 1, parts - 1)
    finish(chunks[1])
    begin(down_copies)
    halves(1, 0, parts)
    finish(chunks[2])
    halves(2, 0, parts)
    finish(down_copies)
    stores = []
    for i in range(groups):
        result = jnp.dot(
            act[...], down[:, i * width : (i + 1) * width], preferred_element_type=F32
        )
        out[i] = result.astype(BF)
        store = pltpu.make_async_copy(out.at[i], out_hbm.at[i], out_sems.at[i])
        store.start()
        stores.append(store)
    for store in stores:
        store.wait()


def experts(x, both_own, both_peer, down_own, down_peer, groups):
    rows, depth = x.shape
    hidden, width = down_own.shape
    column_width = width // groups
    hbm = pl.BlockSpec(memory_space=pltpu.HBM)
    return pl.pallas_call(
        expert_kernel,
        out_shape=jax.ShapeDtypeStruct((groups, rows, column_width), BF),
        in_specs=[hbm] * 5,
        out_specs=hbm,
        scratch_shapes=[
            pltpu.VMEM((rows, depth), BF),
            pltpu.VMEM((2 * hidden, depth), BF),
            pltpu.VMEM((2 * hidden, depth), BF),
            pltpu.VMEM((2 * hidden, width), BF),
            pltpu.VMEM((rows, 2 * hidden), BF),
            pltpu.VMEM((groups, rows, column_width), BF),
            pltpu.SemaphoreType.DMA((3,)),
            pltpu.SemaphoreType.DMA((pl.cdiv(2 * hidden, 256), 2, 2)),
            pltpu.SemaphoreType.DMA((2,)),
            pltpu.SemaphoreType.DMA((groups,)),
        ],
        compiler_params=pltpu.CompilerParams(vmem_limit_bytes=60 << 20),
        cost_estimate=pl.CostEstimate(
            flops=12 * rows * depth * hidden,
            bytes_accessed=15 << 20,
            transcendentals=2 * rows * hidden,
        ),
        name="experts",
    )(x, both_own, both_peer, down_own, down_peer)


def combine_kernel(
    core, high_hbm, back_hbm, mine_hbm, peers_hbm, shared_hbm, out,
    high, back, mine, peers, shared, sems,
):
    rows = mine.shape[0]
    chips, depth = back.shape[0], back.shape[1]
    block = depth // CORES
    pieces = [(chip, pl.ds(c * block, block)) for chip in range(chips) for c in range(CORES)]
    copies = [
        pltpu.make_async_copy(back_hbm.at[chip, here], back.at[chip, here], sems.at[i])
        for i, (chip, here) in enumerate(pieces)
    ]
    rest = [
        pltpu.make_async_copy(source, target, sems.at[len(pieces) + i])
        for i, (source, target) in enumerate(
            (
                (high_hbm, high),
                (shared_hbm, shared),
                (mine_hbm, mine),
                (peers_hbm, peers),
            )
        )
    ]
    for copy in [rest[0]] + copies + rest[1:]:
        copy.start()
    total = None
    for i, (copy, (chip, here)) in enumerate(zip(copies, pieces)):
        if i == 0:
            rest[0].wait()
        copy.wait()
        part = jnp.dot(high[:, here], back[chip, here], preferred_element_type=F32)
        total = part if total is None else total + part
    for copy in rest[1:]:
        copy.wait()
    total += shared[...]
    first = core[0] == 0
    low_half = jnp.where(first, mine[...], peers[...])
    high_half = jnp.where(first, peers[...], mine[...])
    out[0:rows, :] = (total[0:rows] + low_half).astype(BF)
    out[rows : 2 * rows, :] = (total[rows:] + high_half).astype(BF)


def combine(core, high, returned, mine, peers, shared):
    hbm = pl.BlockSpec(memory_space=pltpu.HBM)
    vmem = pl.BlockSpec(memory_space=pltpu.VMEM)
    rows, width = shared.shape
    operands = (high, returned, mine, peers, shared)
    return pl.pallas_call(
        combine_kernel,
        out_shape=jax.ShapeDtypeStruct((rows, width), BF),
        in_specs=[pl.BlockSpec(memory_space=pltpu.SMEM)] + [hbm] * 5,
        out_specs=vmem,
        scratch_shapes=[pltpu.VMEM(o.shape, o.dtype) for o in operands]
        + [pltpu.SemaphoreType.DMA((8,))],
        compiler_params=pltpu.CompilerParams(vmem_limit_bytes=60 << 20),
        cost_estimate=pl.CostEstimate(
            flops=8 * rows * width * high.shape[1], bytes_accessed=7 << 20, transcendentals=0
        ),
        name="combine",
    )(core, *operands)


def page_pieces(keys, values, owner_all, tok_count, head_count, tok_index):
    pages_here = owner_all.shape[1]
    tok_rows = keys.shape[0]
    quarter_page = PAGE // head_count
    mine = lax.dynamic_index_in_dim(owner_all, tok_index, 0, keepdims=False)
    row = jnp.arange(tok_rows, dtype=jnp.int32)
    quarter = row // (tok_count * quarter_page)
    owner = row // quarter_page % tok_count
    line = quarter * quarter_page + row % quarter_page
    token_owner = jnp.repeat(mine, PAGE)
    token_line = jnp.arange(tok_rows, dtype=jnp.int32) % PAGE
    pick = (
        (owner[:, None] == token_owner[None, :]) & (line[:, None] == token_line[None, :])
    ).astype(BF)
    parts = [
        jnp.dot(pick, part, preferred_element_type=F32).astype(BF) for part in (keys, values)
    ]
    return jnp.concatenate(parts, 1).reshape(head_count * tok_count, quarter_page, -1)


def place_pages(landed, slots_all, owner_all, tok_count, head_count, tok_index):
    pages_here = owner_all.shape[1]
    quarter_page = PAGE // head_count
    rows = pages_here * quarter_page
    arrival = jnp.sum(jnp.where(owner_all == tok_index, slots_all % pages_here, 0), 1)
    row = jnp.arange(rows, dtype=jnp.int32)
    target = jnp.repeat(arrival, quarter_page) * quarter_page + row % quarter_page
    place = (row[:, None] == target[None, :]).astype(BF)
    landed = landed.reshape(head_count, rows, -1)
    width = landed.shape[2] // 2
    placed = [
        jnp.dot(place, landed[h], preferred_element_type=F32).astype(BF)
        for h in range(head_count)
    ]
    cache = jnp.concatenate(
        [p[:, :width] for p in placed] + [p[:, width:] for p in placed], 1
    )
    return cache.reshape(pages_here, quarter_page, 2 * head_count * width)


def per_device(
    hidden_in,
    queries,
    keys,
    values,
    request_ids,
    out_proj,
    norm_gain,
    expert_gate_up,
    expert_down,
    shared_gate_up,
    shared_down,
    shared_gate,
    routes,
    route_weights,
    page_slots,
):
    tok_rows, model_width = hidden_in.shape
    head_width = queries.shape[1]
    heads_here = head_width // HD
    tok_count = lax.axis_size("tok")
    head_count = lax.axis_size("head")
    tok_index = lax.axis_index("tok")
    head_index = lax.axis_index("head")
    core = head_index % CORES
    column_width = model_width // head_count
    rows_of_blocks = tok_count // ROW
    half = tok_rows // 2
    slots_core = CAP // CORES

    gate_up_own = jnp.transpose(expert_gate_up[0], (1, 2, 0))
    down_own = expert_down[0]
    out_peer = lax.ppermute(out_proj, "head", INTRA)
    gate_up_peer = lax.ppermute(gate_up_own, "head", INTRA)
    down_peer = lax.ppermute(down_own, "head", INTRA)

    place_in_row = tok_index % ROW
    own = []
    for step, part in enumerate(pack_heads(place_in_row.reshape(1), keys, values)):
        if step:
            part = lax.ppermute(
                part,
                "tok",
                [
                    (r * ROW + y, r * ROW + (y + step) % ROW)
                    for r in range(rows_of_blocks)
                    for y in range(ROW)
                ],
            )
        own.append(part)
    own = jnp.stack(own, 0)
    span = ROW * tok_rows
    base = (tok_index // ROW) * span
    padded_ids = jnp.concatenate([jnp.full((span,), -1, jnp.int32), request_ids], 0)
    window_ids = lax.dynamic_slice_in_dim(padded_ids, base, 2 * span, 0)
    ids_row = window_ids[None, :]
    queries, own, page_keys, page_values = lax.optimization_barrier((queries, own, keys, values))
    place_in_row = tok_index % ROW
    query_parts = []
    for step in range(ROW):
        target = (place_in_row + step) % ROW
        part = lax.dynamic_slice_in_dim(queries, target * HD, HD, 1)
        if step:
            part = lax.ppermute(
                part,
                "tok",
                [
                    (r * ROW + y, r * ROW + (y + step) % ROW)
                    for r in range(rows_of_blocks)
                    for y in range(ROW)
                ],
            )
        query_parts.append(part)
    slots_all = page_slots.reshape(tok_count, tok_rows // PAGE)
    owner_all = slots_all // (tok_rows // PAGE)
    pieces = page_pieces(page_keys, page_values, owner_all, tok_count, head_count, tok_index)
    past = lax.ppermute(
        own, "tok", [(s, s + ROW) for s in range(tok_count - ROW)]
    )
    attended = attention(
        place_in_row.reshape(1), ids_row, jnp.stack(query_parts, 0), own, past
    )

    core_groups = [
        [
            (chip * CORES + c) * tok_count + r * ROW + y
            for c in range(CORES)
            for y in range(ROW)
        ]
        for chip in range(CHIPS)
        for r in range(rows_of_blocks)
    ]
    gathered = lax.all_to_all(
        attended.reshape(CORES * ROW, half, HD),
        BOTH,
        split_axis=0,
        concat_axis=0,
        tiled=True,
        axis_index_groups=core_groups,
    ).reshape(CORES, ROW, half, HD)
    expert_ids = jnp.arange(EXPERTS, dtype=jnp.int32)
    named = routes[:, :, None] == expert_ids[None, None, :]
    onehot = jnp.sum(named.astype(F32), 1)
    weight_of = jnp.sum(jnp.where(named, route_weights[:, :, None], 0.0), 1)
    earlier = (
        jnp.arange(tok_rows, dtype=jnp.int32)[None, :] < jnp.arange(tok_rows, dtype=jnp.int32)[:, None]
    ).astype(BF)
    rank = jnp.dot(earlier, onehot.astype(BF), preferred_element_type=F32).astype(jnp.int32)
    rank = jnp.where(onehot > 0, rank, -1)
    rank_t = rank.T
    rank_rel = jnp.where(core == 0, rank_t, jnp.roll(rank_t, half, 1))
    place = jnp.arange(slots_core, dtype=jnp.int32) * CORES
    select = (rank_rel[:, None, :] == (place + core)[None, :, None]).astype(BF)
    select = select.reshape(EXPERTS * slots_core, tok_rows)
    core_ref = core.reshape(1)
    gathered, select, pieces = lax.optimization_barrier((gathered, select, pieces))
    projected_low = project(core_ref, gathered, out_proj, out_peer)
    projected_far = lax.ppermute(projected_low, "head", CROSS)
    pieces, _ = lax.optimization_barrier((pieces, projected_low))
    landed = lax.all_to_all(pieces, BOTH, split_axis=0, concat_axis=0, tiled=True)
    resid, normed_own = add_and_norm(
        core_ref, hidden_in, projected_low, projected_far, norm_gain[None, :]
    )
    normed_own, landed = lax.optimization_barrier((normed_own, landed))
    normed_peer = lax.ppermute(normed_own, "head", INTRA)

    outgoing = gather_rows(select, normed_own, normed_peer)
    rank, weight_of, _ = lax.optimization_barrier((rank, weight_of, outgoing))
    high = slot_weights(rank, weight_of, CORES * EXPERTS * slots_core)
    late_own, late_peer, _ = lax.optimization_barrier((normed_own, normed_peer, outgoing))
    normed_abs = jnp.where(
        core == 0,
        jnp.concatenate([late_own, late_peer], 0),
        jnp.concatenate([late_peer, late_own], 0),
    )
    arrived = lax.all_to_all(
        outgoing.reshape(tok_count, slots_core, model_width),
        "tok",
        split_axis=0,
        concat_axis=0,
        tiled=True,
    ).reshape(tok_count * slots_core, model_width)
    shared_both = jnp.einsum("td,dgf->tgf", normed_abs, shared_gate_up, preferred_element_type=F32)
    shared_act = (jax.nn.silu(shared_both[:, 0, :]) * shared_both[:, 1, :]).astype(BF)
    shared_scale = jax.nn.sigmoid(jnp.dot(normed_abs, shared_gate, preferred_element_type=F32))
    shared_term = shared_scale[:, None] * jnp.dot(
        shared_act, shared_down, preferred_element_type=F32
    )
    chip = head_index // CORES
    chip_width = CORES * column_width
    shared_near = lax.dynamic_slice_in_dim(shared_term, chip * chip_width, chip_width, 1)
    shared_send = lax.dynamic_slice_in_dim(
        shared_term, (1 - chip) * chip_width, chip_width, 1
    ).astype(BF)
    shared_near, shared_send, arrived = lax.optimization_barrier(
        (shared_near, shared_send, arrived)
    )
    shared_far = lax.ppermute(shared_send, "head", CROSS)

    partial = experts(arrived, gate_up_own, gate_up_peer, down_own, down_peer, head_count)
    partial = partial.reshape(head_count * tok_count, slots_core, column_width)
    partial, shared_far = lax.optimization_barrier((partial, shared_far))
    returned = lax.all_to_all(partial, BOTH, split_axis=0, concat_axis=0, tiled=True)
    returned = returned.reshape(CHIPS, CORES * EXPERTS * slots_core, column_width)

    shared_chip = shared_near + shared_far.astype(F32)
    shared_own = lax.dynamic_slice_in_dim(shared_chip, core * column_width, column_width, 1)
    shared_peer = lax.dynamic_slice_in_dim(
        shared_chip, (1 - core) * column_width, column_width, 1
    ).astype(BF)
    shared_cols = shared_own + lax.ppermute(shared_peer, "head", INTRA).astype(F32)
    own_cols = lax.dynamic_slice_in_dim(resid, head_index * column_width, column_width, 1)
    peer_cols = lax.dynamic_slice_in_dim(
        resid, (head_index + 1 - 2 * core) * column_width, column_width, 1
    )
    from_peer = lax.ppermute(peer_cols, "head", INTRA)
    layer_out = combine(core_ref, high, returned, own_cols, from_peer, shared_cols)
    decode_cache = place_pages(landed, slots_all, owner_all, tok_count, head_count, tok_index)
    return (layer_out, decode_cache)


def solution(mesh):
    in_specs = (
        P("tok", None),
        P("tok", "head"),
        P("tok", "head"),
        P("tok", "head"),
        P(),
        P("head", None),
        P(),
        P("tok", None, None, "head"),
        P("tok", "head", None),
        P(None, None, "head"),
        P("head", None),
        P(),
        P("tok", None),
        P("tok", None),
        P(),
    )
    out_specs = (P("tok", "head"), P("tok", "head", None))
    return jax.shard_map(
        per_device, mesh=mesh, in_specs=in_specs, out_specs=out_specs, check_vma=False
    )
```
